32 devices in a mesh: dp: 4 (over y, x), expert: 8 (over z, core).
Axes of the slice: x: 2, y: 2, z: 4, core: 2. Of those that a mesh axis runs over, the one named last changes fastest.
Arguments:
- tokens: bfloat16 [8192, 1280], P(('dp', 'expert')), may hold values from -6 to 6
- query_weight: bfloat16 [1280, 1280], P('dp'), may hold values from -0.15625 to 0.15625
- key_weight: bfloat16 [1280, 1280], P('dp'), may hold values from -0.15625 to 0.15625
- value_weight: bfloat16 [1280, 1280], P('dp'), may hold values from -0.15625 to 0.15625
- output_weight: bfloat16 [1280, 1280], P('dp'), may hold values from -0.625 to 0.625
- attn_gain: bfloat16 [1280], P('dp'), may hold values from 0.5 to 1.5
- ffn_gain: bfloat16 [1280], P('dp'), may hold values from 0.5 to 1.5
- router_weight: bfloat16 [1280, 16], P('dp'), may hold values from -0.078125 to 0.078125
- shared_gate: bfloat16 [1280, 896], P('dp'), may hold values from -0.15625 to 0.15625
- shared_up: bfloat16 [1280, 896], P('dp'), may hold values from -0.15625 to 0.15625
- shared_down: bfloat16 [896, 1280], P('dp'), may hold values from -0.25 to 0.25
- expert_gate: bfloat16 [16, 1280, 896], P('expert'), may hold values from -0.15625 to 0.15625
- expert_up: bfloat16 [16, 1280, 896], P('expert'), may hold values from -0.15625 to 0.15625
- expert_down: bfloat16 [16, 896, 1280], P('expert'), may hold values from -2 to 2
- expert_ids: int32 [8192, 7], P(('dp', 'expert')), may hold values from 0 to 15, all different within a row; in each aligned block of 256 rows (0 to 255, 256 to 511, ...) at most 128 rows name the same one
- piece_starts: int32 [32], P(('dp', 'expert')), may hold values from 0 to 128
- out_grad: bfloat16 [8192, 1280], P(('dp', 'expert')), may hold values from -6 to 6
Outputs:
- layer_out: bfloat16 [8192, 1280], P(('dp', 'expert'))
- tokens_grad: bfloat16 [8192, 1280], P(('dp', 'expert'))
- query_weight_grad: float32 [1280, 1280], P('dp')
- key_weight_grad: float32 [1280, 1280], P('dp')
- value_weight_grad: float32 [1280, 1280], P('dp')
- output_weight_grad: float32 [1280, 1280], P('dp')
- attn_gain_grad: float32 [1280], P('dp')
- ffn_gain_grad: float32 [1280], P('dp')
- router_weight_grad: float32 [1280, 16], P('dp')
- shared_gate_grad: float32 [1280, 896], P('dp')
- shared_up_grad: float32 [1280, 896], P('dp')
- shared_down_grad: float32 [896, 1280], P('dp')
- expert_gate_grad: float32 [16, 1280, 896], P('expert', 'dp')
- expert_up_grad: float32 [16, 1280, 896], P('expert', 'dp')
- expert_down_grad: float32 [16, 896, 1280], P('expert', 'dp')
- stat_rms: float32 [32, 3], P(('dp', 'expert'))
The draws below stay inside these ranges and needn't reach their ends.
Inputs may be any that keep to these rules, and one draw needn't show every extreme that they name: `expert_ids`: within each sequence (aligned blocks of 256 rows) no expert is named by more than 128 rows; each row names 7 different experts. The picture piece of sequence s is tokens piece_starts[s] to piece_starts[s] + 127 of it.
All inputs are finite; a program needn't handle non-finite values.
Results may differ from the reference program's by a relative error of at most 0.023.
Values may be sent and summed in bfloat16 or wider, within the bound.
No kernel may reach another device: no remote copies, remote signals or barrier semaphores. Data moves between devices by JAX's collectives and lax.ppermute only.
A program may use at most 320 MiB of HBM per device.

```python
import math
import jax
import jax.numpy as jnp
import numpy as np
from jax import lax

D = 1280
HEADS = 10
HEAD_DIM = 128
FF = 896
TOP = 7
LEN = 256
EXPERTS = 16
PIECE = 128
CAP = 128
SEQS = 32
TOKENS = 8192
N_EXPERT = 8


def place_ends(array, stream_key, low, high):
    shape = array.shape
    place = [jax.random.randint(jax.random.fold_in(stream_key, axis), (), 0, shape[axis]) for axis in range(len(shape))]
    array = array.at[tuple(place)].set(low)
    longest = shape.index(max(shape))
    place[longest] = (place[longest] + 1) % shape[longest]
    return array.at[tuple(place)].set(high)


def steps_of(stream_key, extent, shards, smallest, largest):
    factor_of, own = 1.0, jax.random.fold_in(stream_key, 6)
    for axis_at, blocks in shards:
        steps = jnp.exp(jax.random.uniform(jax.random.fold_in(own, axis_at), (blocks,), jnp.float32, smallest / len(shards), largest / len(shards)))
        factor_of = factor_of * jnp.repeat(steps, extent[axis_at] // blocks).reshape([-1 if axis == axis_at else 1 for axis in range(len(extent))])
    return factor_of


def assign_block(stream_key, own, number, rows, count, top, most, slope):
    sequence = jax.random.permutation(stream_key, count)
    crowded, common = shares(count, rows * top, most, slope, True), shares(count, rows * top, most, slope, False)
    places = jnp.arange(count)

    def named(tallies, rotation):
        used = int((tallies > 0).sum())
        fixed = max(1, used // 4)
        shifted = fixed + (places - fixed + rotation * (used - fixed)) % max(1, count - fixed)
        return jnp.zeros((count,), jnp.int32).at[sequence[jnp.where(places < fixed, places, shifted)]].set(jnp.asarray(tallies, jnp.int32))

    tallies = jnp.where(number % 4 == 0, named(crowded, number // 4), named(common, number - number // 4 - 1))
    mixed = jax.random.permutation(jax.random.fold_in(own, 3), count)
    source_of, receiver = mixed[0:count // 2 * 2:2], mixed[1:count // 2 * 2:2]
    room = jnp.minimum(tallies[source_of] - 1, most - tallies[receiver]) // 2
    room = jnp.where((source_of == sequence[0]) | (receiver == sequence[0]) | (tallies[receiver] == 0), 0, jnp.maximum(room, 0))
    shifted = jax.random.randint(jax.random.fold_in(own, 4), (count // 2,), 0, 1 << 20) % (room + 1)
    tallies = tallies.at[source_of].add(-shifted).at[receiver].add(shifted)
    items = jnp.searchsorted(jnp.cumsum(tallies), jnp.arange(rows * top), side="right").astype(jnp.int32)
    listing = items.reshape(top, rows).T
    listing = listing[jax.random.permutation(jax.random.fold_in(own, 1), rows)]
    rotation = jax.random.randint(jax.random.fold_in(own, 2), (rows, 1), 0, top)
    return jnp.take_along_axis(listing, (jnp.arange(top)[None, :] + rotation) % top, axis=1)


def shares(amount, total, most, lean, full):
    weights = [(1 << 20) // math.isqrt(rank ** lean) + 1 for rank in range(1, amount + 1)]
    largest = most if full else min(most, max(-(-total // amount), total * weights[0] // sum(weights)))
    least = 1 if total - largest >= amount - 1 else 0
    holding, rest = [largest] + [least] * (amount - 1), total - largest - least * (amount - 1)
    while rest > 0:
        candidates = [i for i in range(1, amount) if holding[i] < largest] or [i for i in range(1, amount) if holding[i] < most]
        whole, budget = sum([weights[i] for i in candidates]), rest
        for i in candidates:
            more = min(most - holding[i], max(1, budget * weights[i] // whole), rest)
            holding[i] = holding[i] + more
            rest = rest - more
    return np.array(holding)


def normal_values(stream_key, shape, deviation, limit, split=(), kind=jnp.bfloat16):
    drawn = deviation * jax.random.normal(stream_key, shape, jnp.float32)
    if split:
        drawn = drawn * steps_of(stream_key, shape, split, -0.22, 0.18)
    return jnp.clip(drawn, -limit, limit).astype(kind)


def setup_inputs(seed: int = 0) -> dict:
    splits = jax.random.split(jax.random.key(seed), 18)
    tokens = normal_values(splits[0], (TOKENS, D), 1.0, 6.0, ((0, 32),))
    query_weight = normal_values(splits[1], (D, D), D ** -0.5, 0.15625, ((0, 4),))
    key_weight = normal_values(splits[2], (D, D), D ** -0.5, 0.15625, ((0, 4),))
    value_weight = normal_values(splits[3], (D, D), D ** -0.5, 0.15625, ((0, 4),))
    output_weight = normal_values(splits[4], (D, D), (D // 16) ** -0.5, 0.625, ((0, 4),))
    attn_gain = jnp.clip(1.0 + 0.1 * jax.random.normal(splits[5], (D,), jnp.float32), 0.5, 1.5).astype(jnp.bfloat16)
    ffn_gain = jnp.clip(1.0 + 0.1 * jax.random.normal(splits[6], (D,), jnp.float32), 0.5, 1.5).astype(jnp.bfloat16)
    router_weight = normal_values(splits[7], (D, EXPERTS), (4 * D) ** -0.5, 0.078125, ((0, 4),))
    shared_gate = normal_values(splits[8], (D, FF), D ** -0.5, 0.15625, ((0, 4),))
    shared_up = normal_values(splits[9], (D, FF), D ** -0.5, 0.15625, ((0, 4),))
    shared_down = normal_values(splits[10], (FF, D), (FF // 2) ** -0.5, 0.25, ((0, 4),))
    expert_gate = normal_values(splits[11], (EXPERTS, D, FF), D ** -0.5, 0.15625, ((0, 8),))
    expert_up = normal_values(splits[12], (EXPERTS, D, FF), D ** -0.5, 0.15625, ((0, 8),))
    expert_down = normal_values(splits[13], (EXPERTS, FF, D), (max(FF // 100, 1)) ** -0.5, 2.0, ((0, 8),))
    expert_ids_keys = jax.random.split(jax.random.fold_in(splits[14], 1), TOKENS // LEN)
    expert_ids_turns = jax.random.permutation(jax.random.fold_in(splits[14], 3), TOKENS // LEN)
    expert_ids = jax.vmap(lambda own, number: assign_block(jax.random.fold_in(splits[14], 2), own, number, LEN, EXPERTS, TOP, CAP, 2))(expert_ids_keys, expert_ids_turns).reshape((TOKENS, TOP))
    piece_starts = place_ends(jax.random.randint(splits[15], (SEQS,), 0, LEN - PIECE + 1), jax.random.fold_in(splits[15], 1), 0, LEN - PIECE).astype(jnp.int32)
    out_grad = normal_values(splits[16], (TOKENS, D), 1.0, 6.0, ((0, 32),))
    return dict(tokens=tokens, query_weight=query_weight, key_weight=key_weight, value_weight=value_weight, output_weight=output_weight, attn_gain=attn_gain, ffn_gain=ffn_gain, router_weight=router_weight, shared_gate=shared_gate, shared_up=shared_up, shared_down=shared_down, expert_gate=expert_gate, expert_up=expert_up, expert_down=expert_down, expert_ids=expert_ids, piece_starts=piece_starts, out_grad=out_grad)


@jax.custom_vjp
def low(v):
    return lax.optimization_barrier(v.astype(jnp.bfloat16)).astype(jnp.float32)

@jax.custom_vjp
def low_back(v):
    return v

def low_keep(v):
    return (low(v), None)

def low_pass(kept, grad):
    return (grad,)

def back_keep(v):
    return (v, None)

def back_low(kept, grad):
    return (low(grad),)
low.defvjp(low_keep, low_pass)
low_back.defvjp(back_keep, back_low)

def product_high(first_arg, second_arg):
    return jnp.dot(first_arg, second_arg, precision=lax.Precision.HIGHEST, preferred_element_type=jnp.float32)

def rotary_tables(length, head_size):
    half_dim = head_size // 2
    frequency = 10000.0 ** (-jnp.arange(half_dim, dtype=jnp.float32) * 2.0 / head_size)
    angles = jnp.arange(length, dtype=jnp.float32)[:, None] * frequency[None, :]
    return (jnp.cos(angles), jnp.sin(angles))

def rotate(tensor, cosine, sine_part):
    half_dim = tensor.shape[-1] // 2
    first_half = tensor[..., :half_dim]
    second_half = tensor[..., half_dim:]
    cos_rows = cosine[:, None, :]
    sin_rows = sine_part[:, None, :]
    return jnp.concatenate([first_half * cos_rows - second_half * sin_rows, first_half * sin_rows + second_half * cos_rows], axis=-1)

def allowed_mask(length, piece_start, piece_len):
    row_index = jnp.arange(length, dtype=jnp.int32)[:, None]
    col_index = jnp.arange(length, dtype=jnp.int32)[None, :]
    row_inside = (row_index >= piece_start) & (row_index < piece_start + piece_len)
    col_inside = (col_index >= piece_start) & (col_index < piece_start + piece_len)
    return (col_index <= row_index) | row_inside & col_inside

def slot_positions(expert_ids):
    flat_ids = expert_ids.reshape(-1).astype(jnp.int32)
    onehot = (flat_ids[:, None] == jnp.arange(EXPERTS, dtype=jnp.int32)[None, :]).astype(jnp.int32)
    before = jnp.cumsum(onehot, axis=0) - onehot
    slot_index = lax.optimization_barrier(jnp.sum(before * onehot, axis=1)).astype(jnp.int32)
    return (flat_ids * CAP + slot_index).astype(jnp.int32)

def sequence_forward(token_rows, expert_ids, piece_start, weights):
    query_weight, key_weight, value_weight, output_weight, attn_gain, ffn_gain, router_weight, shared_gate, shared_up, shared_down, expert_gate, expert_up, expert_down = weights
    length = token_rows.shape[0]
    norm_one = lax.rsqrt(lax.optimization_barrier(jnp.mean(token_rows * token_rows, axis=-1, keepdims=True)) + 1e-06)
    attn_in = low(token_rows * norm_one * attn_gain)
    cosine, sine_part = rotary_tables(length, HEAD_DIM)
    query_pre = low_back(product_high(attn_in, query_weight)).reshape(length, HEADS, HEAD_DIM)
    key_pre = low_back(product_high(attn_in, key_weight)).reshape(length, HEADS, HEAD_DIM)
    query_rot = low(rotate(query_pre, cosine, sine_part))
    key_rot = low(rotate(key_pre, cosine, sine_part))
    values = low(low_back(product_high(attn_in, value_weight))).reshape(length, HEADS, HEAD_DIM)
    scores = low_back(jnp.einsum('qhd,khd->hqk', query_rot, key_rot, precision=lax.Precision.HIGHEST) * HEAD_DIM ** (-0.5))
    allowed = allowed_mask(length, piece_start, PIECE)
    scores = jnp.where(allowed[None], scores, -1e+30)
    attn_probs = jax.nn.softmax(scores, axis=-1)
    probs_low = low(attn_probs)
    context = jnp.einsum('hqk,khd->qhd', probs_low, values, precision=lax.Precision.HIGHEST)
    context = low_back(low(context)).reshape(length, D)
    attn_out = low_back(product_high(context, output_weight))
    residual = token_rows + attn_out
    norm_two = lax.rsqrt(lax.optimization_barrier(jnp.mean(residual * residual, axis=-1, keepdims=True)) + 1e-06)
    ffn_in = low(residual * norm_two * ffn_gain)
    router_probs = jax.nn.softmax(product_high(ffn_in, router_weight), axis=-1)
    gate_values = jnp.take_along_axis(router_probs, expert_ids, axis=1)
    shared_gate_act = low_back(product_high(ffn_in, shared_gate))
    shared_up_act = low_back(product_high(ffn_in, shared_up))
    shared_hidden = low(jax.nn.silu(shared_gate_act) * shared_up_act)
    shared_out = low_back(product_high(shared_hidden, shared_down))
    position = slot_positions(expert_ids)
    token_index = (jnp.arange(length * TOP, dtype=jnp.int32) // TOP).astype(jnp.int32)
    buffer_rows = jnp.zeros((EXPERTS * CAP, D), jnp.float32).at[position].set(ffn_in[token_index])
    expert_in = low_back(buffer_rows).reshape(EXPERTS, CAP, D)
    routed_gate = low_back(jnp.einsum('ecd,edf->ecf', expert_in, expert_gate, precision=lax.Precision.HIGHEST))
    routed_up = low_back(jnp.einsum('ecd,edf->ecf', expert_in, expert_up, precision=lax.Precision.HIGHEST))
    routed_hidden = low(jax.nn.silu(routed_gate) * routed_up)
    routed_res = low(low_back(jnp.einsum('ecf,efd->ecd', routed_hidden, expert_down, precision=lax.Precision.HIGHEST)))
    picked = routed_res.reshape(EXPERTS * CAP, D)[position].reshape(length, TOP, D)
    routed_out = lax.optimization_barrier(jnp.sum(gate_values[:, :, None] * picked, axis=1))
    moe_out = shared_out + routed_out
    stream_out = residual + moe_out
    stat_row = jnp.stack([jnp.sqrt(jnp.mean(attn_out * attn_out)), jnp.sqrt(jnp.mean(moe_out * moe_out)), jnp.sqrt(jnp.mean(stream_out * stream_out))])
    return (stream_out, stat_row)

def reference(tokens, query_weight, key_weight, value_weight, output_weight, attn_gain, ffn_gain, router_weight, shared_gate, shared_up, shared_down, expert_gate, expert_up, expert_down, expert_ids, piece_starts, out_grad):
    weights = tuple((item.astype(jnp.float32) for item in (query_weight, key_weight, value_weight, output_weight, attn_gain, ffn_gain, router_weight, shared_gate, shared_up, shared_down, expert_gate, expert_up, expert_down)))
    token_f = tokens.astype(jnp.float32)
    group_count = SEQS // N_EXPERT

    def forward(token_all, weight_all):
        block_tokens = token_all.reshape(group_count, N_EXPERT, LEN, D)
        block_ids = expert_ids.reshape(group_count, N_EXPERT, LEN, TOP)
        block_starts = piece_starts.reshape(group_count, N_EXPERT)

        def one_sequence(token_rows, id_rows, piece_start):
            return sequence_forward(token_rows, id_rows, piece_start, weight_all)

        def group_step(carry_state, inputs):
            group_out, group_stats = jax.vmap(one_sequence)(inputs[0], inputs[1], inputs[2])
            return (carry_state, (group_out, group_stats))
        carry_state, (stream_all, stat_all) = lax.scan(jax.checkpoint(group_step), jnp.zeros((), jnp.float32), (block_tokens, block_ids, block_starts))
        return (stream_all.reshape(TOKENS, D), stat_all.reshape(SEQS, 3))
    stream_out, vjp_fn, stat_rows = jax.vjp(forward, token_f, weights, has_aux=True)
    token_grad, weight_grads = vjp_fn(out_grad.astype(jnp.float32))
    return (stream_out.astype(jnp.bfloat16), token_grad.astype(jnp.bfloat16), weight_grads[0], weight_grads[1], weight_grads[2], weight_grads[3], weight_grads[4], weight_grads[5], weight_grads[6], weight_grads[7], weight_grads[8], weight_grads[9], weight_grads[10], weight_grads[11], weight_grads[12], stat_rows)
```

```python
import jax
import jax.numpy as jnp
from jax import lax
from jax.sharding import PartitionSpec as P

HEAD_DIM = 128
TOP = 7
EXP_DEV = 2
BF = jnp.bfloat16


def product(first_arg, second_arg):
    return jnp.dot(first_arg, second_arg, preferred_element_type=jnp.float32)


def product_high(first_arg, second_arg):
    return jnp.dot(
        first_arg, second_arg, precision=lax.Precision.HIGHEST, preferred_element_type=jnp.float32
    )


def rotary_tables(length, head_size):
    half_dim = head_size // 2
    frequency = 10000.0 ** (-jnp.arange(half_dim, dtype=jnp.float32) * 2.0 / head_size)
    angles = jnp.arange(length, dtype=jnp.float32)[:, None] * frequency[None, :]
    return (jnp.cos(angles), jnp.sin(angles))


def rotate(tensor, cosine, sine_part):
    half_dim = tensor.shape[-1] // 2
    first_half = tensor[..., :half_dim]
    second_half = tensor[..., half_dim:]
    cos_rows = cosine[:, None, :]
    sin_rows = sine_part[:, None, :]
    return jnp.concatenate(
        [
            first_half * cos_rows - second_half * sin_rows,
            first_half * sin_rows + second_half * cos_rows,
        ],
        axis=-1,
    )


def allowed_mask(length, piece_start, piece_len):
    row_index = jnp.arange(length, dtype=jnp.int32)[:, None]
    col_index = jnp.arange(length, dtype=jnp.int32)[None, :]
    row_inside = (row_index >= piece_start) & (row_index < piece_start + piece_len)
    col_inside = (col_index >= piece_start) & (col_index < piece_start + piece_len)
    return (col_index <= row_index) | row_inside & col_inside


def silu_grad(inputs):
    sigmoid_part = jax.nn.sigmoid(inputs)
    return sigmoid_part * (1.0 + inputs * (1.0 - sigmoid_part))


def high_low(values):
    high = values.astype(BF)
    low = (values - high.astype(jnp.float32)).astype(BF)
    return high, low


def body(
    tokens,
    query_weight,
    key_weight,
    value_weight,
    output_weight,
    attn_gain,
    ffn_gain,
    router_weight,
    shared_gate,
    shared_up,
    shared_down,
    expert_gate,
    expert_up,
    expert_down,
    expert_ids,
    piece_starts,
    out_grad,
):
    dp = lax.axis_size("dp")
    owners = lax.axis_size("expert")
    me = lax.axis_index("expert")
    experts = EXP_DEV * owners
    length, width = tokens.shape
    rows = query_weight.shape[0]
    hidden = shared_gate.shape[1]
    head_count = width // HEAD_DIM
    score_scale = HEAD_DIM ** (-0.5)
    piece_len = min(256, length // 2)
    capacity = 8 * length // experts

    chosen = (expert_ids[:, :, None] == jnp.arange(experts, dtype=jnp.int32)).any(axis=1)
    chosen_low = jnp.pad(chosen.astype(BF), ((0, 0), (0, 128 - experts)))
    grads_all = lax.all_gather(
        jnp.concatenate([out_grad, chosen_low], axis=1), "expert", axis=0, tiled=True
    ).reshape(owners, length, width + 128)

    small = jnp.concatenate(
        [router_weight, attn_gain[:, None], ffn_gain[:, None]], axis=1
    )
    small = jnp.pad(small, ((0, 0), (0, 128 - small.shape[1])))
    first_full = lax.all_gather(
        jnp.concatenate([query_weight, key_weight, value_weight, small], axis=1),
        "dp", axis=0, tiled=True,
    )
    second_full = lax.all_gather(
        jnp.concatenate(
            [output_weight, shared_gate, shared_up, shared_down.reshape(rows, -1)], axis=1
        ),
        "dp", axis=0, tiled=True,
    )
    query_full = first_full[:, :width]
    key_full = first_full[:, width : 2 * width]
    value_full = first_full[:, 2 * width : 3 * width]
    small_full = first_full[:, 3 * width :]
    router_full = small_full[:, :experts]
    gain_one_f = small_full[:, experts].astype(jnp.float32)
    gain_two_f = small_full[:, experts + 1].astype(jnp.float32)
    output_full = second_full[:, :width]
    shared_gate_full = second_full[:, width : width + hidden]
    shared_up_full = second_full[:, width + hidden : width + 2 * hidden]
    shared_down_full = second_full[:, width + 2 * hidden :].reshape(hidden, width)

    token_f = tokens.astype(jnp.float32)
    norm_one = lax.rsqrt(jnp.mean(token_f * token_f, axis=-1, keepdims=True) + 1e-06)
    attn_in = (token_f * norm_one * gain_one_f).astype(BF)
    cosine, sine_part = rotary_tables(length, HEAD_DIM)
    query_pre = product(attn_in, query_full).reshape(length, head_count, HEAD_DIM)
    key_pre = product(attn_in, key_full).reshape(length, head_count, HEAD_DIM)
    query_rot = rotate(query_pre, cosine, sine_part).astype(BF)
    key_rot = rotate(key_pre, cosine, sine_part).astype(BF)
    values = product(attn_in, value_full).astype(BF).reshape(length, head_count, HEAD_DIM)
    allowed = allowed_mask(length, piece_starts[0], piece_len)
    scores = (
        jnp.einsum("qhd,khd->hqk", query_rot, key_rot, preferred_element_type=jnp.float32)
        * score_scale
    )
    scores = jnp.where(allowed[None], scores, -1e30)
    row_max = jnp.max(scores, axis=-1, keepdims=True)
    exps = jnp.exp(scores - row_max)
    attn_probs = exps / jnp.sum(exps, axis=-1, keepdims=True)
    probs_low = attn_probs.astype(BF)
    context = jnp.einsum("hqk,khd->qhd", probs_low, values, preferred_element_type=jnp.float32)
    context = context.astype(BF).reshape(length, width)
    attn_out = product(context, output_full)
    residual = token_f + attn_out
    norm_two = lax.rsqrt(jnp.mean(residual * residual, axis=-1, keepdims=True) + 1e-06)
    ffn_in = (residual * norm_two * gain_two_f).astype(BF)
    router_probs = jax.nn.softmax(product(ffn_in, router_full), axis=-1)
    gates = jnp.where(chosen, router_probs, 0.0)
    gates_high, gates_low = high_low(gates)
    sent = jnp.concatenate(
        [ffn_in, gates_high, gates_low, jnp.zeros((length, 128 - 2 * experts), BF)], axis=1
    )
    rows_all = lax.all_gather(sent, "expert", axis=0, tiled=True).reshape(
        owners, length, width + 128
    )

    grad_f = out_grad.astype(jnp.float32)
    shared_gate_act = product(ffn_in, shared_gate_full)
    shared_up_act = product(ffn_in, shared_up_full)
    shared_hidden = (jax.nn.silu(shared_gate_act) * shared_up_act).astype(BF)
    shared_out = product(shared_hidden, shared_down_full)
    shared_hidden_grad = product(out_grad, shared_down_full.T)
    shared_down_grad = product(shared_hidden.T, out_grad)
    shared_gate_act_grad = (shared_hidden_grad * shared_up_act * silu_grad(shared_gate_act)).astype(
        BF
    )
    shared_up_act_grad = (shared_hidden_grad * jax.nn.silu(shared_gate_act)).astype(BF)
    shared_gate_grad = product(ffn_in.T, shared_gate_act_grad)
    shared_up_grad = product(ffn_in.T, shared_up_act_grad)
    shared_in_grad = product(shared_gate_act_grad, shared_gate_full.T) + product(
        shared_up_act_grad, shared_up_full.T
    )
    shared_parts = jnp.concatenate(
        [
            shared_gate_grad.astype(BF),
            shared_up_grad.astype(BF),
            shared_down_grad.astype(BF).reshape(dp * rows, -1),
        ],
        axis=1,
    )
    shared_share = lax.psum_scatter(shared_parts, "dp", scatter_dimension=0, tiled=True)

    own = me * EXP_DEV + jnp.arange(EXP_DEV)
    own_hot = (own[:, None] == jnp.arange(experts)[None, :]).astype(jnp.float32)
    mask = jnp.einsum("ste,oe->ost", grads_all[:, :, width : width + experts].astype(jnp.float32), own_hot)
    slot = jnp.cumsum(mask, axis=2) - 1.0
    spread = (
        (slot[:, :, None, :] == jnp.arange(capacity, dtype=jnp.float32)[None, None, :, None])
        & (mask[:, :, None, :] > 0)
    ).astype(BF)
    gates_pair = (
        rows_all[:, :, width : width + experts].astype(jnp.float32)
        + rows_all[:, :, width + experts : width + 2 * experts].astype(jnp.float32)
    )
    gates_own = jnp.einsum("ste,oe->ost", gates_pair, own_hot, precision=lax.Precision.HIGHEST)
    slot_gates = jnp.einsum(
        "osct,ost->osc", spread.astype(jnp.float32), gates_own, precision=lax.Precision.HIGHEST
    )
    take = lambda source: jnp.einsum(
        "osct,std->oscd", spread, source, preferred_element_type=jnp.float32
    ).astype(BF)
    expert_in = take(rows_all[:, :, :width]).reshape(EXP_DEV, owners * capacity, width)
    slot_out_grad = take(grads_all[:, :, :width])
    res_grad = (slot_gates[..., None] * slot_out_grad.astype(jnp.float32)).astype(BF)
    res_grad = res_grad.reshape(EXP_DEV, owners * capacity, width)
    mm = lambda spec, a, b: jnp.einsum(spec, a, b, preferred_element_type=jnp.float32)
    routed_gate = mm("erd,edf->erf", expert_in, expert_gate)
    routed_up = mm("erd,edf->erf", expert_in, expert_up)
    routed_hidden = (jax.nn.silu(routed_gate) * routed_up).astype(BF)
    hidden_grad = mm("erd,efd->erf", res_grad, expert_down)
    routed_gate_grad = (hidden_grad * routed_up * silu_grad(routed_gate)).astype(BF)
    routed_up_grad = (hidden_grad * jax.nn.silu(routed_gate)).astype(BF)
    expert_in_grad = (
        mm("erf,edf->erd", routed_gate_grad, expert_gate)
        + mm("erf,edf->erd", routed_up_grad, expert_up)
    ).astype(BF).reshape(EXP_DEV, owners, capacity, width)
    routed_res = mm("erf,efd->erd", routed_hidden, expert_down).astype(BF)
    routed_res = routed_res.reshape(EXP_DEV, owners, capacity, width)
    slot_gate_grad = jnp.sum(
        routed_res.astype(jnp.float32) * slot_out_grad.astype(jnp.float32), axis=-1
    )
    token_gate_grad = jnp.einsum(
        "osct,osc,oe->ste", spread.astype(jnp.float32), slot_gate_grad, own_hot,
        precision=lax.Precision.HIGHEST,
    )
    gg_high, gg_low = high_low(token_gate_grad)
    in_grad_part = mm("osct,oscd->std", spread, expert_in_grad).astype(BF)
    back = jnp.concatenate(
        [in_grad_part, gg_high, gg_low, jnp.zeros((owners, length, 128 - 2 * experts), BF)], axis=2
    ).reshape(owners * length, width + 128)
    back = lax.psum_scatter(back, "expert", scatter_dimension=0, tiled=True)
    out_part = mm(
        "osct,oscd->std", (spread.astype(jnp.float32) * slot_gates[..., None]).astype(BF), routed_res
    ).astype(BF)
    expert_down_part = mm("erf,erd->efd", routed_hidden, res_grad).astype(BF)
    expert_gate_part = mm("erd,erf->edf", expert_in, routed_gate_grad).astype(BF)
    expert_up_part = mm("erd,erf->edf", expert_in, routed_up_grad).astype(BF)
    expert_parts = jnp.concatenate(
        [
            expert_gate_part.reshape(EXP_DEV, dp, rows, hidden),
            expert_up_part.reshape(EXP_DEV, dp, rows, hidden),
            expert_down_part.reshape(EXP_DEV, dp, rows, hidden),
        ],
        axis=0,
    ).transpose(1, 0, 2, 3)
    expert_share = lax.psum_scatter(expert_parts, "dp", scatter_dimension=0, tiled=True)[0]
    expert_share = expert_share.astype(jnp.float32)
    out_sum = lax.psum_scatter(
        out_part.reshape(owners * length, width), "expert", scatter_dimension=0, tiled=True
    )

    routed_in_grad = back[:, :width].astype(jnp.float32)
    probs_grad = back[:, width : width + experts].astype(jnp.float32) + back[
        :, width + experts : width + 2 * experts
    ].astype(jnp.float32)
    logits_grad = router_probs * (
        probs_grad - jnp.sum(router_probs * probs_grad, axis=-1, keepdims=True)
    )
    router_grad = product_high(ffn_in.astype(jnp.float32).T, logits_grad)
    router_in_grad = product_high(logits_grad, router_full.astype(jnp.float32).T)
    ffn_in_grad = shared_in_grad + routed_in_grad + router_in_grad
    ffn_gain_grad = jnp.sum(ffn_in_grad * residual * norm_two, axis=0)
    upstream_two = ffn_in_grad * gain_two_f
    residual_grad = (
        grad_f
        + norm_two * upstream_two
        - residual * norm_two**3 * jnp.mean(upstream_two * residual, axis=-1, keepdims=True)
    )
    attn_out_grad = residual_grad.astype(BF)
    output_grad = product(context.T, attn_out_grad)
    context_grad = (
        product(attn_out_grad, output_full.T).astype(BF).reshape(length, head_count, HEAD_DIM)
    )
    value_grad = mm("hqk,qhd->khd", probs_low, context_grad).astype(BF).reshape(length, width)
    probs_grad_att = mm("qhd,khd->hqk", context_grad, values)
    row_delta = jnp.sum(attn_probs * probs_grad_att, axis=-1, keepdims=True)
    scores_grad = (attn_probs * (probs_grad_att - row_delta)).astype(BF)
    query_grad = mm("hqk,khd->qhd", scores_grad, key_rot) * score_scale
    key_grad = mm("hqk,qhd->khd", scores_grad, query_rot) * score_scale
    query_pre_grad = rotate(query_grad, cosine, -sine_part).astype(BF).reshape(length, width)
    key_pre_grad = rotate(key_grad, cosine, -sine_part).astype(BF).reshape(length, width)
    query_wgrad = product(attn_in.T, query_pre_grad)
    key_wgrad = product(attn_in.T, key_pre_grad)
    value_wgrad = product(attn_in.T, value_grad)
    attn_in_grad = (
        product(query_pre_grad, query_full.T)
        + product(key_pre_grad, key_full.T)
        + product(value_grad, value_full.T)
    )
    attn_gain_grad = jnp.sum(attn_in_grad * token_f * norm_one, axis=0)
    upstream_one = attn_in_grad * gain_one_f
    tokens_grad = (
        residual_grad
        + norm_one * upstream_one
        - token_f * norm_one**3 * jnp.mean(upstream_one * token_f, axis=-1, keepdims=True)
    )
    small_grads = jnp.concatenate(
        [router_grad, attn_gain_grad[:, None], ffn_gain_grad[:, None]], axis=1
    ).astype(BF)
    small_grads = jnp.pad(small_grads, ((0, 0), (0, 128 - small_grads.shape[1])))
    attn_parts = jnp.concatenate(
        [
            query_wgrad.astype(BF),
            key_wgrad.astype(BF),
            value_wgrad.astype(BF),
            output_grad.astype(BF),
            small_grads,
        ],
        axis=1,
    )
    attn_share = lax.psum_scatter(attn_parts, "dp", scatter_dimension=0, tiled=True)
    shared_share = lax.psum(shared_share, "expert").astype(jnp.float32)
    attn_share = lax.psum(attn_share, "expert").astype(jnp.float32)

    moe_out = shared_out + out_sum.astype(jnp.float32)
    stream_out = residual + moe_out
    stat_rms = jnp.stack(
        [
            jnp.sqrt(jnp.mean(attn_out * attn_out)),
            jnp.sqrt(jnp.mean(moe_out * moe_out)),
            jnp.sqrt(jnp.mean(stream_out * stream_out)),
        ]
    )[None, :]
    return (
        stream_out.astype(BF),
        tokens_grad.astype(BF),
        attn_share[:, :width],
        attn_share[:, width : 2 * width],
        attn_share[:, 2 * width : 3 * width],
        attn_share[:, 3 * width : 4 * width],
        attn_share[:, 4 * width + experts],
        attn_share[:, 4 * width + experts + 1],
        attn_share[:, 4 * width : 4 * width + experts],
        shared_share[:, :hidden],
        shared_share[:, hidden : 2 * hidden],
        shared_share[:, 2 * hidden :].reshape(shared_down.shape),
        expert_share[0:2],
        expert_share[2:4],
        expert_share[4:6].reshape(EXP_DEV, shared_down.shape[0], width),
        stat_rms,
    )


def solution(mesh):
    in_specs = (
        P(("dp", "expert"), None),
        P("dp", None),
        P("dp", None),
        P("dp", None),
        P("dp", None),
        P("dp"),
        P("dp"),
        P("dp", None),
        P("dp", None),
        P("dp", None),
        P("dp", None),
        P("expert", None, None),
        P("expert", None, None),
        P("expert", None, None),
        P(("dp", "expert"), None),
        P(("dp", "expert")),
        P(("dp", "expert"), None),
    )
    out_specs = (
        P(("dp", "expert"), None),
        P(("dp", "expert"), None),
        P("dp", None),
        P("dp", None),
        P("dp", None),
        P("dp", None),
        P("dp"),
        P("dp"),
        P("dp", None),
        P("dp", None),
        P("dp", None),
        P("dp", None),
        P("expert", "dp", None),
        P("expert", "dp", None),
        P("expert", "dp", None),
        P(("dp", "expert"), None),
    )
    return jax.shard_map(body, mesh=mesh, in_specs=in_specs, out_specs=out_specs, check_vma=False)
```

```python
import math

import jax
import jax.numpy as jnp
from jax import lax
from jax.sharding import Mesh
from jax.sharding import PartitionSpec as P

HEAD_DIM = 128
TOP = 7
EXP_DEV = 2
BF = jnp.bfloat16
F32 = jnp.float32
DP = ("y", "x")
OWN = ("z", "c")


def product(first_arg, second_arg):
    return jnp.dot(first_arg, second_arg, preferred_element_type=F32)


def product_high(first_arg, second_arg):
    return jnp.dot(
        first_arg, second_arg, precision=lax.Precision.HIGHEST, preferred_element_type=F32
    )


def mm(spec, first_arg, second_arg):
    return jnp.einsum(spec, first_arg, second_arg, preferred_element_type=F32)


def mm_high(spec, *args):
    return jnp.einsum(spec, *args, precision=lax.Precision.HIGHEST, preferred_element_type=F32)


def rotary_tables(length, head_size):
    half_dim = head_size // 2
    frequency = 10000.0 ** (-jnp.arange(half_dim, dtype=F32) * 2.0 / head_size)
    angles = jnp.arange(length, dtype=F32)[:, None] * frequency[None, :]
    return (jnp.cos(angles), jnp.sin(angles))


def rotate(tensor, cosine, sine_part):
    half_dim = tensor.shape[-1] // 2
    first_half = tensor[..., :half_dim]
    second_half = tensor[..., half_dim:]
    cos_rows = cosine[:, None, :]
    sin_rows = sine_part[:, None, :]
    return jnp.concatenate(
        [
            first_half * cos_rows - second_half * sin_rows,
            first_half * sin_rows + second_half * cos_rows,
        ],
        axis=-1,
    )


def allowed_mask(length, piece_start, piece_len):
    row_index = jnp.arange(length, dtype=jnp.int32)[:, None]
    col_index = jnp.arange(length, dtype=jnp.int32)[None, :]
    row_inside = (row_index >= piece_start) & (row_index < piece_start + piece_len)
    col_inside = (col_index >= piece_start) & (col_index < piece_start + piece_len)
    return (col_index <= row_index) | row_inside & col_inside


def silu_grad(inputs):
    sigmoid_part = jax.nn.sigmoid(inputs)
    return sigmoid_part * (1.0 + inputs * (1.0 - sigmoid_part))


def high_low(values):
    high = values.astype(BF)
    low = (values - high.astype(F32)).astype(BF)
    return high, low


def swap(value):
    return lax.ppermute(value, "c", [(0, 1), (1, 0)])


def half(value, index, axis):
    size = value.shape[axis] // 2
    return lax.dynamic_slice_in_dim(value, index * size, size, axis)


def joined(mine, other, core, axis):
    return jnp.where(
        core == 0, jnp.concatenate([mine, other], axis), jnp.concatenate([other, mine], axis)
    )


def body(
    tokens,
    query_weight,
    key_weight,
    value_weight,
    output_weight,
    attn_gain,
    ffn_gain,
    router_weight,
    shared_gate,
    shared_up,
    shared_down,
    expert_gate,
    expert_up,
    expert_down,
    expert_ids,
    piece_starts,
    out_grad,
):
    dp = lax.axis_size(DP)
    owners = lax.axis_size(OWN)
    depth = lax.axis_size("z")
    core, level = lax.axis_index("c"), lax.axis_index("z")
    me = lax.axis_index(OWN)
    experts = EXP_DEV * owners
    length, width = tokens.shape
    rows = query_weight.shape[0]
    hidden = shared_gate.shape[1]
    part = hidden // (2 * dp)
    wide, narrow = width // 2, hidden // 2
    head_count = wide // HEAD_DIM
    score_scale = HEAD_DIM ** (-0.5)
    piece_len = min(256, length // 2)
    capacity = 8 * length // experts
    two = lambda mine: jnp.stack([mine, swap(mine)])

    small = jnp.concatenate([router_weight, attn_gain[:, None], ffn_gain[:, None]], axis=1)
    small = jnp.pad(small, ((0, 0), (0, 128 - small.shape[1])))
    first_full = lax.all_gather(
        jnp.concatenate(
            [half(query_weight, core, 1), half(key_weight, core, 1), half(value_weight, core, 1), small],
            axis=1,
        ),
        DP, axis=0, tiled=True,
    )
    units = lambda weight: lax.dynamic_index_in_dim(
        weight.reshape(rows, dp, 2, part), core, 2, False
    ).reshape(rows, narrow)
    second_full = lax.all_gather(
        jnp.concatenate(
            [
                half(output_weight, core, 1),
                units(shared_gate),
                units(shared_up),
                half(shared_down, core, 0).reshape(rows, narrow),
            ],
            axis=1,
        ),
        DP, axis=0, tiled=True,
    )
    tokens_two = two(tokens)
    starts_two = two(piece_starts[0])
    out_grad_two = two(out_grad)

    chosen = (expert_ids[:, :, None] == jnp.arange(experts, dtype=jnp.int32)).any(axis=1)
    chosen_low = jnp.pad(chosen.astype(BF), ((0, 0), (0, 128 - experts)))
    grads_all = lax.all_gather(
        jnp.concatenate([out_grad, chosen_low], axis=1), OWN, axis=0, tiled=True
    ).reshape(owners, length, width + 128)

    query_half = first_full[:, :wide]
    key_half = first_full[:, wide : 2 * wide]
    value_half = first_full[:, 2 * wide : 3 * wide]
    small_full = first_full[:, 3 * wide :]
    router_full = small_full[:, :experts]
    gain_one_f = small_full[:, experts].astype(F32)
    gain_two_f = small_full[:, experts + 1].astype(F32)
    output_cols = second_full[:, :wide]
    gate_half = second_full[:, wide : wide + narrow]
    up_half = second_full[:, wide + narrow : wide + 2 * narrow]
    down_half = second_full[:, wide + 2 * narrow :].reshape(narrow, width)
    output_half = joined(
        half(output_cols, core, 0), swap(half(output_cols, 1 - core, 0)), core, 1
    )

    token_f = tokens_two.astype(F32)
    norm_one = lax.rsqrt(jnp.mean(token_f * token_f, axis=-1, keepdims=True) + 1e-06)
    attn_in = (token_f * norm_one * gain_one_f).astype(BF).reshape(2 * length, width)
    cosine, sine_part = rotary_tables(length, HEAD_DIM)
    by_head = lambda value: value.reshape(2, length, head_count, HEAD_DIM)
    flat = lambda value: value.reshape(2 * length, wide)
    query_rot = rotate(by_head(product(attn_in, query_half)), cosine, sine_part).astype(BF)
    key_rot = rotate(by_head(product(attn_in, key_half)), cosine, sine_part).astype(BF)
    values = by_head(product(attn_in, value_half).astype(BF))
    allowed = jnp.stack([allowed_mask(length, starts_two[i], piece_len) for i in range(2)])
    scores = mm("sqhd,skhd->shqk", query_rot, key_rot) * score_scale
    scores = jnp.where(allowed[:, None], scores, -1e30)
    row_max = jnp.max(scores, axis=-1, keepdims=True)
    exps = jnp.exp(scores - row_max)
    attn_probs = exps / jnp.sum(exps, axis=-1, keepdims=True)
    probs_low = attn_probs.astype(BF)
    context = flat(mm("shqk,skhd->sqhd", probs_low, values).astype(BF))
    out_partial = product(context, output_half).reshape(2, length, width)
    attn_out = out_partial[0] + swap(out_partial[1].astype(BF)).astype(F32)
    residual = token_f[0] + attn_out
    norm_two = lax.rsqrt(jnp.mean(residual * residual, axis=-1, keepdims=True) + 1e-06)
    ffn_in = (residual * norm_two * gain_two_f).astype(BF)
    router_probs = jax.nn.softmax(product(ffn_in, router_full), axis=-1)
    gates = jnp.where(chosen, router_probs, 0.0)
    gates_high, gates_low = high_low(gates)
    sent = jnp.concatenate(
        [ffn_in, gates_high, gates_low, jnp.zeros((length, 128 - 2 * experts), BF)], axis=1
    )
    rows_all = lax.all_gather(sent, OWN, axis=0, tiled=True).reshape(owners, length, width + 128)

    ffn_two = two(ffn_in).reshape(2 * length, width)
    grad_two = out_grad_two.reshape(2 * length, width)
    shared_gate_act = product(ffn_two, gate_half)
    shared_up_act = product(ffn_two, up_half)
    shared_hidden = (jax.nn.silu(shared_gate_act) * shared_up_act).astype(BF)
    shared_out = product(shared_hidden, down_half).reshape(2, length, width)
    shared_hidden_grad = product(grad_two, down_half.T)
    shared_down_grad = product(shared_hidden.T, grad_two)
    shared_gate_act_grad = (shared_hidden_grad * shared_up_act * silu_grad(shared_gate_act)).astype(
        BF
    )
    shared_up_act_grad = (shared_hidden_grad * jax.nn.silu(shared_gate_act)).astype(BF)
    shared_gate_grad = product(ffn_two.T, shared_gate_act_grad)
    shared_up_grad = product(ffn_two.T, shared_up_act_grad)
    shared_in_grad = (
        product(shared_gate_act_grad, gate_half.T) + product(shared_up_act_grad, up_half.T)
    ).reshape(2, length, width)
    shared_parts = jnp.concatenate(
        [
            shared_gate_grad.astype(BF),
            shared_up_grad.astype(BF),
            shared_down_grad.astype(BF).reshape(dp * rows, narrow),
        ],
        axis=1,
    )
    shared_share = lax.psum_scatter(shared_parts, DP, scatter_dimension=0, tiled=True)

    own = me * EXP_DEV + jnp.arange(EXP_DEV)
    own_hot = (own[:, None] == jnp.arange(experts)[None, :]).astype(F32)
    mask = mm("ste,oe->ost", grads_all[:, :, width : width + experts].astype(F32), own_hot)
    slot = jnp.cumsum(mask, axis=2) - 1.0
    spread = (
        (slot[:, :, None, :] == jnp.arange(capacity, dtype=F32)[None, None, :, None])
        & (mask[:, :, None, :] > 0)
    ).astype(BF)
    gates_pair = rows_all[:, :, width : width + experts].astype(F32) + rows_all[
        :, :, width + experts : width + 2 * experts
    ].astype(F32)
    gates_own = mm_high("ste,oe->ost", gates_pair, own_hot)
    slot_gates = mm_high("osct,ost->osc", spread.astype(F32), gates_own)
    take = lambda source: mm("osct,std->oscd", spread, source).astype(BF)
    expert_in = take(rows_all[:, :, :width]).reshape(EXP_DEV, owners * capacity, width)
    slot_out_grad = take(grads_all[:, :, :width])
    res_grad = (slot_gates[..., None] * slot_out_grad.astype(F32)).astype(BF)
    res_grad = res_grad.reshape(EXP_DEV, owners * capacity, width)
    routed_gate = mm("erd,edf->erf", expert_in, expert_gate)
    routed_up = mm("erd,edf->erf", expert_in, expert_up)
    routed_hidden = (jax.nn.silu(routed_gate) * routed_up).astype(BF)
    hidden_grad = mm("erd,efd->erf", res_grad, expert_down)
    routed_gate_grad = (hidden_grad * routed_up * silu_grad(routed_gate)).astype(BF)
    routed_up_grad = (hidden_grad * jax.nn.silu(routed_gate)).astype(BF)
    expert_in_grad = (
        (
            mm("erf,edf->erd", routed_gate_grad, expert_gate)
            + mm("erf,edf->erd", routed_up_grad, expert_up)
        )
        .astype(BF)
        .reshape(EXP_DEV, owners, capacity, width)
    )
    routed_res = mm("erf,efd->erd", routed_hidden, expert_down).astype(BF)
    routed_res = routed_res.reshape(EXP_DEV, owners, capacity, width)
    slot_gate_grad = jnp.sum(routed_res.astype(F32) * slot_out_grad.astype(F32), axis=-1)
    token_gate_grad = mm_high(
        "osct,osc,oe->ste", spread.astype(F32), slot_gate_grad, own_hot
    )
    gg_high, gg_low = high_low(token_gate_grad)
    seat = jnp.arange(owners)[:, None, None]
    placed = lambda pair: jnp.where(
        seat == me, pair[0][None], jnp.where(seat == me + 1 - 2 * core, pair[1][None], 0.0)
    )
    in_grad_part = (mm("osct,oscd->std", spread, expert_in_grad) + placed(shared_in_grad)).astype(BF)
    back = jnp.concatenate(
        [in_grad_part, gg_high, gg_low, jnp.zeros((owners, length, 128 - 2 * experts), BF)], axis=2
    ).reshape(owners * length, width + 128)
    back = lax.psum_scatter(back, OWN, scatter_dimension=0, tiled=True)

    expert_down_part = mm("erf,erd->efd", routed_hidden, res_grad).astype(BF)
    expert_gate_part = mm("erd,erf->edf", expert_in, routed_gate_grad).astype(BF)
    expert_up_part = mm("erd,erf->edf", expert_in, routed_up_grad).astype(BF)
    expert_parts = jnp.concatenate(
        [
            expert_gate_part.reshape(EXP_DEV, dp, rows, hidden),
            expert_up_part.reshape(EXP_DEV, dp, rows, hidden),
            expert_down_part.reshape(EXP_DEV, dp, rows, hidden),
        ],
        axis=0,
    ).transpose(1, 0, 2, 3)
    expert_share = lax.psum_scatter(expert_parts, DP, scatter_dimension=0, tiled=True)[0]
    expert_share = expert_share.astype(F32)

    out_part = (
        mm(
            "osct,oscd->std", (spread.astype(F32) * slot_gates[..., None]).astype(BF), routed_res
        )
        + placed(shared_out)
    ).astype(BF)
    out_part = out_part.reshape(depth, 2, length, width)
    kept = lax.dynamic_index_in_dim(out_part, core, 1, False)
    given = swap(lax.dynamic_index_in_dim(out_part, 1 - core, 1, False))
    chip_part = (kept.astype(F32) + given.astype(F32)).astype(BF)
    moe_out = lax.dynamic_index_in_dim(chip_part, level, 0, False).astype(F32)
    for step in range(1, depth):
        block = lax.dynamic_index_in_dim(chip_part, (level + step) % depth, 0, False)
        moe_out += lax.ppermute(
            block, "z", [(i, (i + step) % depth) for i in range(depth)]
        ).astype(F32)

    routed_in_grad = back[:, :width].astype(F32)
    probs_grad = back[:, width : width + experts].astype(F32) + back[
        :, width + experts : width + 2 * experts
    ].astype(F32)
    logits_grad = router_probs * (
        probs_grad - jnp.sum(router_probs * probs_grad, axis=-1, keepdims=True)
    )
    router_grad = product_high(ffn_in.astype(F32).T, logits_grad)
    router_in_grad = product_high(logits_grad, router_full.astype(F32).T)
    ffn_in_grad = routed_in_grad + router_in_grad
    ffn_gain_grad = jnp.sum(ffn_in_grad * residual * norm_two, axis=0)
    upstream_two = ffn_in_grad * gain_two_f
    residual_grad = (
        out_grad.astype(F32)
        + norm_two * upstream_two
        - residual * norm_two**3 * jnp.mean(upstream_two * residual, axis=-1, keepdims=True)
    )
    attn_grad_two = two(residual_grad.astype(BF)).reshape(2 * length, width)
    output_grad = product(context.T, attn_grad_two).astype(BF)
    output_grad = joined(half(output_grad, core, 1), swap(half(output_grad, 1 - core, 1)), core, 0)
    context_grad = by_head(product(attn_grad_two, output_half.T).astype(BF))
    value_grad = flat(mm("shqk,sqhd->skhd", probs_low, context_grad).astype(BF))
    probs_grad_att = mm("sqhd,skhd->shqk", context_grad, values)
    row_delta = jnp.sum(attn_probs * probs_grad_att, axis=-1, keepdims=True)
    scores_grad = (attn_probs * (probs_grad_att - row_delta)).astype(BF)
    query_grad = mm("shqk,skhd->sqhd", scores_grad, key_rot) * score_scale
    key_grad = mm("shqk,sqhd->skhd", scores_grad, query_rot) * score_scale
    query_pre_grad = flat(rotate(query_grad, cosine, -sine_part).astype(BF))
    key_pre_grad = flat(rotate(key_grad, cosine, -sine_part).astype(BF))
    query_wgrad = product(attn_in.T, query_pre_grad)
    key_wgrad = product(attn_in.T, key_pre_grad)
    value_wgrad = product(attn_in.T, value_grad)
    in_partial = (
        product(query_pre_grad, query_half.T)
        + product(key_pre_grad, key_half.T)
        + product(value_grad, value_half.T)
    ).reshape(2, length, width)
    attn_in_grad = in_partial[0] + swap(in_partial[1].astype(BF)).astype(F32)
    token_mine, norm_mine = token_f[0], norm_one[0]
    attn_gain_grad = jnp.sum(attn_in_grad * token_mine * norm_mine, axis=0)
    upstream_one = attn_in_grad * gain_one_f
    tokens_grad = (
        residual_grad
        + norm_mine * upstream_one
        - token_mine * norm_mine**3 * jnp.mean(upstream_one * token_mine, axis=-1, keepdims=True)
    )
    small_grads = jnp.concatenate(
        [router_grad, attn_gain_grad[:, None], ffn_gain_grad[:, None]], axis=1
    ).astype(BF)
    small_grads = jnp.pad(small_grads, ((0, 0), (0, 128 - small_grads.shape[1])))
    attn_parts = jnp.concatenate(
        [
            query_wgrad.astype(BF),
            key_wgrad.astype(BF),
            value_wgrad.astype(BF),
            output_grad,
            small_grads,
        ],
        axis=1,
    )
    attn_share = lax.psum_scatter(attn_parts, DP, scatter_dimension=0, tiled=True)
    shared_share = lax.psum(shared_share, "z")
    attn_share = lax.psum(attn_share, "z")
    attn_other, shared_other = swap(attn_share), swap(shared_share)
    attn_col = lambda i: joined(
        attn_share[:, i * wide : (i + 1) * wide],
        attn_other[:, i * wide : (i + 1) * wide],
        core,
        1,
    ).astype(F32)
    small_sum = attn_share[:, 4 * wide :].astype(F32) + attn_other[:, 4 * wide :].astype(F32)
    unit_col = lambda i: joined(
        shared_share[:, i * narrow : (i + 1) * narrow].reshape(rows, dp, 1, part),
        shared_other[:, i * narrow : (i + 1) * narrow].reshape(rows, dp, 1, part),
        core,
        2,
    ).reshape(rows, hidden).astype(F32)
    down_rows = joined(
        shared_share[:, 2 * narrow :].reshape(part, width),
        shared_other[:, 2 * narrow :].reshape(part, width),
        core,
        0,
    ).astype(F32)

    stream_out = residual + moe_out
    stat_rms = jnp.stack(
        [
            jnp.sqrt(jnp.mean(attn_out * attn_out)),
            jnp.sqrt(jnp.mean(moe_out * moe_out)),
            jnp.sqrt(jnp.mean(stream_out * stream_out)),
        ]
    )[None, :]
    return (
        stream_out.astype(BF),
        tokens_grad.astype(BF),
        attn_col(0),
        attn_col(1),
        attn_col(2),
        attn_col(3),
        small_sum[:, experts],
        small_sum[:, experts + 1],
        small_sum[:, :experts],
        unit_col(0),
        unit_col(1),
        down_rows,
        expert_share[0:2],
        expert_share[2:4],
        expert_share[4:6].reshape(EXP_DEV, shared_down.shape[0], width),
        stat_rms,
    )


def solution(mesh):
    side = math.isqrt(mesh.shape["dp"])
    fine = Mesh(
        mesh.devices.reshape(side, side, mesh.shape["expert"] // 2, 2), ("y", "x", "z", "c")
    )
    whole = P(("y", "x", "z", "c"), None)
    dense = P(DP, None)
    routed = P(OWN, None, None)
    in_specs = (
        whole, dense, dense, dense, dense, P(DP), P(DP), dense, dense, dense, dense,
        routed, routed, routed, whole, P(("y", "x", "z", "c")), whole,
    )
    shares = P(OWN, DP, None)
    out_specs = (
        whole, whole, dense, dense, dense, dense, P(DP), P(DP), dense, dense, dense, dense,
        shares, shares, shares, whole,
    )
    return jax.shard_map(body, mesh=fine, in_specs=in_specs, out_specs=out_specs, check_vma=False)
```

```python
import functools
import math

import jax
import jax.numpy as jnp
from jax import lax
from jax.experimental import pallas as pl
from jax.experimental.pallas import tpu as pltpu
from jax.sharding import Mesh
from jax.sharding import PartitionSpec as P

HEAD_DIM = 128
TOP = 7
EXP_DEV = 2
BF = jnp.bfloat16
F32 = jnp.float32
DP = ("y", "x")
OWN = ("z", "c")
NT = (((1,), (1,)), ((), ()))
TN = (((0,), (0,)), ((), ()))


def dot(first, second, dims=(((1,), (0,)), ((), ()))):
    return lax.dot_general(first, second, dims, preferred_element_type=F32)


def expert_kernel(count, width, capacity, experts, chunk, me_ref, slots_ref, *refs):
    rows_refs = refs[:count]
    grads_refs = refs[count : 2 * count]
    gate_ref, up_ref, down_ref = refs[2 * count : 2 * count + 3]
    in_mine, in_other, res_mine, res_other, xin, rgrad, hid, ggrad, ugrad = refs[-14:-5]
    ograd, in_ext, res_low, in_acc, out_acc = refs[-5:]
    step = pl.program_id(0)
    expert = me_ref[0] * EXP_DEV + step
    lane = lax.broadcasted_iota(jnp.int32, (capacity, 128), 1)
    mine = (lane == expert) | (lane == expert + experts)

    def spread(piece):
        want = slots_ref[step, piece]
        place = lax.broadcasted_iota(jnp.int32, (capacity, want.shape[-1]), 0)
        return (want == place).astype(F32)

    for piece in range(count):
        hot = spread(piece).astype(BF)
        area = pl.ds(piece * capacity, capacity)
        rows = dot(hot, rows_refs[piece][...])
        xin[0, area, :] = rows[:, :width].astype(BF)
        gates = jnp.sum(jnp.where(mine, rows[:, width:], 0.0), axis=1, keepdims=True)
        grads = dot(hot, grads_refs[piece][:, :width])
        ograd[area, :] = grads.astype(BF)
        rgrad[0, area, :] = (grads * gates).astype(BF)

    def part(index, carry):
        area = pl.ds(pl.multiple_of(index * chunk, chunk), chunk)
        rows = xin[0, area, :]
        res_grad = rgrad[0, area, :]
        gate = dot(rows, gate_ref[0])
        up = dot(rows, up_ref[0])
        hidden_grad = dot(res_grad, down_ref[0], NT)
        sig = jax.nn.sigmoid(gate)
        silu = gate * sig
        hidden = (silu * up).astype(BF)
        hid[0, area, :] = hidden
        gate_grad = (hidden_grad * up * (sig * (1.0 + gate * (1.0 - sig)))).astype(BF)
        up_grad = (hidden_grad * silu).astype(BF)
        ggrad[0, area, :] = gate_grad
        ugrad[0, area, :] = up_grad
        in_ext[area, pl.ds(0, width)] = (
            dot(gate_grad, gate_ref[0], NT) + dot(up_grad, up_ref[0], NT)
        ).astype(BF)
        res = dot(hidden, down_ref[0]).astype(BF)
        res_low[area, :] = res
        slot_gate = jnp.sum(res.astype(F32) * ograd[area, :].astype(F32), axis=1, keepdims=True)
        high = slot_gate.astype(BF).astype(F32)
        lanes = lax.broadcasted_iota(jnp.int32, (chunk, 128), 1)
        in_ext[area, pl.ds(width, 128)] = jnp.where(
            lanes == expert, high, jnp.where(lanes == expert + experts, slot_gate - high, 0.0)
        ).astype(BF)
        return carry

    lax.fori_loop(0, count * capacity // chunk, part, 0)

    for piece in range(count):
        hot = spread(piece)
        area = pl.ds(piece * capacity, capacity)
        low = hot.astype(BF)
        gates = jnp.sum(
            jnp.where(mine, dot(low, rows_refs[piece][:, width:]), 0.0), axis=1, keepdims=True
        )
        back = dot(low, in_ext[area, :], TN)
        result = dot((hot * gates).astype(BF), res_low[area, :], TN)
        in_out, res_out = ((in_mine, res_mine), (in_other, res_other))[piece % 2]

        @pl.when(step == 0)
        def _():
            in_acc[piece] = back
            out_acc[piece] = result

        @pl.when(step == EXP_DEV - 1)
        def _():
            in_out[piece // 2] = (in_acc[piece] + back).astype(BF)
            res_out[piece // 2] = (out_acc[piece] + result).astype(BF)


def expert_call(me, slots, rows, grads, gate, up, down, owners, first, carried=None):
    count = len(rows)
    length, wide = rows[0].shape
    width, hidden = gate.shape[1:]
    experts = EXP_DEV * owners
    capacity = 8 * length // experts
    block = count * capacity
    total = owners * capacity
    still = lambda shape: pl.BlockSpec(
        shape, lambda e, m: (0,) * len(shape), pipeline_mode=pl.Buffered(1)
    )
    weight = lambda a, b: pl.BlockSpec((1, a, b), lambda e, m: (e, 0, 0))
    kept = lambda cols: pl.BlockSpec((1, block, cols), lambda e, m: (e, first, 0))
    kept_cols = (width, width, hidden, hidden, hidden)
    in_specs = (
        [still((EXP_DEV, count, 1, length))]
        + [still((length, wide))] * (2 * count)
        + [weight(width, hidden), weight(width, hidden), weight(hidden, width)]
    )
    args = [me, slots, *rows, *grads, gate, up, down]
    alias = {}
    if carried is not None:
        for i, value in enumerate(carried):
            alias[len(args)] = 4 + i
            args.append(value)
            in_specs.append(pl.BlockSpec(memory_space=pl.ANY))
    sums = [(count // 2, length, wide)] * 2 + [(count // 2, length, width)] * 2
    return pl.pallas_call(
        functools.partial(expert_kernel, count, width, capacity, experts, min(512, block)),
        out_shape=[jax.ShapeDtypeStruct(shape, BF) for shape in sums]
        + [jax.ShapeDtypeStruct((EXP_DEV, total, cols), BF) for cols in kept_cols],
        grid_spec=pltpu.PrefetchScalarGridSpec(
            num_scalar_prefetch=1,
            grid=(EXP_DEV,),
            in_specs=in_specs,
            out_specs=[still(shape) for shape in sums] + [kept(cols) for cols in kept_cols],
            scratch_shapes=[
                pltpu.VMEM((block, width), BF),
                pltpu.VMEM((block, wide), BF),
                pltpu.VMEM((block, width), BF),
                pltpu.VMEM((count, length, wide), F32),
                pltpu.VMEM((count, length, width), F32),
            ],
        ),
        input_output_aliases=alias,
        compiler_params=pltpu.CompilerParams(
            dimension_semantics=("arbitrary",), vmem_limit_bytes=60 * 1024 * 1024
        ),
        cost_estimate=pl.CostEstimate(
            flops=14 * EXP_DEV * block * width * hidden,
            transcendentals=EXP_DEV * block * hidden,
            bytes_accessed=60 * 1024 * 1024,
        ),
        name="experts",
    )(*args)


def place_kernel(count, offsets_ref, *refs):
    pieces, out = refs[:count], refs[count]
    for i in range(count):
        start = pl.multiple_of(offsets_ref[i], 16)
        out[pl.ds(start, pieces[i].shape[0]), :] = pieces[i][...]


def place(pieces, offsets, total):
    count, cols = len(pieces), pieces[0].shape[1]
    return pl.pallas_call(
        functools.partial(place_kernel, count),
        out_shape=jax.ShapeDtypeStruct((total, cols), pieces[0].dtype),
        in_specs=[pl.BlockSpec(memory_space=pltpu.SMEM)]
        + [pl.BlockSpec(memory_space=pltpu.VMEM)] * count,
        out_specs=pl.BlockSpec(memory_space=pltpu.VMEM),
        cost_estimate=pl.CostEstimate(
            flops=0, transcendentals=0, bytes_accessed=4 * total * cols
        ),
        name="place",
    )(jnp.stack(offsets).astype(jnp.int32), *pieces)


def product(first_arg, second_arg):
    return jnp.dot(first_arg, second_arg, preferred_element_type=F32)


def product_high(first_arg, second_arg):
    return jnp.dot(
        first_arg, second_arg, precision=lax.Precision.HIGHEST, preferred_element_type=F32
    )


def mm(spec, first_arg, second_arg):
    return jnp.einsum(spec, first_arg, second_arg, preferred_element_type=F32)


def rotary_tables(length, head_size):
    half_dim = head_size // 2
    frequency = 10000.0 ** (-jnp.arange(half_dim, dtype=F32) * 2.0 / head_size)
    angles = jnp.arange(length, dtype=F32)[:, None] * frequency[None, :]
    return (jnp.cos(angles), jnp.sin(angles))


def rotate(tensor, cosine, sine_part):
    half_dim = tensor.shape[-1] // 2
    first_half = tensor[..., :half_dim]
    second_half = tensor[..., half_dim:]
    cos_rows = cosine[:, None, :]
    sin_rows = sine_part[:, None, :]
    return jnp.concatenate(
        [
            first_half * cos_rows - second_half * sin_rows,
            first_half * sin_rows + second_half * cos_rows,
        ],
        axis=-1,
    )


def allowed_mask(length, piece_start, piece_len):
    row_index = jnp.arange(length, dtype=jnp.int32)[:, None]
    col_index = jnp.arange(length, dtype=jnp.int32)[None, :]
    row_inside = (row_index >= piece_start) & (row_index < piece_start + piece_len)
    col_inside = (col_index >= piece_start) & (col_index < piece_start + piece_len)
    return (col_index <= row_index) | row_inside & col_inside


def silu_grad(inputs):
    sigmoid_part = jax.nn.sigmoid(inputs)
    return sigmoid_part * (1.0 + inputs * (1.0 - sigmoid_part))


def high_low(values):
    high = values.astype(BF)
    low = (values - high.astype(F32)).astype(BF)
    return high, low


def shifted(value, axis, by):
    size = lax.axis_size(axis)
    return lax.ppermute(value, axis, [(i, (i + by) % size) for i in range(size)])


def swap(value):
    return shifted(value, "c", 1)


def half(value, index, axis):
    size = value.shape[axis] // 2
    return lax.dynamic_slice_in_dim(value, index * size, size, axis)


def joined(mine, other, core, axis):
    return jnp.where(
        core == 0, jnp.concatenate([mine, other], axis), jnp.concatenate([other, mine], axis)
    )


def pick(value, index, axis):
    return lax.dynamic_index_in_dim(value, index % value.shape[axis], axis, False)


def after(value, *first):
    return lax.optimization_barrier((value, *first))[0]


def ring_gather(value, axis):
    found = [value]
    for _ in range(lax.axis_size(axis) - 1):
        found.append(shifted(found[-1], axis, 1))
    return found


def gather_dp(value):
    rows = value.shape[0]
    cut = (rows // 2 + 15) // 16 * 16
    side = lax.axis_size("x")
    pieces, offsets = [], []
    for start, part, order in ((0, value[:cut], "xy"), (cut, value[cut:], "yx")):
        for first, kept in enumerate(ring_gather(part, order[0])):
            for second, piece in enumerate(ring_gather(kept, order[1])):
                back = dict(zip(order, (first, second)))
                pieces.append(piece)
                from_y = (lax.axis_index("y") - back["y"]) % side
                from_x = (lax.axis_index("x") - back["x"]) % side
                offsets.append((from_y * side + from_x) * rows + start)
    return place(pieces, offsets, rows * side * side)


def ring_reduce(value, axis, at):
    size, index = lax.axis_size(axis), lax.axis_index(axis)
    moving = pick(value, index - 1, at)
    for step in range(2, size + 1):
        other = shifted(moving, axis, 1)
        moving = (other.astype(F32) + pick(value, index - step, at).astype(F32)).astype(BF)
    return moving


def reduce_dp(value, order):
    dims = value.ndim
    if order == "yx":
        return ring_reduce(ring_reduce(value, "y", dims - 4), "x", dims - 4)
    return ring_reduce(ring_reduce(value, "x", dims - 3), "y", dims - 4)


def reduce_level(value):
    depth, level = lax.axis_size("z"), lax.axis_index("z")
    rows, cols = value.shape
    parts = value.reshape(depth, rows // depth, cols)
    total = pick(parts, level, 0).astype(F32)
    for step in range(1, depth):
        total += shifted(pick(parts, level + step, 0), "z", step).astype(F32)
    mine = total.astype(BF)
    found = [mine] + [shifted(mine, "z", step) for step in range(1, depth)]
    turned = jnp.stack(found[::-1] * 2)
    return lax.dynamic_slice_in_dim(turned, depth - 1 - level, depth, 0).reshape(rows, cols)


def body(
    tokens,
    query_weight,
    key_weight,
    value_weight,
    output_weight,
    attn_gain,
    ffn_gain,
    router_weight,
    shared_gate,
    shared_up,
    shared_down,
    expert_gate,
    expert_up,
    expert_down,
    expert_ids,
    piece_starts,
    out_grad,
):
    side = lax.axis_size("x")
    dp = side * side
    owners = lax.axis_size(OWN)
    depth = lax.axis_size("z")
    core = lax.axis_index("c")
    me = lax.axis_index(OWN)
    experts = EXP_DEV * owners
    length, width = tokens.shape
    rows = query_weight.shape[0]
    hidden = shared_gate.shape[1]
    part = hidden // (2 * dp)
    wide, narrow = width // 2, hidden // 2
    head_count = wide // HEAD_DIM
    score_scale = HEAD_DIM ** (-0.5)
    piece_len = min(256, length // 2)
    capacity = 8 * length // experts
    two = lambda mine: jnp.stack([mine, swap(mine)])

    small = jnp.concatenate([router_weight, attn_gain[:, None], ffn_gain[:, None]], axis=1)
    small = jnp.pad(small, ((0, 0), (0, 128 - small.shape[1])))
    first_full = gather_dp(
        jnp.concatenate(
            [half(query_weight, core, 1), half(key_weight, core, 1), half(value_weight, core, 1), small],
            axis=1,
        )
    )
    units = lambda weight: pick(weight.reshape(rows, dp, 2, part), core, 2).reshape(rows, narrow)
    second_shard = jnp.concatenate(
        [
            half(output_weight, core, 1),
            units(shared_gate),
            units(shared_up),
            half(shared_down, core, 0).reshape(rows, narrow),
        ],
        axis=1,
    )
    second_full = gather_dp(after(second_shard, first_full))
    tokens_two = two(tokens)
    starts_two = two(piece_starts[0])

    chosen = (expert_ids[:, :, None] == jnp.arange(experts, dtype=jnp.int32)).any(axis=1)
    chosen_low = jnp.pad(chosen.astype(BF), ((0, 0), (0, 128 - experts)))

    def spread_out(mine):
        found = []
        for step in range(depth):
            piece = shifted(mine, "z", step) if step else mine
            found += [piece, swap(piece)]
        return found

    grads_all = spread_out(jnp.concatenate([out_grad, chosen_low], axis=1))
    own = me * EXP_DEV + jnp.arange(EXP_DEV)
    own_hot = (own[:, None] == jnp.arange(experts)[None, :]).astype(F32)
    marks = jnp.stack([piece[:, width : width + experts] for piece in grads_all]).astype(F32)
    mask = mm("ste,oe->ost", marks, own_hot)
    slots = jnp.where(mask > 0, jnp.cumsum(mask, axis=2) - 1.0, -1.0).astype(jnp.int32)
    slots = slots[:, :, None, :]

    query_half = first_full[:, :wide]
    key_half = first_full[:, wide : 2 * wide]
    value_half = first_full[:, 2 * wide : 3 * wide]
    small_full = first_full[:, 3 * wide :]
    router_full = small_full[:, :experts]
    gain_one_f = small_full[:, experts].astype(F32)
    gain_two_f = small_full[:, experts + 1].astype(F32)
    output_cols = second_full[:, :wide]
    gate_half = second_full[:, wide : wide + narrow]
    up_half = second_full[:, wide + narrow : wide + 2 * narrow]
    down_half = second_full[:, wide + 2 * narrow :].reshape(narrow, width)
    output_half = joined(
        half(output_cols, core, 0), swap(half(output_cols, 1 - core, 0)), core, 1
    )

    token_f = tokens_two.astype(F32)
    norm_one = lax.rsqrt(jnp.mean(token_f * token_f, axis=-1, keepdims=True) + 1e-06)
    attn_in = (token_f * norm_one * gain_one_f).astype(BF).reshape(2 * length, width)
    cosine, sine_part = rotary_tables(length, HEAD_DIM)
    by_head = lambda value: value.reshape(2, length, head_count, HEAD_DIM)
    flat = lambda value: value.reshape(2 * length, wide)
    query_rot = rotate(by_head(product(attn_in, query_half)), cosine, sine_part).astype(BF)
    key_rot = rotate(by_head(product(attn_in, key_half)), cosine, sine_part).astype(BF)
    values = by_head(product(attn_in, value_half).astype(BF))
    allowed = jnp.stack([allowed_mask(length, starts_two[i], piece_len) for i in range(2)])
    scores = mm("sqhd,skhd->shqk", query_rot, key_rot) * score_scale
    scores = jnp.where(allowed[:, None], scores, -1e30)
    row_max = jnp.max(scores, axis=-1, keepdims=True)
    exps = jnp.exp(scores - row_max)
    attn_probs = exps / jnp.sum(exps, axis=-1, keepdims=True)
    probs_low = attn_probs.astype(BF)
    context = flat(mm("shqk,skhd->sqhd", probs_low, values).astype(BF))
    out_partial = product(context, output_half).reshape(2, length, width)
    attn_out = out_partial[0] + swap(out_partial[1].astype(BF)).astype(F32)
    residual = token_f[0] + attn_out
    norm_two = lax.rsqrt(jnp.mean(residual * residual, axis=-1, keepdims=True) + 1e-06)
    ffn_in = (residual * norm_two * gain_two_f).astype(BF)
    router_probs = jax.nn.softmax(product(ffn_in, router_full), axis=-1)
    gates = jnp.where(chosen, router_probs, 0.0)
    gates_high, gates_low = high_low(gates)
    sent = jnp.concatenate(
        [ffn_in, gates_high, gates_low, jnp.zeros((length, 128 - 2 * experts), BF)], axis=1
    )
    rows_all = spread_out(sent)

    ffn_two = jnp.stack([ffn_in, rows_all[1][:, :width]]).reshape(2 * length, width)
    grad_two = jnp.stack([out_grad, grads_all[1][:, :width]]).reshape(2 * length, width)
    shared_gate_act = product(ffn_two, gate_half)
    shared_up_act = product(ffn_two, up_half)
    shared_hidden = (jax.nn.silu(shared_gate_act) * shared_up_act).astype(BF)
    shared_out = product(shared_hidden, down_half).astype(BF).reshape(2, length, width)
    shared_hidden_grad = product(grad_two, down_half.T)
    shared_down_grad = product(shared_hidden.T, grad_two).astype(BF)
    shared_gate_act_grad = (shared_hidden_grad * shared_up_act * silu_grad(shared_gate_act)).astype(
        BF
    )
    shared_up_act_grad = (shared_hidden_grad * jax.nn.silu(shared_gate_act)).astype(BF)
    shared_gate_grad = product(ffn_two.T, shared_gate_act_grad).astype(BF)
    shared_up_grad = product(ffn_two.T, shared_up_act_grad).astype(BF)
    shared_in_grad = (
        (product(shared_gate_act_grad, gate_half.T) + product(shared_up_act_grad, up_half.T))
        .astype(BF)
        .reshape(2, length, width)
    )
    shares = lambda value: value.reshape(side, side, rows, -1)
    gate_share = reduce_dp(shares(shared_gate_grad), "yx")
    up_share = reduce_dp(shares(shared_up_grad), "xy")
    down_share = reduce_dp(shares(shared_down_grad), "yx")
    shared_share = reduce_level(jnp.concatenate([gate_share, up_share, down_share], axis=1))

    place_me = me.reshape(1).astype(jnp.int32)
    near = expert_call(
        place_me, slots[:, : owners // 2], rows_all[: owners // 2], grads_all[: owners // 2],
        expert_gate, expert_up, expert_down, owners, 0,
    )
    far = expert_call(
        place_me, slots[:, owners // 2 :], rows_all[owners // 2 :], grads_all[owners // 2 :],
        expert_gate, expert_up, expert_down, owners, 1, near[4:],
    )
    expert_in, res_grad, routed_hidden, routed_gate_grad, routed_up_grad = far[4:]

    def collected(mine, other, shared, barrier=None):
        chip = []
        for step in range(depth):
            own_part, far_part = mine[step], other[step]
            if step == 0:
                far_part = lax.dynamic_update_slice(
                    far_part, far_part[:, :width] + shared[1], (0, 0)
                )
            chip.append(own_part.astype(F32) + swap(far_part).astype(F32))
        total = chip[0]
        for step in range(1, depth):
            moving = chip[step].astype(BF)
            if barrier is not None:
                moving = after(moving, barrier)
            total += shifted(moving, "z", -step).astype(F32)
        return total

    unstack = lambda i: [call[i][k] for call in (near, far) for k in range(depth // 2)]
    back = collected(unstack(0), unstack(1), shared_in_grad)
    moe_out = collected(unstack(2), unstack(3), shared_out, back) + shared_out[0].astype(F32)

    down_grad = mm("erf,erd->efd", routed_hidden, res_grad).astype(BF)
    gate_grad = mm("erd,erf->edf", expert_in, routed_gate_grad).astype(BF)
    up_grad = mm("erd,erf->edf", expert_in, routed_up_grad).astype(BF)
    expert_shares = []
    for grad in (gate_grad, up_grad, down_grad):
        blocks = grad.reshape(EXP_DEV, side, side, grad.shape[1] // dp, grad.shape[2])
        expert_shares.append(
            jnp.stack([reduce_dp(blocks[0], "yx"), reduce_dp(blocks[1], "xy")]).astype(F32)
        )

    probs_grad = back[:, width : width + experts] + back[:, width + experts : width + 2 * experts]
    logits_grad = router_probs * (
        probs_grad - jnp.sum(router_probs * probs_grad, axis=-1, keepdims=True)
    )
    router_grad = product_high(ffn_in.astype(F32).T, logits_grad)
    router_in_grad = product_high(logits_grad, router_full.astype(F32).T)
    ffn_in_grad = back[:, :width] + shared_in_grad[0].astype(F32) + router_in_grad
    ffn_gain_grad = jnp.sum(ffn_in_grad * residual * norm_two, axis=0)
    upstream_two = ffn_in_grad * gain_two_f
    residual_grad = (
        out_grad.astype(F32)
        + norm_two * upstream_two
        - residual * norm_two**3 * jnp.mean(upstream_two * residual, axis=-1, keepdims=True)
    )
    attn_grad_two = two(residual_grad.astype(BF)).reshape(2 * length, width)
    output_grad = product(context.T, attn_grad_two).astype(BF)
    output_grad = joined(half(output_grad, core, 1), swap(half(output_grad, 1 - core, 1)), core, 0)
    context_grad = by_head(product(attn_grad_two, output_half.T).astype(BF))
    value_grad = flat(mm("shqk,sqhd->skhd", probs_low, context_grad).astype(BF))
    probs_grad_att = mm("sqhd,skhd->shqk", context_grad, values)
    row_delta = jnp.sum(attn_probs * probs_grad_att, axis=-1, keepdims=True)
    scores_grad = (attn_probs * (probs_grad_att - row_delta)).astype(BF)
    query_grad = mm("shqk,skhd->sqhd", scores_grad, key_rot) * score_scale
    key_grad = mm("shqk,sqhd->skhd", scores_grad, query_rot) * score_scale
    query_pre_grad = flat(rotate(query_grad, cosine, -sine_part).astype(BF))
    key_pre_grad = flat(rotate(key_grad, cosine, -sine_part).astype(BF))
    query_wgrad = product(attn_in.T, query_pre_grad).astype(BF)
    key_wgrad = product(attn_in.T, key_pre_grad).astype(BF)
    value_wgrad = product(attn_in.T, value_grad).astype(BF)
    in_partial = (
        product(query_pre_grad, query_half.T)
        + product(key_pre_grad, key_half.T)
        + product(value_grad, value_half.T)
    ).reshape(2, length, width)
    attn_in_grad = in_partial[0] + swap(in_partial[1].astype(BF)).astype(F32)
    token_mine, norm_mine = token_f[0], norm_one[0]
    attn_gain_grad = jnp.sum(attn_in_grad * token_mine * norm_mine, axis=0)
    upstream_one = attn_in_grad * gain_one_f
    tokens_grad = (
        residual_grad
        + norm_mine * upstream_one
        - token_mine * norm_mine**3 * jnp.mean(upstream_one * token_mine, axis=-1, keepdims=True)
    )
    small_grads = jnp.concatenate(
        [router_grad, attn_gain_grad[:, None], ffn_gain_grad[:, None]], axis=1
    ).astype(BF)
    small_grads = jnp.pad(small_grads, ((0, 0), (0, 128 - small_grads.shape[1])))
    output_share = reduce_dp(shares(output_grad), "yx")
    value_share = reduce_dp(shares(value_wgrad), "xy")
    early_share = reduce_level(jnp.concatenate([output_share, value_share], axis=1))
    query_share = reduce_dp(shares(query_wgrad), "yx")
    key_share = reduce_dp(shares(jnp.concatenate([key_wgrad, small_grads], axis=1)), "xy")
    late_share = reduce_level(jnp.concatenate([query_share, key_share], axis=1))

    early_other, late_other, shared_other = swap(early_share), swap(late_share), swap(shared_share)
    column = lambda mine, other, i: joined(
        mine[:, i * wide : (i + 1) * wide], other[:, i * wide : (i + 1) * wide], core, 1
    ).astype(F32)
    small_sum = late_share[:, 2 * wide :].astype(F32) + late_other[:, 2 * wide :].astype(F32)
    unit_col = lambda i: joined(
        shared_share[:, i * narrow : (i + 1) * narrow].reshape(rows, dp, 1, part),
        shared_other[:, i * narrow : (i + 1) * narrow].reshape(rows, dp, 1, part),
        core,
        2,
    ).reshape(rows, hidden).astype(F32)
    down_rows = joined(
        shared_share[:, 2 * narrow :].reshape(part, width),
        shared_other[:, 2 * narrow :].reshape(part, width),
        core,
        0,
    ).astype(F32)

    stream_out = residual + moe_out
    stat_rms = jnp.stack(
        [
            jnp.sqrt(jnp.mean(attn_out * attn_out)),
            jnp.sqrt(jnp.mean(moe_out * moe_out)),
            jnp.sqrt(jnp.mean(stream_out * stream_out)),
        ]
    )[None, :]
    return (
        stream_out.astype(BF),
        tokens_grad.astype(BF),
        column(late_share, late_other, 0),
        column(late_share, late_other, 1),
        column(early_share, early_other, 1),
        column(early_share, early_other, 0),
        small_sum[:, experts],
        small_sum[:, experts + 1],
        small_sum[:, :experts],
        unit_col(0),
        unit_col(1),
        down_rows,
        *expert_shares,
        stat_rms,
    )


def solution(mesh):
    side = math.isqrt(mesh.shape["dp"])
    fine = Mesh(
        mesh.devices.reshape(side, side, mesh.shape["expert"] // 2, 2), ("y", "x", "z", "c")
    )
    whole = P(("y", "x", "z", "c"), None)
    dense = P(DP, None)
    routed = P(OWN, None, None)
    in_specs = (
        whole, dense, dense, dense, dense, P(DP), P(DP), dense, dense, dense, dense,
        routed, routed, routed, whole, P(("y", "x", "z", "c")), whole,
    )
    shares = P(OWN, DP, None)
    out_specs = (
        whole, whole, dense, dense, dense, dense, P(DP), P(DP), dense, dense, dense, dense,
        shares, shares, shares, whole,
    )
    return jax.shard_map(body, mesh=fine, in_specs=in_specs, out_specs=out_specs, check_vma=False)
```

```python
import functools
import math

import jax
import jax.numpy as jnp
from jax import lax
from jax.experimental import pallas as pl
from jax.experimental.pallas import tpu as pltpu
from jax.sharding import Mesh
from jax.sharding import PartitionSpec as P

HEAD_DIM = 128
TOP = 7
EXP_DEV = 2
BF = jnp.bfloat16
F32 = jnp.float32
DP = ("y", "x")
OWN = ("z", "c")
NT = (((1,), (1,)), ((), ()))
TN = (((0,), (0,)), ((), ()))


def dot(first, second, dims=(((1,), (0,)), ((), ()))):
    return lax.dot_general(first, second, dims, preferred_element_type=F32)


def expert_kernel(count, width, capacity, experts, chunk, me_ref, slots_ref, *refs):
    rows_refs = refs[:count]
    grads_refs = refs[count : 2 * count]
    gate_ref, up_ref, down_ref = refs[2 * count : 2 * count + 3]
    sums = refs[-10 - count : -10]
    xin, rgrad, hid, ggrad, ugrad = refs[-10:-5]
    ograd, in_ext, res_low, in_acc, out_acc = refs[-5:]
    step = pl.program_id(0)
    expert = me_ref[0] * EXP_DEV + step
    lane = lax.broadcasted_iota(jnp.int32, (capacity, 128), 1)
    mine = (lane == expert) | (lane == expert + experts)

    def spread(piece):
        want = slots_ref[step, piece]
        place = lax.broadcasted_iota(jnp.int32, (capacity, want.shape[-1]), 0)
        return (want == place).astype(F32)

    for piece in range(count):
        hot = spread(piece).astype(BF)
        area = pl.ds(piece * capacity, capacity)
        rows = dot(hot, rows_refs[piece][...])
        xin[0, area, :] = rows[:, :width].astype(BF)
        gates = jnp.sum(jnp.where(mine, rows[:, width:], 0.0), axis=1, keepdims=True)
        grads = dot(hot, grads_refs[piece][:, :width])
        ograd[area, :] = grads.astype(BF)
        rgrad[0, area, :] = (grads * gates).astype(BF)

    def part(index, carry):
        area = pl.ds(pl.multiple_of(index * chunk, chunk), chunk)
        rows = xin[0, area, :]
        res_grad = rgrad[0, area, :]
        gate = dot(rows, gate_ref[0])
        up = dot(rows, up_ref[0])
        hidden_grad = dot(res_grad, down_ref[0], NT)
        sig = jax.nn.sigmoid(gate)
        silu = gate * sig
        hidden = (silu * up).astype(BF)
        hid[0, area, :] = hidden
        gate_grad = (hidden_grad * up * (sig * (1.0 + gate * (1.0 - sig)))).astype(BF)
        up_grad = (hidden_grad * silu).astype(BF)
        ggrad[0, area, :] = gate_grad
        ugrad[0, area, :] = up_grad
        in_ext[area, pl.ds(0, width)] = (
            dot(gate_grad, gate_ref[0], NT) + dot(up_grad, up_ref[0], NT)
        ).astype(BF)
        res = dot(hidden, down_ref[0]).astype(BF)
        res_low[area, :] = res
        slot_gate = jnp.sum(res.astype(F32) * ograd[area, :].astype(F32), axis=1, keepdims=True)
        high = slot_gate.astype(BF).astype(F32)
        lanes = lax.broadcasted_iota(jnp.int32, (chunk, 128), 1)
        in_ext[area, pl.ds(width, 128)] = jnp.where(
            lanes == expert, high, jnp.where(lanes == expert + experts, slot_gate - high, 0.0)
        ).astype(BF)
        return carry

    lax.fori_loop(0, count * capacity // chunk, part, 0)

    for piece in range(count):
        hot = spread(piece)
        area = pl.ds(piece * capacity, capacity)
        low = hot.astype(BF)
        gates = jnp.sum(
            jnp.where(mine, dot(low, rows_refs[piece][:, width:]), 0.0), axis=1, keepdims=True
        )
        back = dot(low, in_ext[area, :], TN)
        result = dot((hot * gates).astype(BF), res_low[area, :], TN)

        @pl.when(step == 0)
        def _():
            in_acc[piece] = back
            out_acc[piece] = result

        @pl.when(step == EXP_DEV - 1)
        def _():
            wide = back.shape[1]
            sums[piece][:, :wide] = (in_acc[piece] + back).astype(BF)
            sums[piece][:, wide:] = (out_acc[piece] + result).astype(BF)


def expert_call(me, slots, rows, grads, gate, up, down, owners, first, carried=None):
    count = len(rows)
    length, wide = rows[0].shape
    width, hidden = gate.shape[1:]
    experts = EXP_DEV * owners
    capacity = 8 * length // experts
    block = count * capacity
    total = owners * capacity
    still = lambda shape: pl.BlockSpec(
        shape, lambda e, m: (0,) * len(shape), pipeline_mode=pl.Buffered(1)
    )
    weight = lambda a, b: pl.BlockSpec((1, a, b), lambda e, m: (e, 0, 0))
    kept = lambda cols: pl.BlockSpec((1, block, cols), lambda e, m: (e, first, 0))
    kept_cols = (width, width, hidden, hidden, hidden)
    in_specs = (
        [still((EXP_DEV, count, 1, length))]
        + [still((length, wide))] * (2 * count)
        + [weight(width, hidden), weight(width, hidden), weight(hidden, width)]
    )
    args = [me, slots, *rows, *grads, gate, up, down]
    alias = {}
    if carried is not None:
        for i, value in enumerate(carried):
            alias[len(args)] = count + i
            args.append(value)
            in_specs.append(pl.BlockSpec(memory_space=pl.ANY))
    sums = [(length, wide + width)] * count
    return pl.pallas_call(
        functools.partial(expert_kernel, count, width, capacity, experts, min(512, block)),
        out_shape=[jax.ShapeDtypeStruct(shape, BF) for shape in sums]
        + [jax.ShapeDtypeStruct((EXP_DEV, total, cols), BF) for cols in kept_cols],
        grid_spec=pltpu.PrefetchScalarGridSpec(
            num_scalar_prefetch=1,
            grid=(EXP_DEV,),
            in_specs=in_specs,
            out_specs=[still(shape) for shape in sums] + [kept(cols) for cols in kept_cols],
            scratch_shapes=[
                pltpu.VMEM((block, width), BF),
                pltpu.VMEM((block, wide), BF),
                pltpu.VMEM((block, width), BF),
                pltpu.VMEM((count, length, wide), F32),
                pltpu.VMEM((count, length, width), F32),
            ],
        ),
        input_output_aliases=alias,
        compiler_params=pltpu.CompilerParams(
            dimension_semantics=("arbitrary",), vmem_limit_bytes=60 * 1024 * 1024
        ),
        cost_estimate=pl.CostEstimate(
            flops=14 * EXP_DEV * block * width * hidden,
            transcendentals=EXP_DEV * block * hidden,
            bytes_accessed=60 * 1024 * 1024,
        ),
        name="experts",
    )(*args)


def place_kernel(count, offsets_ref, *refs):
    pieces, out = refs[:count], refs[count]
    for i in range(count):
        start = pl.multiple_of(offsets_ref[i], 16)
        out[pl.ds(start, pieces[i].shape[0]), :] = pieces[i][...]


def place(pieces, offsets, total):
    count, cols = len(pieces), pieces[0].shape[1]
    return pl.pallas_call(
        functools.partial(place_kernel, count),
        out_shape=jax.ShapeDtypeStruct((total, cols), pieces[0].dtype),
        in_specs=[pl.BlockSpec(memory_space=pltpu.SMEM)]
        + [pl.BlockSpec(memory_space=pltpu.VMEM)] * count,
        out_specs=pl.BlockSpec(memory_space=pltpu.VMEM),
        cost_estimate=pl.CostEstimate(
            flops=0, transcendentals=0, bytes_accessed=4 * total * cols
        ),
        name="place",
    )(jnp.stack(offsets).astype(jnp.int32), *pieces)


def product(first_arg, second_arg):
    return jnp.dot(first_arg, second_arg, preferred_element_type=F32)


def product_high(first_arg, second_arg):
    return jnp.dot(
        first_arg, second_arg, precision=lax.Precision.HIGHEST, preferred_element_type=F32
    )


def mm(spec, first_arg, second_arg):
    return jnp.einsum(spec, first_arg, second_arg, preferred_element_type=F32)


def rotary_tables(length, head_size):
    half_dim = head_size // 2
    frequency = 10000.0 ** (-jnp.arange(half_dim, dtype=F32) * 2.0 / head_size)
    angles = jnp.arange(length, dtype=F32)[:, None] * frequency[None, :]
    return (jnp.cos(angles), jnp.sin(angles))


def rotate(tensor, cosine, sine_part):
    half_dim = tensor.shape[-1] // 2
    first_half = tensor[..., :half_dim]
    second_half = tensor[..., half_dim:]
    cos_rows = cosine[:, None, :]
    sin_rows = sine_part[:, None, :]
    return jnp.concatenate(
        [
            first_half * cos_rows - second_half * sin_rows,
            first_half * sin_rows + second_half * cos_rows,
        ],
        axis=-1,
    )


def allowed_mask(length, piece_start, piece_len):
    row_index = jnp.arange(length, dtype=jnp.int32)[:, None]
    col_index = jnp.arange(length, dtype=jnp.int32)[None, :]
    row_inside = (row_index >= piece_start) & (row_index < piece_start + piece_len)
    col_inside = (col_index >= piece_start) & (col_index < piece_start + piece_len)
    return (col_index <= row_index) | row_inside & col_inside


def silu_grad(inputs):
    sigmoid_part = jax.nn.sigmoid(inputs)
    return sigmoid_part * (1.0 + inputs * (1.0 - sigmoid_part))


def high_low(values):
    high = values.astype(BF)
    low = (values - high.astype(F32)).astype(BF)
    return high, low


def shifted(value, axis, by):
    size = lax.axis_size(axis)
    return lax.ppermute(value, axis, [(i, (i + by) % size) for i in range(size)])


def swap(value):
    return shifted(value, "c", 1)


def half(value, index, axis):
    size = value.shape[axis] // 2
    return lax.dynamic_slice_in_dim(value, index * size, size, axis)


def joined(mine, other, core, axis):
    return jnp.where(
        core == 0, jnp.concatenate([mine, other], axis), jnp.concatenate([other, mine], axis)
    )


def pick(value, index, axis):
    return lax.dynamic_index_in_dim(value, index % value.shape[axis], axis, False)


def after(values, *first):
    if not isinstance(values, (list, tuple)):
        return lax.optimization_barrier((values, *first))[0]
    return list(lax.optimization_barrier((*values, *first))[: len(values)])


def ring_gather(value, axis):
    found = [value]
    for _ in range(lax.axis_size(axis) - 1):
        found.append(shifted(found[-1], axis, 1))
    return found


def gather_dp(value):
    rows = value.shape[0]
    cut = (rows // 2 + 15) // 16 * 16
    side = lax.axis_size("x")
    pieces, offsets = [], []

    def add(piece, start, back):
        from_y = (lax.axis_index("y") - back["y"]) % side
        from_x = (lax.axis_index("x") - back["x"]) % side
        pieces.append(piece)
        offsets.append((from_y * side + from_x) * rows + start)

    add(value, 0, {"x": 0, "y": 0})
    along = {axis: ring_gather(value, axis) for axis in "xy"}
    for axis, other in ("xy", "yx"):
        for step in range(1, side):
            add(along[axis][step], 0, {axis: step, other: 0})
    near = len(pieces)
    for start, stop, order in ((0, cut, "xy"), (cut, rows, "yx")):
        for first in range(1, side):
            kept = ring_gather(along[order[0]][first][start:stop], order[1])
            for second in range(1, side):
                add(kept[second], start, {order[0]: first, order[1]: second})
    return place(pieces, offsets, rows * side * side), pieces[1:near], pieces[near:]


def ring_reduce(value, axis, at, late):
    size, index = lax.axis_size(axis), lax.axis_index(axis)
    moving = pick(value, index - 1, at)
    for step in range(2, size + 1):
        other = shifted(moving, axis, 1)
        if late:
            other = after(other, *late)
        moving = (other.astype(F32) + pick(value, index - step, at).astype(F32)).astype(BF)
    return moving


def stage_one(values, orders, first=(), late=()):
    values = after(values, *first) if first else values
    return [ring_reduce(v, o[0], "yx".index(o[0]), late) for v, o in zip(values, orders)]


def stage_two(values, orders, first=(), late=()):
    values = after(values, *first) if first else values
    return [ring_reduce(v, o[1], 0, late) for v, o in zip(values, orders)]


def reduce_level(value):
    depth, level = lax.axis_size("z"), lax.axis_index("z")
    rows, cols = value.shape
    parts = value.reshape(depth, rows // depth, cols)
    total = pick(parts, level, 0).astype(F32)
    for step in range(1, depth):
        total += shifted(pick(parts, level + step, 0), "z", step).astype(F32)
    mine = total.astype(BF)
    found = [mine] + [shifted(mine, "z", step) for step in range(1, depth)]
    turned = jnp.stack(found[::-1] * 2)
    return lax.dynamic_slice_in_dim(turned, depth - 1 - level, depth, 0).reshape(rows, cols)


def body(
    tokens,
    query_weight,
    key_weight,
    value_weight,
    output_weight,
    attn_gain,
    ffn_gain,
    router_weight,
    shared_gate,
    shared_up,
    shared_down,
    expert_gate,
    expert_up,
    expert_down,
    expert_ids,
    piece_starts,
    out_grad,
):
    side = lax.axis_size("x")
    dp = side * side
    owners = lax.axis_size(OWN)
    depth = lax.axis_size("z")
    core = lax.axis_index("c")
    me = lax.axis_index(OWN)
    experts = EXP_DEV * owners
    length, width = tokens.shape
    rows = query_weight.shape[0]
    hidden = shared_gate.shape[1]
    wide, narrow = width // 2, hidden // 2
    head_count = wide // HEAD_DIM
    score_scale = HEAD_DIM ** (-0.5)
    piece_len = min(256, length // 2)
    capacity = 8 * length // experts
    two = lambda mine: jnp.stack([mine, swap(mine)])

    small = jnp.concatenate([router_weight, attn_gain[:, None], ffn_gain[:, None]], axis=1)
    small = jnp.pad(small, ((0, 0), (0, 128 - small.shape[1])))
    first_full, first_near, first_far = gather_dp(
        jnp.concatenate(
            [half(query_weight, core, 1), half(key_weight, core, 1), half(value_weight, core, 1), small],
            axis=1,
        )
    )
    tokens_two = two(tokens)
    starts_two = two(piece_starts[0])
    later = after([output_weight, shared_gate, shared_up, shared_down, out_grad], *first_near)
    second_shard = jnp.concatenate(
        [half(later[0], core, 1), half(later[1], core, 1), half(later[2], core, 1)]
        + [half(later[3], core, 1).reshape(rows, narrow)],
        axis=1,
    )
    second_full, _, _ = gather_dp(after(second_shard, *first_far))

    chosen = (expert_ids[:, :, None] == jnp.arange(experts, dtype=jnp.int32)).any(axis=1)
    chosen_low = jnp.pad(chosen.astype(BF), ((0, 0), (0, 128 - experts)))

    levels = [0, depth // 2] + [step for step in range(1, depth) if step != depth // 2]

    def spread_out(mine, paired, *filler):
        found = {0: mine, levels[1]: shifted(mine, "z", levels[1])}
        mine = after(mine, found[levels[1]], *filler)
        for step in levels[2:]:
            found[step] = shifted(mine, "z", step)
        rest = [piece for step in levels[1:] for piece in (found[step], swap(found[step]))]
        return [found[0], paired, *rest]

    grads_sent = jnp.concatenate([later[4], chosen_low], axis=1)
    grads_all = spread_out(grads_sent, swap(grads_sent))
    own = me * EXP_DEV + jnp.arange(EXP_DEV)
    own_hot = (own[:, None] == jnp.arange(experts)[None, :]).astype(F32)
    marks = jnp.stack([piece[:, width : width + experts] for piece in grads_all]).astype(F32)
    mask = mm("ste,oe->ost", marks, own_hot)
    slots = jnp.where(mask > 0, jnp.cumsum(mask, axis=2) - 1.0, -1.0).astype(jnp.int32)
    slots = slots[:, :, None, :]

    query_half = first_full[:, :wide]
    key_half = first_full[:, wide : 2 * wide]
    value_half = first_full[:, 2 * wide : 3 * wide]
    small_full = first_full[:, 3 * wide :]
    router_full = small_full[:, :experts]
    gain_one_f = small_full[:, experts].astype(F32)
    gain_two_f = small_full[:, experts + 1].astype(F32)
    output_cols = second_full[:, :wide]
    gate_half = second_full[:, wide : wide + narrow]
    up_half = second_full[:, wide + narrow : wide + 2 * narrow]
    down_cols = second_full[:, wide + 2 * narrow :].reshape(hidden, wide)
    met = swap(
        jnp.concatenate([half(output_cols, 1 - core, 0), half(down_cols, 1 - core, 0)], axis=0)
    )
    output_half = joined(half(output_cols, core, 0), met[:wide], core, 1)
    down_half = joined(half(down_cols, core, 0), met[wide:], core, 1)

    token_f = tokens_two.astype(F32)
    norm_one = lax.rsqrt(jnp.mean(token_f * token_f, axis=-1, keepdims=True) + 1e-06)
    attn_in = (token_f * norm_one * gain_one_f).astype(BF).reshape(2 * length, width)
    cosine, sine_part = rotary_tables(length, HEAD_DIM)
    by_head = lambda value: value.reshape(2, length, head_count, HEAD_DIM)
    flat = lambda value: value.reshape(2 * length, wide)
    query_rot = rotate(by_head(product(attn_in, query_half)), cosine, sine_part).astype(BF)
    key_rot = rotate(by_head(product(attn_in, key_half)), cosine, sine_part).astype(BF)
    values = by_head(product(attn_in, value_half).astype(BF))
    allowed = jnp.stack([allowed_mask(length, starts_two[i], piece_len) for i in range(2)])
    scores = mm("sqhd,skhd->shqk", query_rot, key_rot) * score_scale
    scores = jnp.where(allowed[:, None], scores, -1e30)
    row_max = jnp.max(scores, axis=-1, keepdims=True)
    exps = jnp.exp(scores - row_max)
    attn_probs = exps / jnp.sum(exps, axis=-1, keepdims=True)
    probs_low = attn_probs.astype(BF)
    context = flat(mm("shqk,skhd->sqhd", probs_low, values).astype(BF))
    out_partial = product(context, output_half).reshape(2, length, width)
    attn_out = out_partial[0] + swap(out_partial[1].astype(BF)).astype(F32)
    residual = token_f[0] + attn_out
    norm_two = lax.rsqrt(jnp.mean(residual * residual, axis=-1, keepdims=True) + 1e-06)
    ffn_in = (residual * norm_two * gain_two_f).astype(BF)
    router_probs = jax.nn.softmax(product(ffn_in, router_full), axis=-1)
    gates = jnp.where(chosen, router_probs, 0.0)
    gates_high, gates_low = high_low(gates)
    sent = jnp.concatenate(
        [ffn_in, gates_high, gates_low, jnp.zeros((length, 128 - 2 * experts), BF)], axis=1
    )
    sent_other = swap(sent)

    ffn_two = jnp.stack([ffn_in, sent_other[:, :width]]).reshape(2 * length, width)
    grad_two = jnp.stack([out_grad, grads_all[1][:, :width]]).reshape(2 * length, width)
    shared_gate_act = product(ffn_two, gate_half)
    shared_up_act = product(ffn_two, up_half)
    shared_hidden = (jax.nn.silu(shared_gate_act) * shared_up_act).astype(BF)
    shared_out = product(shared_hidden, down_half).astype(BF).reshape(2, length, width)
    shared_hidden_grad = product(grad_two, down_half.T)
    shared_down_grad = product(shared_hidden.T, grad_two).astype(BF)
    shared_gate_act_grad = (shared_hidden_grad * shared_up_act * silu_grad(shared_gate_act)).astype(
        BF
    )
    shared_up_act_grad = (shared_hidden_grad * jax.nn.silu(shared_gate_act)).astype(BF)
    shared_gate_grad = product(ffn_two.T, shared_gate_act_grad).astype(BF)
    shared_up_grad = product(ffn_two.T, shared_up_act_grad).astype(BF)
    shared_in_grad = (
        (product(shared_gate_act_grad, gate_half.T) + product(shared_up_act_grad, up_half.T))
        .astype(BF)
        .reshape(2, length, width)
    )
    rows_all = spread_out(sent, sent_other, shared_gate_grad, shared_in_grad)
    shared_both = jnp.concatenate(
        [shared_in_grad, jnp.zeros((2, length, 128), BF), shared_out], axis=2
    )
    turn = lambda grad: joined(half(grad, core, 1), swap(half(grad, 1 - core, 1)), core, 0)
    shares = lambda value: value.reshape(side, side, value.shape[0] // dp, -1)
    shared_orders = ("yx", "xy", "yx")
    shared_part = [shares(g) for g in (shared_gate_grad, shared_up_grad, turn(shared_down_grad))]

    place_me = me.reshape(1).astype(jnp.int32)
    block = owners // 2
    near = expert_call(
        place_me, slots[:, :block], rows_all[:block], grads_all[:block],
        expert_gate, expert_up, expert_down, owners, 0,
    )
    wider = width + 128
    shared_part = stage_one(shared_part, shared_orders, late=(near[block],))
    chips = [None] * depth
    for place_at in range(1, depth // 2):
        chips[place_at] = near[2 * place_at].astype(F32) + swap(near[2 * place_at + 1]).astype(F32)
    sent_back = [None] + [chips[i][:, :wider].astype(BF) for i in range(1, depth // 2)]
    far_slots = after(slots[:, block:], *sent_back[1:])
    far = expert_call(
        place_me, far_slots, rows_all[block:], grads_all[block:],
        expert_gate, expert_up, expert_down, owners, 1, near[block:],
    )
    expert_in, res_grad, routed_hidden, routed_gate_grad, routed_up_grad = far[block:]
    for place_at in range(depth // 2, depth):
        mine, other = far[2 * place_at - block], far[2 * place_at - block + 1]
        chips[place_at] = mine.astype(F32) + swap(other).astype(F32)
        sent_back.append(chips[place_at][:, :wider].astype(BF))
    back_in = [shifted(sent_back[i], "z", -levels[i]) for i in range(1, depth)]
    shared_part = stage_two(shared_part, shared_orders, late=(far[block],))

    gate_grad = mm("erd,erf->edf", expert_in, routed_gate_grad).astype(BF)
    up_grad = mm("erd,erf->edf", expert_in, routed_up_grad).astype(BF)
    down_grad = mm("erf,erd->efd", routed_hidden, res_grad).astype(BF)
    both = ("yx", "xy")
    blocks = [
        [grad[e].reshape(side, side, grad.shape[1] // dp, grad.shape[2]) for e in range(EXP_DEV)]
        for grad in (gate_grad, up_grad, down_grad)
    ]
    gate_one = stage_one(blocks[0], both)
    back_in = after(back_in, *gate_one)
    chips[0] = (near[0].astype(F32) + shared_both[0].astype(F32)) + swap(
        near[1] + shared_both[1]
    ).astype(F32)
    back = chips[0][:, :wider]
    for piece in back_in:
        back += piece.astype(F32)

    probs_grad = back[:, width : width + experts] + back[:, width + experts : width + 2 * experts]
    logits_grad = router_probs * (
        probs_grad - jnp.sum(router_probs * probs_grad, axis=-1, keepdims=True)
    )
    router_grad = product_high(ffn_in.astype(F32).T, logits_grad)
    router_in_grad = product_high(logits_grad, router_full.astype(F32).T)
    ffn_in_grad = back[:, :width] + router_in_grad
    ffn_gain_grad = jnp.sum(ffn_in_grad * residual * norm_two, axis=0)
    upstream_two = ffn_in_grad * gain_two_f
    residual_grad = (
        out_grad.astype(F32)
        + norm_two * upstream_two
        - residual * norm_two**3 * jnp.mean(upstream_two * residual, axis=-1, keepdims=True)
    )
    residual_low = residual_grad.astype(BF)
    up_one = stage_one(blocks[1], both, gate_one, (residual_low,))
    gate_two = stage_two(gate_one, both, (back,), ())
    attn_grad_two = two(residual_low).reshape(2 * length, width)
    output_grad = product(context.T, attn_grad_two).astype(BF)
    output_grad = turn(output_grad)
    context_grad = by_head(product(attn_grad_two, output_half.T).astype(BF))
    value_grad = flat(mm("shqk,sqhd->skhd", probs_low, context_grad).astype(BF))
    probs_grad_att = mm("sqhd,skhd->shqk", context_grad, values)
    row_delta = jnp.sum(attn_probs * probs_grad_att, axis=-1, keepdims=True)
    scores_grad = (attn_probs * (probs_grad_att - row_delta)).astype(BF)
    down_one = stage_one(blocks[2], both, up_one, (scores_grad,))
    up_two = stage_two(up_one, both, gate_two, (scores_grad,))
    query_grad = mm("shqk,skhd->sqhd", scores_grad, key_rot) * score_scale
    key_grad = mm("shqk,sqhd->skhd", scores_grad, query_rot) * score_scale
    query_pre_grad = flat(rotate(query_grad, cosine, -sine_part).astype(BF))
    key_pre_grad = flat(rotate(key_grad, cosine, -sine_part).astype(BF))
    query_wgrad = product(attn_in.T, query_pre_grad).astype(BF)
    key_wgrad = product(attn_in.T, key_pre_grad).astype(BF)
    value_wgrad = product(attn_in.T, value_grad).astype(BF)
    in_partial = (
        product(query_pre_grad, query_half.T)
        + product(key_pre_grad, key_half.T)
        + product(value_grad, value_half.T)
    ).reshape(2, length, width)
    attn_in_grad = in_partial[0] + swap(in_partial[1].astype(BF)).astype(F32)
    token_mine, norm_mine = token_f[0], norm_one[0]
    attn_gain_grad = jnp.sum(attn_in_grad * token_mine * norm_mine, axis=0)
    upstream_one = attn_in_grad * gain_one_f
    tokens_grad = (
        residual_grad
        + norm_mine * upstream_one
        - token_mine * norm_mine**3 * jnp.mean(upstream_one * token_mine, axis=-1, keepdims=True)
    )
    small_grads = jnp.concatenate(
        [router_grad, attn_gain_grad[:, None], ffn_gain_grad[:, None]], axis=1
    ).astype(BF)
    small_grads = jnp.pad(small_grads, ((0, 0), (0, 128 - small_grads.shape[1])))
    early = stage_one([shares(output_grad), shares(value_wgrad)], both, (*down_one, *up_two))
    down_two = stage_two(down_one, both)
    early = stage_two(early, both)
    late = [shares(query_wgrad), shares(jnp.concatenate([key_wgrad, small_grads], axis=1))]
    late = stage_two(stage_one(late, both, early), both)
    expert_shares = [jnp.stack(pair).astype(F32) for pair in (gate_two, up_two, down_two)]
    shared_share = lax.psum(
        jnp.concatenate([*shared_part[:2], shared_part[2].reshape(rows, narrow)], axis=1), "z"
    )
    early_share = reduce_level(jnp.concatenate(early, axis=1))
    late_share = reduce_level(jnp.concatenate(late, axis=1))

    moe_out = chips[0][:, wider:]
    for i in range(1, depth):
        moving = after(chips[i][:, wider:].astype(BF), back)
        if i > 1:
            moving = after(moving, piece)
        piece = after(shifted(moving, "z", -levels[i]), (scores_grad, query_wgrad, early[0])[min(i - 1, 2)])
        moe_out += piece.astype(F32)

    early_other, late_other, shared_other = swap(early_share), swap(late_share), swap(shared_share)
    column = lambda mine, other, start, size: joined(
        mine[:, start : start + size], other[:, start : start + size], core, 1
    ).astype(F32)
    small_sum = late_share[:, 2 * wide :].astype(F32) + late_other[:, 2 * wide :].astype(F32)
    down_rows = joined(
        shared_share[:, 2 * narrow :].reshape(-1, wide),
        shared_other[:, 2 * narrow :].reshape(-1, wide),
        core,
        1,
    ).astype(F32)

    stream_out = residual + moe_out
    stat_rms = jnp.stack(
        [
            jnp.sqrt(jnp.mean(attn_out * attn_out)),
            jnp.sqrt(jnp.mean(moe_out * moe_out)),
            jnp.sqrt(jnp.mean(stream_out * stream_out)),
        ]
    )[None, :]
    return (
        stream_out.astype(BF),
        tokens_grad.astype(BF),
        column(late_share, late_other, 0, wide),
        column(late_share, late_other, wide, wide),
        column(early_share, early_other, wide, wide),
        column(early_share, early_other, 0, wide),
        small_sum[:, experts],
        small_sum[:, experts + 1],
        small_sum[:, :experts],
        column(shared_share, shared_other, 0, narrow),
        column(shared_share, shared_other, narrow, narrow),
        down_rows,
        *expert_shares,
        stat_rms,
    )


def solution(mesh):
    side = math.isqrt(mesh.shape["dp"])
    fine = Mesh(
        mesh.devices.reshape(side, side, mesh.shape["expert"] // 2, 2), ("y", "x", "z", "c")
    )
    whole = P(("y", "x", "z", "c"), None)
    dense = P(DP, None)
    routed = P(OWN, None, None)
    in_specs = (
        whole, dense, dense, dense, dense, P(DP), P(DP), dense, dense, dense, dense,
        routed, routed, routed, whole, P(("y", "x", "z", "c")), whole,
    )
    shares = P(OWN, DP, None)
    out_specs = (
        whole, whole, dense, dense, dense, dense, P(DP), P(DP), dense, dense, dense, dense,
        shares, shares, shares, whole,
    )
    return jax.shard_map(body, mesh=fine, in_specs=in_specs, out_specs=out_specs, check_vma=False)
```

```python
import functools
import math

import jax
import jax.numpy as jnp
from jax import lax
from jax.experimental import pallas as pl
from jax.experimental.pallas import tpu as pltpu
from jax.sharding import Mesh
from jax.sharding import PartitionSpec as P

HEAD_DIM = 128
TOP = 7
EXP_DEV = 2
BF = jnp.bfloat16
F32 = jnp.float32
DP = ("y", "x")
OWN = ("z", "c")
NT = (((1,), (1,)), ((), ()))
TN = (((0,), (0,)), ((), ()))


def dot(first, second, dims=(((1,), (0,)), ((), ()))):
    return lax.dot_general(first, second, dims, preferred_element_type=F32)


def expert_kernel(count, width, capacity, experts, chunk, me_ref, slots_ref, *refs):
    rows_refs = refs[:count]
    grads_refs = refs[count : 2 * count]
    gate_ref, up_ref, down_ref = refs[2 * count : 2 * count + 3]
    sums = refs[-10 - count : -10]
    xin, rgrad, hid, ggrad, ugrad = refs[-10:-5]
    ograd, in_ext, res_low, in_acc, out_acc = refs[-5:]
    step = pl.program_id(0)
    expert = me_ref[0] * EXP_DEV + step
    lane = lax.broadcasted_iota(jnp.int32, (capacity, 128), 1)
    mine = (lane == expert) | (lane == expert + experts)

    def spread(piece):
        want = slots_ref[step, piece]
        place = lax.broadcasted_iota(jnp.int32, (capacity, want.shape[-1]), 0)
        return (want == place).astype(F32)

    for piece in range(count):
        hot = spread(piece).astype(BF)
        area = pl.ds(piece * capacity, capacity)
        rows = dot(hot, rows_refs[piece][...])
        xin[0, area, :] = rows[:, :width].astype(BF)
        gates = jnp.sum(jnp.where(mine, rows[:, width:], 0.0), axis=1, keepdims=True)
        grads = dot(hot, grads_refs[piece][:, :width])
        ograd[area, :] = grads.astype(BF)
        rgrad[0, area, :] = (grads * gates).astype(BF)

    def part(index, carry):
        area = pl.ds(pl.multiple_of(index * chunk, chunk), chunk)
        rows = xin[0, area, :]
        res_grad = rgrad[0, area, :]
        gate = dot(rows, gate_ref[0])
        up = dot(rows, up_ref[0])
        hidden_grad = dot(res_grad, down_ref[0], NT)
        sig = jax.nn.sigmoid(gate)
        silu = gate * sig
        hidden = (silu * up).astype(BF)
        hid[0, area, :] = hidden
        gate_grad = (hidden_grad * up * (sig * (1.0 + gate * (1.0 - sig)))).astype(BF)
        up_grad = (hidden_grad * silu).astype(BF)
        ggrad[0, area, :] = gate_grad
        ugrad[0, area, :] = up_grad
        in_ext[area, pl.ds(0, width)] = (
            dot(gate_grad, gate_ref[0], NT) + dot(up_grad, up_ref[0], NT)
        ).astype(BF)
        res = dot(hidden, down_ref[0]).astype(BF)
        res_low[area, :] = res
        slot_gate = jnp.sum(res.astype(F32) * ograd[area, :].astype(F32), axis=1, keepdims=True)
        high = slot_gate.astype(BF).astype(F32)
        lanes = lax.broadcasted_iota(jnp.int32, (chunk, 128), 1)
        in_ext[area, pl.ds(width, 128)] = jnp.where(
            lanes == expert, high, jnp.where(lanes == expert + experts, slot_gate - high, 0.0)
        ).astype(BF)
        return carry

    lax.fori_loop(0, count * capacity // chunk, part, 0)

    for piece in range(count):
        hot = spread(piece)
        area = pl.ds(piece * capacity, capacity)
        low = hot.astype(BF)
        gates = jnp.sum(
            jnp.where(mine, dot(low, rows_refs[piece][:, width:]), 0.0), axis=1, keepdims=True
        )
        back = dot(low, in_ext[area, :], TN)
        result = dot((hot * gates).astype(BF), res_low[area, :], TN)

        @pl.when(step == 0)
        def _():
            in_acc[piece] = back
            out_acc[piece] = result

        @pl.when(step == EXP_DEV - 1)
        def _():
            wide = back.shape[1]
            sums[piece][:, :wide] = (in_acc[piece] + back).astype(BF)
            sums[piece][:, wide:] = (out_acc[piece] + result).astype(BF)


def expert_call(me, slots, rows, grads, gate, up, down, owners, first, carried=None):
    count = len(rows)
    length, wide = rows[0].shape
    width, hidden = gate.shape[1:]
    experts = EXP_DEV * owners
    capacity = 8 * length // experts
    block = count * capacity
    total = owners * capacity
    still = lambda shape: pl.BlockSpec(
        shape, lambda e, m: (0,) * len(shape), pipeline_mode=pl.Buffered(1)
    )
    weight = lambda a, b: pl.BlockSpec((1, a, b), lambda e, m: (e, 0, 0))
    kept = lambda cols: pl.BlockSpec((1, block, cols), lambda e, m: (e, first, 0))
    kept_cols = (width, width, hidden, hidden, hidden)
    in_specs = (
        [still((EXP_DEV, count, 1, length))]
        + [still((length, wide))] * (2 * count)
        + [weight(width, hidden), weight(width, hidden), weight(hidden, width)]
    )
    args = [me, slots, *rows, *grads, gate, up, down]
    alias = {}
    if carried is not None:
        for i, value in enumerate(carried):
            alias[len(args)] = count + i
            args.append(value)
            in_specs.append(pl.BlockSpec(memory_space=pl.ANY))
    sums = [(length, wide + width)] * count
    return pl.pallas_call(
        functools.partial(expert_kernel, count, width, capacity, experts, min(512, block)),
        out_shape=[jax.ShapeDtypeStruct(shape, BF) for shape in sums]
        + [jax.ShapeDtypeStruct((EXP_DEV, total, cols), BF) for cols in kept_cols],
        grid_spec=pltpu.PrefetchScalarGridSpec(
            num_scalar_prefetch=1,
            grid=(EXP_DEV,),
            in_specs=in_specs,
            out_specs=[still(shape) for shape in sums] + [kept(cols) for cols in kept_cols],
            scratch_shapes=[
                pltpu.VMEM((block, width), BF),
                pltpu.VMEM((block, wide), BF),
                pltpu.VMEM((block, width), BF),
                pltpu.VMEM((count, length, wide), F32),
                pltpu.VMEM((count, length, width), F32),
            ],
        ),
        input_output_aliases=alias,
        compiler_params=pltpu.CompilerParams(
            dimension_semantics=("arbitrary",), vmem_limit_bytes=60 * 1024 * 1024
        ),
        cost_estimate=pl.CostEstimate(
            flops=14 * EXP_DEV * block * width * hidden,
            transcendentals=EXP_DEV * block * hidden,
            bytes_accessed=60 * 1024 * 1024,
        ),
        name="experts",
    )(*args)


def place_kernel(count, offsets_ref, *refs):
    pieces, out = refs[:count], refs[count]
    for i in range(count):
        start = pl.multiple_of(offsets_ref[i], 16)
        out[pl.ds(start, pieces[i].shape[0]), :] = pieces[i][...]


def place(pieces, offsets, total):
    count, cols = len(pieces), pieces[0].shape[1]
    return pl.pallas_call(
        functools.partial(place_kernel, count),
        out_shape=jax.ShapeDtypeStruct((total, cols), pieces[0].dtype),
        in_specs=[pl.BlockSpec(memory_space=pltpu.SMEM)]
        + [pl.BlockSpec(memory_space=pltpu.VMEM)] * count,
        out_specs=pl.BlockSpec(memory_space=pltpu.VMEM),
        cost_estimate=pl.CostEstimate(
            flops=0, transcendentals=0, bytes_accessed=4 * total * cols
        ),
        name="place",
    )(jnp.stack(offsets).astype(jnp.int32), *pieces)


def product(first_arg, second_arg):
    return jnp.dot(first_arg, second_arg, preferred_element_type=F32)


def product_high(first_arg, second_arg):
    return jnp.dot(
        first_arg, second_arg, precision=lax.Precision.HIGHEST, preferred_element_type=F32
    )


def mm(spec, first_arg, second_arg):
    return jnp.einsum(spec, first_arg, second_arg, preferred_element_type=F32)


def rotary_tables(length, head_size):
    half_dim = head_size // 2
    frequency = 10000.0 ** (-jnp.arange(half_dim, dtype=F32) * 2.0 / head_size)
    angles = jnp.arange(length, dtype=F32)[:, None] * frequency[None, :]
    return (jnp.cos(angles), jnp.sin(angles))


def rotate(tensor, cosine, sine_part):
    half_dim = tensor.shape[-1] // 2
    first_half = tensor[..., :half_dim]
    second_half = tensor[..., half_dim:]
    cos_rows = cosine[:, None, :]
    sin_rows = sine_part[:, None, :]
    return jnp.concatenate(
        [
            first_half * cos_rows - second_half * sin_rows,
            first_half * sin_rows + second_half * cos_rows,
        ],
        axis=-1,
    )


def allowed_mask(length, piece_start, piece_len):
    row_index = jnp.arange(length, dtype=jnp.int32)[:, None]
    col_index = jnp.arange(length, dtype=jnp.int32)[None, :]
    row_inside = (row_index >= piece_start) & (row_index < piece_start + piece_len)
    col_inside = (col_index >= piece_start) & (col_index < piece_start + piece_len)
    return (col_index <= row_index) | row_inside & col_inside


def silu_grad(inputs):
    sigmoid_part = jax.nn.sigmoid(inputs)
    return sigmoid_part * (1.0 + inputs * (1.0 - sigmoid_part))


def high_low(values):
    high = values.astype(BF)
    low = (values - high.astype(F32)).astype(BF)
    return high, low


def shifted(value, axis, by):
    size = lax.axis_size(axis)
    return lax.ppermute(value, axis, [(i, (i + by) % size) for i in range(size)])


def swap(value):
    return shifted(value, "c", 1)


def half(value, index, axis):
    size = value.shape[axis] // 2
    return lax.dynamic_slice_in_dim(value, index * size, size, axis)


def joined(mine, other, core, axis):
    return jnp.where(
        core == 0, jnp.concatenate([mine, other], axis), jnp.concatenate([other, mine], axis)
    )


def pick(value, index, axis):
    return lax.dynamic_index_in_dim(value, index % value.shape[axis], axis, False)


def after(values, *first):
    if not isinstance(values, (list, tuple)):
        return lax.optimization_barrier((values, *first))[0]
    return list(lax.optimization_barrier((*values, *first))[: len(values)])


def ring_gather(value, axis):
    found = [value]
    for _ in range(lax.axis_size(axis) - 1):
        found.append(shifted(found[-1], axis, 1))
    return found


def gather_dp(value):
    rows = value.shape[0]
    cut = (rows // 2 + 15) // 16 * 16
    side = lax.axis_size("x")
    pieces, offsets = [], []

    def add(piece, start, back):
        from_y = (lax.axis_index("y") - back["y"]) % side
        from_x = (lax.axis_index("x") - back["x"]) % side
        pieces.append(piece)
        offsets.append((from_y * side + from_x) * rows + start)

    add(value, 0, {"x": 0, "y": 0})
    along = {axis: ring_gather(value, axis) for axis in "xy"}
    for axis, other in ("xy", "yx"):
        for step in range(1, side):
            add(along[axis][step], 0, {axis: step, other: 0})
    near = len(pieces)
    for start, stop, order in ((0, cut, "xy"), (cut, rows, "yx")):
        for first in range(1, side):
            kept = ring_gather(along[order[0]][first][start:stop], order[1])
            for second in range(1, side):
                add(kept[second], start, {order[0]: first, order[1]: second})
    return place(pieces, offsets, rows * side * side), pieces[1:near], pieces[near:]


def ring_reduce(value, axis, at, late):
    size, index = lax.axis_size(axis), lax.axis_index(axis)
    moving = pick(value, index - 1, at)
    for step in range(2, size + 1):
        other = shifted(moving, axis, 1)
        if late:
            other = after(other, *late)
        moving = (other.astype(F32) + pick(value, index - step, at).astype(F32)).astype(BF)
    return moving


def stage_one(values, orders, first=(), late=()):
    values = after(values, *first) if first else values
    return [ring_reduce(v, o[0], "yx".index(o[0]), late) for v, o in zip(values, orders)]


def stage_two(values, orders, first=(), late=()):
    values = after(values, *first) if first else values
    return [ring_reduce(v, o[1], 0, late) for v, o in zip(values, orders)]


def crossed(value, bit):
    depth = lax.axis_size("z")
    return lax.ppermute(value, "z", [(i, i ^ bit) for i in range(depth)])


def reduce_level(value, late=((), (), (), ())):
    depth, level = lax.axis_size("z"), lax.axis_index("z")
    rows, cols = value.shape
    bits = depth.bit_length() - 1
    hold = lambda piece, first: after(piece, *first) if first else piece
    moving = value.reshape(*(2,) * bits, rows // depth, cols)
    for i in range(bits):
        mine = (level >> i) & 1
        at = bits - 1 - i
        other = hold(crossed(pick(moving, 1 - mine, at), 1 << i), late[i])
        moving = (other.astype(F32) + pick(moving, mine, at).astype(F32)).astype(BF)
    for i in reversed(range(bits)):
        mine = (level >> i) & 1
        other = hold(crossed(moving, 1 << i), late[2 * bits - 1 - i])
        at = bits - 1 - i
        moving = jnp.where(
            mine == 0, jnp.stack([moving, other], at), jnp.stack([other, moving], at)
        )
    return moving.reshape(rows, cols)


def body(
    tokens,
    query_weight,
    key_weight,
    value_weight,
    output_weight,
    attn_gain,
    ffn_gain,
    router_weight,
    shared_gate,
    shared_up,
    shared_down,
    expert_gate,
    expert_up,
    expert_down,
    expert_ids,
    piece_starts,
    out_grad,
):
    side = lax.axis_size("x")
    dp = side * side
    owners = lax.axis_size(OWN)
    depth = lax.axis_size("z")
    core = lax.axis_index("c")
    me = lax.axis_index(OWN)
    experts = EXP_DEV * owners
    length, width = tokens.shape
    rows = query_weight.shape[0]
    hidden = shared_gate.shape[1]
    wide, narrow = width // 2, hidden // 2
    head_count = wide // HEAD_DIM
    score_scale = HEAD_DIM ** (-0.5)
    piece_len = min(256, length // 2)
    capacity = 8 * length // experts
    two = lambda mine: jnp.stack([mine, swap(mine)])

    small = jnp.concatenate([router_weight, attn_gain[:, None], ffn_gain[:, None]], axis=1)
    small = jnp.pad(small, ((0, 0), (0, 128 - small.shape[1])))
    first_full, first_near, first_far = gather_dp(
        jnp.concatenate(
            [half(query_weight, core, 1), half(key_weight, core, 1), half(value_weight, core, 1), small],
            axis=1,
        )
    )
    tokens_two = two(tokens)
    starts_two = two(piece_starts[0])
    later = after([output_weight, shared_gate, shared_up, shared_down, out_grad], *first_near)
    second_shard = jnp.concatenate(
        [half(later[0], core, 1), half(later[1], core, 1), half(later[2], core, 1)]
        + [half(later[3], core, 1).reshape(rows, narrow)],
        axis=1,
    )
    second_full, second_near, _ = gather_dp(after(second_shard, *first_far))

    chosen = (expert_ids[:, :, None] == jnp.arange(experts, dtype=jnp.int32)).any(axis=1)
    chosen_low = jnp.pad(chosen.astype(BF), ((0, 0), (0, 128 - experts)))

    levels = [0, depth // 2] + [step for step in range(1, depth) if step != depth // 2]

    grads_sent = jnp.concatenate([later[4], chosen_low], axis=1)
    grads_pair = swap(grads_sent)
    grads_far = {levels[1]: shifted(grads_sent, "z", levels[1])}
    grads_next = after(grads_sent, grads_far[levels[1]])
    for step in levels[2:]:
        grads_far[step] = shifted(grads_next, "z", step)

    query_half = first_full[:, :wide]
    key_half = first_full[:, wide : 2 * wide]
    value_half = first_full[:, 2 * wide : 3 * wide]
    small_full = first_full[:, 3 * wide :]
    router_full = small_full[:, :experts]
    gain_one_f = small_full[:, experts].astype(F32)
    gain_two_f = small_full[:, experts + 1].astype(F32)
    output_cols = second_full[:, :wide]
    gate_half = second_full[:, wide : wide + narrow]
    up_half = second_full[:, wide + narrow : wide + 2 * narrow]
    down_cols = second_full[:, wide + 2 * narrow :].reshape(hidden, wide)
    met = swap(
        jnp.concatenate([half(output_cols, 1 - core, 0), half(down_cols, 1 - core, 0)], axis=0)
    )
    output_half = joined(half(output_cols, core, 0), met[:wide], core, 1)
    down_half = joined(half(down_cols, core, 0), met[wide:], core, 1)

    token_f = tokens_two.astype(F32)
    norm_one = lax.rsqrt(jnp.mean(token_f * token_f, axis=-1, keepdims=True) + 1e-06)
    attn_in = (token_f * norm_one * gain_one_f).astype(BF).reshape(2 * length, width)
    cosine, sine_part = rotary_tables(length, HEAD_DIM)
    by_head = lambda value: value.reshape(2, length, head_count, HEAD_DIM)
    flat = lambda value: value.reshape(2 * length, wide)
    query_rot = rotate(by_head(product(attn_in, query_half)), cosine, sine_part).astype(BF)
    key_rot = rotate(by_head(product(attn_in, key_half)), cosine, sine_part).astype(BF)
    values = by_head(product(attn_in, value_half).astype(BF))
    allowed = jnp.stack([allowed_mask(length, starts_two[i], piece_len) for i in range(2)])
    scores = mm("sqhd,skhd->shqk", query_rot, key_rot) * score_scale
    scores = jnp.where(allowed[:, None], scores, -1e30)
    row_max = jnp.max(scores, axis=-1, keepdims=True)
    exps = jnp.exp(scores - row_max)
    attn_probs = exps / jnp.sum(exps, axis=-1, keepdims=True)
    probs_low = attn_probs.astype(BF)
    context = flat(mm("shqk,skhd->sqhd", probs_low, after(values, *second_near)).astype(BF))
    out_partial = product(context, output_half).reshape(2, length, width)
    attn_out = out_partial[0] + swap(out_partial[1].astype(BF)).astype(F32)
    residual = token_f[0] + attn_out
    norm_two = lax.rsqrt(jnp.mean(residual * residual, axis=-1, keepdims=True) + 1e-06)
    ffn_in = (residual * norm_two * gain_two_f).astype(BF)
    router_probs = jax.nn.softmax(product(ffn_in, router_full), axis=-1)
    gates = jnp.where(chosen, router_probs, 0.0)
    gates_high, gates_low = high_low(gates)
    sent = jnp.concatenate(
        [ffn_in, gates_high, gates_low, jnp.zeros((length, 128 - 2 * experts), BF)], axis=1
    )
    sent_other = swap(sent)
    rows_far = {levels[1]: shifted(sent, "z", levels[1])}
    grads_late = after([grads_far[step] for step in levels[1:]], sent)
    grads_all = [grads_sent, grads_pair]
    for piece in grads_late:
        grads_all += [piece, swap(piece)]
    own = me * EXP_DEV + jnp.arange(EXP_DEV)
    own_hot = (own[:, None] == jnp.arange(experts)[None, :]).astype(F32)
    named = jnp.stack([piece[:, width : width + experts] for piece in grads_all]).astype(F32)
    mask = mm("ste,oe->ost", named, own_hot)
    slots = jnp.where(mask > 0, jnp.cumsum(mask, axis=2) - 1.0, -1.0).astype(jnp.int32)
    slots = slots[:, :, None, :]

    ffn_two = jnp.stack([ffn_in, sent_other[:, :width]]).reshape(2 * length, width)
    grad_two = jnp.stack([out_grad, grads_pair[:, :width]]).reshape(2 * length, width)
    shared_gate_act = product(ffn_two, gate_half)
    shared_up_act = product(ffn_two, up_half)
    shared_hidden = (jax.nn.silu(shared_gate_act) * shared_up_act).astype(BF)
    shared_out = product(shared_hidden, down_half).astype(BF).reshape(2, length, width)
    shared_hidden_grad = product(grad_two, down_half.T)
    shared_down_grad = product(shared_hidden.T, grad_two).astype(BF)
    shared_gate_act_grad = (shared_hidden_grad * shared_up_act * silu_grad(shared_gate_act)).astype(
        BF
    )
    shared_up_act_grad = (shared_hidden_grad * jax.nn.silu(shared_gate_act)).astype(BF)
    shared_gate_grad = product(ffn_two.T, shared_gate_act_grad).astype(BF)
    shared_up_grad = product(ffn_two.T, shared_up_act_grad).astype(BF)
    shared_in_grad = (
        (product(shared_gate_act_grad, gate_half.T) + product(shared_up_act_grad, up_half.T))
        .astype(BF)
        .reshape(2, length, width)
    )
    shared_both = jnp.concatenate(
        [shared_in_grad, jnp.zeros((2, length, 128), BF), shared_out], axis=2
    )
    turn = lambda grad: joined(half(grad, core, 1), swap(half(grad, 1 - core, 1)), core, 0)
    shares = lambda value: value.reshape(side, side, value.shape[0] // dp, -1)
    down_turned = turn(shared_down_grad).reshape(width, narrow)
    cut = narrow // 2
    shared_part = [
        jnp.concatenate([shared_gate_grad, down_turned[:, :cut]], axis=1),
        jnp.concatenate([shared_up_grad, down_turned[:, cut:]], axis=1),
    ]
    sent_next = after(sent, rows_far[levels[1]], shared_in_grad, *shared_part)
    for step in levels[2:]:
        rows_far[step] = shifted(sent_next, "z", step)
    rows_all = [sent, sent_other]
    for step in levels[1:]:
        rows_all += [rows_far[step], swap(rows_far[step])]
    both = ("yx", "xy")
    shared_part = [shares(part) for part in shared_part]

    place_me = me.reshape(1).astype(jnp.int32)
    block = owners // 2
    near = expert_call(
        place_me, slots[:, :block], rows_all[:block], grads_all[:block],
        expert_gate, expert_up, expert_down, owners, 0,
    )
    wider = width + 128
    shared_one = stage_one(shared_part, both, late=(near[block],))
    chips = [None] * depth
    for place_at in range(1, depth // 2):
        chips[place_at] = near[2 * place_at].astype(F32) + swap(near[2 * place_at + 1]).astype(F32)
    sent_back = [None] + [chips[i][:, :wider].astype(BF) for i in range(1, depth // 2)]
    far_slots = after(slots[:, block:], *sent_back[1:], *shared_one)
    far = expert_call(
        place_me, far_slots, rows_all[block:], grads_all[block:],
        expert_gate, expert_up, expert_down, owners, 1, near[block:],
    )
    expert_in, res_grad, routed_hidden, routed_gate_grad, routed_up_grad = far[block:]
    for place_at in range(depth // 2, depth):
        mine, other = far[2 * place_at - block], far[2 * place_at - block + 1]
        chips[place_at] = mine.astype(F32) + swap(other).astype(F32)
        sent_back.append(chips[place_at][:, :wider].astype(BF))
    back_in = [shifted(sent_back[i], "z", -levels[i]) for i in range(1, depth)]
    chips[0] = (near[0].astype(F32) + shared_both[0].astype(F32)) + swap(
        near[1] + shared_both[1]
    ).astype(F32)
    back = chips[0][:, :wider]
    for piece in back_in[: depth // 2 - 1]:
        back += after(piece, far[block]).astype(F32)
    shared_two = stage_two(shared_one, both, late=(far[block],))
    routed_gate_grad = after(routed_gate_grad, *sent_back[depth // 2 :], back)

    gate_grad = mm("erd,erf->edf", expert_in, routed_gate_grad).astype(BF)
    up_grad = mm("erd,erf->edf", expert_in, routed_up_grad).astype(BF)
    down_grad = mm("erf,erd->efd", routed_hidden, res_grad).astype(BF)
    blocks = [
        [grad[e].reshape(side, side, grad.shape[1] // dp, grad.shape[2]) for e in range(EXP_DEV)]
        for grad in (gate_grad, up_grad, down_grad)
    ]
    gate_one = stage_one(blocks[0], both, shared_two)
    for piece in after(back_in[depth // 2 - 1 :], *gate_one):
        back += piece.astype(F32)

    probs_grad = back[:, width : width + experts] + back[:, width + experts : width + 2 * experts]
    logits_grad = router_probs * (
        probs_grad - jnp.sum(router_probs * probs_grad, axis=-1, keepdims=True)
    )
    router_grad = product_high(ffn_in.astype(F32).T, logits_grad)
    router_in_grad = product_high(logits_grad, router_full.astype(F32).T)
    ffn_in_grad = back[:, :width] + router_in_grad
    ffn_gain_grad = jnp.sum(ffn_in_grad * residual * norm_two, axis=0)
    upstream_two = ffn_in_grad * gain_two_f
    residual_grad = (
        out_grad.astype(F32)
        + norm_two * upstream_two
        - residual * norm_two**3 * jnp.mean(upstream_two * residual, axis=-1, keepdims=True)
    )
    residual_low = residual_grad.astype(BF)
    attn_grad_two = two(residual_low).reshape(2 * length, width)
    output_grad = product(context.T, attn_grad_two).astype(BF)
    output_grad = turn(output_grad)
    context_grad = by_head(product(attn_grad_two, output_half.T).astype(BF))
    value_grad = flat(mm("shqk,sqhd->skhd", probs_low, context_grad).astype(BF))
    probs_grad_att = mm("sqhd,skhd->shqk", context_grad, values)
    row_delta = jnp.sum(attn_probs * probs_grad_att, axis=-1, keepdims=True)
    scores_grad = (attn_probs * (probs_grad_att - row_delta)).astype(BF)
    query_grad = mm("shqk,skhd->sqhd", scores_grad, key_rot) * score_scale
    key_grad = mm("shqk,sqhd->skhd", scores_grad, query_rot) * score_scale
    query_pre_grad = flat(rotate(query_grad, cosine, -sine_part).astype(BF))
    key_pre_grad = flat(rotate(key_grad, cosine, -sine_part).astype(BF))
    query_wgrad = product(attn_in.T, query_pre_grad).astype(BF)
    key_wgrad = product(attn_in.T, key_pre_grad).astype(BF)
    value_wgrad = product(attn_in.T, value_grad).astype(BF)
    in_partial = (
        product(query_pre_grad, query_half.T)
        + product(key_pre_grad, key_half.T)
        + product(value_grad, value_half.T)
    ).reshape(2, length, width)
    attn_in_grad = in_partial[0] + swap(in_partial[1].astype(BF)).astype(F32)
    token_mine, norm_mine = token_f[0], norm_one[0]
    attn_gain_grad = jnp.sum(attn_in_grad * token_mine * norm_mine, axis=0)
    upstream_one = attn_in_grad * gain_one_f
    tokens_grad = (
        residual_grad
        + norm_mine * upstream_one
        - token_mine * norm_mine**3 * jnp.mean(upstream_one * token_mine, axis=-1, keepdims=True)
    )
    small_grads = jnp.concatenate(
        [router_grad, attn_gain_grad[:, None], ffn_gain_grad[:, None]], axis=1
    ).astype(BF)
    small_grads = jnp.pad(small_grads, ((0, 0), (0, 128 - small_grads.shape[1])))
    marks = ((value_grad,), (scores_grad,), (query_wgrad,), ())
    up_one = stage_one(blocks[1], both, gate_one, marks[0])
    gate_two = stage_two(gate_one, both, up_one, marks[1])
    early = [shares(output_grad), shares(value_wgrad)]
    early_one = stage_one(early, both, gate_two, marks[2])
    early_two = stage_two(early_one, both)
    late = [shares(query_wgrad), shares(jnp.concatenate([key_wgrad, small_grads], axis=1))]
    late_one = stage_one(late, both, early_one)
    late_two = stage_two(late_one, both, early_two)
    up_two = stage_two(up_one, both, late_one)
    down_two = stage_two(stage_one(blocks[2], both, late_two), both)
    expert_shares = [jnp.stack(pair).astype(F32) for pair in (gate_two, up_two, down_two)]
    shared_share = reduce_level(after(jnp.concatenate(shared_two, axis=1), back), marks)
    early_share = reduce_level(jnp.concatenate(early_two, axis=1))
    late_share = reduce_level(jnp.concatenate(late_two, axis=1))

    moe_out = chips[0][:, wider:]
    piece = back
    for i in range(1, depth):
        moving = after(chips[i][:, wider:].astype(BF), piece)
        piece = after(shifted(moving, "z", -levels[i]), *marks[min(i - 1, 2)])
        moe_out += piece.astype(F32)

    early_other, late_other, shared_other = swap(early_share), swap(late_share), swap(shared_share)
    column = lambda mine, other, start, size: joined(
        mine[:, start : start + size], other[:, start : start + size], core, 1
    ).astype(F32)
    small_sum = late_share[:, 2 * wide :].astype(F32) + late_other[:, 2 * wide :].astype(F32)
    down_cols = lambda share: jnp.concatenate(
        [share[:, narrow : narrow + cut], share[:, 2 * narrow + cut :]], axis=1
    ).reshape(-1, wide)
    down_rows = joined(down_cols(shared_share), down_cols(shared_other), core, 1).astype(F32)

    stream_out = residual + moe_out
    stat_rms = jnp.stack(
        [
            jnp.sqrt(jnp.mean(attn_out * attn_out)),
            jnp.sqrt(jnp.mean(moe_out * moe_out)),
            jnp.sqrt(jnp.mean(stream_out * stream_out)),
        ]
    )[None, :]
    return (
        stream_out.astype(BF),
        tokens_grad.astype(BF),
        column(late_share, late_other, 0, wide),
        column(late_share, late_other, wide, wide),
        column(early_share, early_other, wide, wide),
        column(early_share, early_other, 0, wide),
        small_sum[:, experts],
        small_sum[:, experts + 1],
        small_sum[:, :experts],
        column(shared_share, shared_other, 0, narrow),
        column(shared_share, shared_other, narrow + cut, narrow),
        down_rows,
        *expert_shares,
        stat_rms,
    )


def solution(mesh):
    side = math.isqrt(mesh.shape["dp"])
    fine = Mesh(
        mesh.devices.reshape(side, side, mesh.shape["expert"] // 2, 2), ("y", "x", "z", "c")
    )
    whole = P(("y", "x", "z", "c"), None)
    dense = P(DP, None)
    routed = P(OWN, None, None)
    in_specs = (
        whole, dense, dense, dense, dense, P(DP), P(DP), dense, dense, dense, dense,
        routed, routed, routed, whole, P(("y", "x", "z", "c")), whole,
    )
    shares = P(OWN, DP, None)
    out_specs = (
        whole, whole, dense, dense, dense, dense, P(DP), P(DP), dense, dense, dense, dense,
        shares, shares, shares, whole,
    )
    return jax.shard_map(body, mesh=fine, in_specs=in_specs, out_specs=out_specs, check_vma=False)
```

```python
import functools
import math

import jax
import jax.numpy as jnp
from jax import lax
from jax.experimental import pallas as pl
from jax.experimental.pallas import tpu as pltpu
from jax.sharding import Mesh
from jax.sharding import PartitionSpec as P

HEAD_DIM = 128
TOP = 7
EXP_DEV = 2
BF = jnp.bfloat16
F32 = jnp.float32
DP = ("y", "x")
OWN = ("z", "c")
NT = (((1,), (1,)), ((), ()))
TN = (((0,), (0,)), ((), ()))


def dot(first, second, dims=(((1,), (0,)), ((), ()))):
    return lax.dot_general(first, second, dims, preferred_element_type=F32)


def expert_kernel(count, width, capacity, experts, chunk, me_ref, slots_ref, *refs):
    rows_refs = refs[:count]
    grads_refs = refs[count : 2 * count]
    gate_ref, up_ref, down_ref = refs[2 * count : 2 * count + 3]
    sums = refs[-10 - count : -10]
    xin, rgrad, hid, ggrad, ugrad = refs[-10:-5]
    ograd, in_ext, res_low, in_acc, out_acc = refs[-5:]
    step = pl.program_id(0)
    expert = me_ref[0] * EXP_DEV + step
    lane = lax.broadcasted_iota(jnp.int32, (capacity, 128), 1)
    mine = (lane == expert) | (lane == expert + experts)

    def spread(piece):
        want = slots_ref[step, piece]
        place = lax.broadcasted_iota(jnp.int32, (capacity, want.shape[-1]), 0)
        return (want == place).astype(F32)

    for piece in range(count):
        hot = spread(piece).astype(BF)
        area = pl.ds(piece * capacity, capacity)
        rows = dot(hot, rows_refs[piece][...])
        xin[0, area, :] = rows[:, :width].astype(BF)
        gates = jnp.sum(jnp.where(mine, rows[:, width:], 0.0), axis=1, keepdims=True)
        grads = dot(hot, grads_refs[piece][:, :width])
        ograd[area, :] = grads.astype(BF)
        rgrad[0, area, :] = (grads * gates).astype(BF)

    def part(index, carry):
        area = pl.ds(pl.multiple_of(index * chunk, chunk), chunk)
        rows = xin[0, area, :]
        res_grad = rgrad[0, area, :]
        gate = dot(rows, gate_ref[0])
        up = dot(rows, up_ref[0])
        hidden_grad = dot(res_grad, down_ref[0], NT)
        sig = jax.nn.sigmoid(gate)
        silu = gate * sig
        hidden = (silu * up).astype(BF)
        hid[0, area, :] = hidden
        gate_grad = (hidden_grad * up * (sig * (1.0 + gate * (1.0 - sig)))).astype(BF)
        up_grad = (hidden_grad * silu).astype(BF)
        ggrad[0, area, :] = gate_grad
        ugrad[0, area, :] = up_grad
        in_ext[area, pl.ds(0, width)] = (
            dot(gate_grad, gate_ref[0], NT) + dot(up_grad, up_ref[0], NT)
        ).astype(BF)
        res = dot(hidden, down_ref[0]).astype(BF)
        res_low[area, :] = res
        slot_gate = jnp.sum(res.astype(F32) * ograd[area, :].astype(F32), axis=1, keepdims=True)
        high = slot_gate.astype(BF).astype(F32)
        lanes = lax.broadcasted_iota(jnp.int32, (chunk, 128), 1)
        in_ext[area, pl.ds(width, 128)] = jnp.where(
            lanes == expert, high, jnp.where(lanes == expert + experts, slot_gate - high, 0.0)
        ).astype(BF)
        return carry

    lax.fori_loop(0, count * capacity // chunk, part, 0)

    for piece in range(count):
        hot = spread(piece)
        area = pl.ds(piece * capacity, capacity)
        low = hot.astype(BF)
        gates = jnp.sum(
            jnp.where(mine, dot(low, rows_refs[piece][:, width:]), 0.0), axis=1, keepdims=True
        )
        back = dot(low, in_ext[area, :], TN)
        result = dot((hot * gates).astype(BF), res_low[area, :], TN)

        @pl.when(step == 0)
        def _():
            in_acc[piece] = back
            out_acc[piece] = result

        @pl.when(step == EXP_DEV - 1)
        def _():
            wide = back.shape[1]
            sums[piece][:, :wide] = (in_acc[piece] + back).astype(BF)
            sums[piece][:, wide:] = (out_acc[piece] + result).astype(BF)


def expert_call(me, slots, rows, grads, gate, up, down, owners, first, carried=None):
    count = len(rows)
    length, wide = rows[0].shape
    width, hidden = gate.shape[1:]
    experts = EXP_DEV * owners
    capacity = 8 * length // experts
    block = count * capacity
    total = owners * capacity
    still = lambda shape: pl.BlockSpec(
        shape, lambda e, m: (0,) * len(shape), pipeline_mode=pl.Buffered(1)
    )
    weight = lambda a, b: pl.BlockSpec((1, a, b), lambda e, m: (e, 0, 0))
    kept = lambda cols: pl.BlockSpec((1, block, cols), lambda e, m: (e, first, 0))
    kept_cols = (width, width, hidden, hidden, hidden)
    in_specs = (
        [still((EXP_DEV, count, 1, length))]
        + [still((length, wide))] * (2 * count)
        + [weight(width, hidden), weight(width, hidden), weight(hidden, width)]
    )
    args = [me, slots, *rows, *grads, gate, up, down]
    alias = {}
    if carried is not None:
        for i, value in enumerate(carried):
            alias[len(args)] = count + i
            args.append(value)
            in_specs.append(pl.BlockSpec(memory_space=pl.ANY))
    sums = [(length, wide + width)] * count
    return pl.pallas_call(
        functools.partial(expert_kernel, count, width, capacity, experts, min(512, block)),
        out_shape=[jax.ShapeDtypeStruct(shape, BF) for shape in sums]
        + [jax.ShapeDtypeStruct((EXP_DEV, total, cols), BF) for cols in kept_cols],
        grid_spec=pltpu.PrefetchScalarGridSpec(
            num_scalar_prefetch=1,
            grid=(EXP_DEV,),
            in_specs=in_specs,
            out_specs=[still(shape) for shape in sums] + [kept(cols) for cols in kept_cols],
            scratch_shapes=[
                pltpu.VMEM((block, width), BF),
                pltpu.VMEM((block, wide), BF),
                pltpu.VMEM((block, width), BF),
                pltpu.VMEM((count, length, wide), F32),
                pltpu.VMEM((count, length, width), F32),
            ],
        ),
        input_output_aliases=alias,
        compiler_params=pltpu.CompilerParams(
            dimension_semantics=("arbitrary",), vmem_limit_bytes=60 * 1024 * 1024
        ),
        cost_estimate=pl.CostEstimate(
            flops=14 * EXP_DEV * block * width * hidden,
            transcendentals=EXP_DEV * block * hidden,
            bytes_accessed=60 * 1024 * 1024,
        ),
        name="experts",
    )(*args)


def place_kernel(count, offsets_ref, *refs):
    pieces, out = refs[:count], refs[count]
    for i in range(count):
        start = pl.multiple_of(offsets_ref[i], 16)
        out[pl.ds(start, pieces[i].shape[0]), :] = pieces[i][...]


def place(pieces, offsets, total):
    count, cols = len(pieces), pieces[0].shape[1]
    return pl.pallas_call(
        functools.partial(place_kernel, count),
        out_shape=jax.ShapeDtypeStruct((total, cols), pieces[0].dtype),
        in_specs=[pl.BlockSpec(memory_space=pltpu.SMEM)]
        + [pl.BlockSpec(memory_space=pltpu.VMEM)] * count,
        out_specs=pl.BlockSpec(memory_space=pltpu.VMEM),
        cost_estimate=pl.CostEstimate(
            flops=0, transcendentals=0, bytes_accessed=4 * total * cols
        ),
        name="place",
    )(jnp.stack(offsets).astype(jnp.int32), *pieces)


def product(first_arg, second_arg):
    return jnp.dot(first_arg, second_arg, preferred_element_type=F32)


def product_high(first_arg, second_arg):
    return jnp.dot(
        first_arg, second_arg, precision=lax.Precision.HIGHEST, preferred_element_type=F32
    )


def mm(spec, first_arg, second_arg):
    return jnp.einsum(spec, first_arg, second_arg, preferred_element_type=F32)


def rotary_tables(length, head_size):
    half_dim = head_size // 2
    frequency = 10000.0 ** (-jnp.arange(half_dim, dtype=F32) * 2.0 / head_size)
    angles = jnp.arange(length, dtype=F32)[:, None] * frequency[None, :]
    return (jnp.cos(angles), jnp.sin(angles))


def rotate(tensor, cosine, sine_part):
    half_dim = tensor.shape[-1] // 2
    first_half = tensor[..., :half_dim]
    second_half = tensor[..., half_dim:]
    cos_rows = cosine[:, None, :]
    sin_rows = sine_part[:, None, :]
    return jnp.concatenate(
        [
            first_half * cos_rows - second_half * sin_rows,
            first_half * sin_rows + second_half * cos_rows,
        ],
        axis=-1,
    )


def allowed_mask(length, piece_start, piece_len):
    row_index = jnp.arange(length, dtype=jnp.int32)[:, None]
    col_index = jnp.arange(length, dtype=jnp.int32)[None, :]
    row_inside = (row_index >= piece_start) & (row_index < piece_start + piece_len)
    col_inside = (col_index >= piece_start) & (col_index < piece_start + piece_len)
    return (col_index <= row_index) | row_inside & col_inside


def silu_grad(inputs):
    sigmoid_part = jax.nn.sigmoid(inputs)
    return sigmoid_part * (1.0 + inputs * (1.0 - sigmoid_part))


def high_low(values):
    high = values.astype(BF)
    low = (values - high.astype(F32)).astype(BF)
    return high, low


def shifted(value, axis, by):
    size = lax.axis_size(axis)
    return lax.ppermute(value, axis, [(i, (i + by) % size) for i in range(size)])


def swap(value):
    return shifted(value, "c", 1)


def half(value, index, axis):
    size = value.shape[axis] // 2
    return lax.dynamic_slice_in_dim(value, index * size, size, axis)


def joined(mine, other, core, axis):
    return jnp.where(
        core == 0, jnp.concatenate([mine, other], axis), jnp.concatenate([other, mine], axis)
    )


def pick(value, index, axis):
    return lax.dynamic_index_in_dim(value, index % value.shape[axis], axis, False)


def after(values, *first):
    if not isinstance(values, (list, tuple)):
        return lax.optimization_barrier((values, *first))[0]
    return list(lax.optimization_barrier((*values, *first))[: len(values)])


def ring_gather(value, axis):
    found = [value]
    for _ in range(lax.axis_size(axis) - 1):
        found.append(shifted(found[-1], axis, 1))
    return found


def gather_dp(value):
    rows = value.shape[0]
    cut = (rows // 2 + 15) // 16 * 16
    side = lax.axis_size("x")
    pieces, offsets = [], []

    def add(piece, start, back):
        from_y = (lax.axis_index("y") - back["y"]) % side
        from_x = (lax.axis_index("x") - back["x"]) % side
        pieces.append(piece)
        offsets.append((from_y * side + from_x) * rows + start)

    add(value, 0, {"x": 0, "y": 0})
    along = {axis: ring_gather(value, axis) for axis in "xy"}
    for axis, other in ("xy", "yx"):
        for step in range(1, side):
            add(along[axis][step], 0, {axis: step, other: 0})
    near = len(pieces)
    for start, stop, order in ((0, cut, "xy"), (cut, rows, "yx")):
        for first in range(1, side):
            kept = ring_gather(along[order[0]][first][start:stop], order[1])
            for second in range(1, side):
                add(kept[second], start, {order[0]: first, order[1]: second})
    return place(pieces, offsets, rows * side * side), pieces[1:near], pieces[near:]


def ring_reduce(value, axis, at, late):
    size, index = lax.axis_size(axis), lax.axis_index(axis)
    moving = pick(value, index - 1, at)
    for step in range(2, size + 1):
        other = shifted(moving, axis, 1)
        if late:
            other = after(other, *late)
        moving = (other.astype(F32) + pick(value, index - step, at).astype(F32)).astype(BF)
    return moving


def stage_one(values, orders, first=(), late=()):
    values = after(values, *first) if first else values
    return [ring_reduce(v, o[0], "yx".index(o[0]), late) for v, o in zip(values, orders)]


def stage_two(values, orders, first=(), late=()):
    values = after(values, *first) if first else values
    return [ring_reduce(v, o[1], 0, late) for v, o in zip(values, orders)]


def crossed(value, bit):
    depth = lax.axis_size("z")
    return lax.ppermute(value, "z", [(i, i ^ bit) for i in range(depth)])


def reduce_level(value, late=((), (), (), ())):
    depth, level = lax.axis_size("z"), lax.axis_index("z")
    rows, cols = value.shape
    bits = depth.bit_length() - 1
    hold = lambda piece, first: after(piece, *first) if first else piece
    moving = value.reshape(*(2,) * bits, rows // depth, cols)
    for i in range(bits):
        mine = (level >> i) & 1
        at = bits - 1 - i
        other = hold(crossed(pick(moving, 1 - mine, at), 1 << i), late[i])
        moving = (other.astype(F32) + pick(moving, mine, at).astype(F32)).astype(BF)
    for i in reversed(range(bits)):
        mine = (level >> i) & 1
        other = hold(crossed(moving, 1 << i), late[2 * bits - 1 - i])
        at = bits - 1 - i
        moving = jnp.where(
            mine == 0, jnp.stack([moving, other], at), jnp.stack([other, moving], at)
        )
    return moving.reshape(rows, cols)


def body(
    tokens,
    query_weight,
    key_weight,
    value_weight,
    output_weight,
    attn_gain,
    ffn_gain,
    router_weight,
    shared_gate,
    shared_up,
    shared_down,
    expert_gate,
    expert_up,
    expert_down,
    expert_ids,
    piece_starts,
    out_grad,
):
    side = lax.axis_size("x")
    dp = side * side
    owners = lax.axis_size(OWN)
    depth = lax.axis_size("z")
    core = lax.axis_index("c")
    me = lax.axis_index(OWN)
    experts = EXP_DEV * owners
    length, width = tokens.shape
    rows = query_weight.shape[0]
    hidden = shared_gate.shape[1]
    wide, narrow = width // 2, hidden // 2
    head_count = wide // HEAD_DIM
    score_scale = HEAD_DIM ** (-0.5)
    piece_len = min(256, length // 2)
    capacity = 8 * length // experts
    two = lambda mine: jnp.stack([mine, swap(mine)])

    small = jnp.concatenate([router_weight, attn_gain[:, None], ffn_gain[:, None]], axis=1)
    small = jnp.pad(small, ((0, 0), (0, 128 - small.shape[1])))
    first_full, first_near, first_far = gather_dp(
        jnp.concatenate(
            [half(query_weight, core, 1), half(key_weight, core, 1), half(value_weight, core, 1), small],
            axis=1,
        )
    )
    tokens_two = two(tokens)
    starts_two = two(piece_starts[0])
    later = after([output_weight, shared_gate, shared_up, shared_down, out_grad], *first_near)
    second_shard = jnp.concatenate(
        [half(later[0], core, 1), half(later[1], core, 1), half(later[2], core, 1)]
        + [half(later[3], core, 1).reshape(rows, narrow)],
        axis=1,
    )
    second_full, second_near, _ = gather_dp(after(second_shard, *first_far))

    chosen = (expert_ids[:, :, None] == jnp.arange(experts, dtype=jnp.int32)).any(axis=1)
    chosen_low = jnp.pad(chosen.astype(BF), ((0, 0), (0, 128 - experts)))

    levels = [0, depth // 2] + [step for step in range(1, depth) if step != depth // 2]

    grads_sent = jnp.concatenate([later[4], chosen_low], axis=1)
    grads_pair = swap(grads_sent)
    grads_far = {levels[1]: shifted(grads_sent, "z", levels[1])}
    turn_at = after(grads_sent, grads_far[levels[1]])
    for step in levels[2:]:
        grads_far[step] = shifted(turn_at, "z", step)
        turn_at = after(turn_at, grads_far[step])

    query_half = first_full[:, :wide]
    key_half = first_full[:, wide : 2 * wide]
    value_half = first_full[:, 2 * wide : 3 * wide]
    small_full = first_full[:, 3 * wide :]
    router_full = small_full[:, :experts]
    gain_one_f = small_full[:, experts].astype(F32)
    gain_two_f = small_full[:, experts + 1].astype(F32)
    output_cols = second_full[:, :wide]
    gate_half = second_full[:, wide : wide + narrow]
    up_half = second_full[:, wide + narrow : wide + 2 * narrow]
    down_cols = second_full[:, wide + 2 * narrow :].reshape(hidden, wide)
    met = swap(
        jnp.concatenate([half(output_cols, 1 - core, 0), half(down_cols, 1 - core, 0)], axis=0)
    )
    output_half = joined(half(output_cols, core, 0), met[:wide], core, 1)
    down_half = joined(half(down_cols, core, 0), met[wide:], core, 1)

    token_f = tokens_two.astype(F32)
    norm_one = lax.rsqrt(jnp.mean(token_f * token_f, axis=-1, keepdims=True) + 1e-06)
    attn_in = (token_f * norm_one * gain_one_f).astype(BF).reshape(2 * length, width)
    cosine, sine_part = rotary_tables(length, HEAD_DIM)
    by_head = lambda value: value.reshape(2, length, head_count, HEAD_DIM)
    flat = lambda value: value.reshape(2 * length, wide)
    query_rot = rotate(by_head(product(attn_in, query_half)), cosine, sine_part).astype(BF)
    key_rot = rotate(by_head(product(attn_in, key_half)), cosine, sine_part).astype(BF)
    values = by_head(product(attn_in, value_half).astype(BF))
    allowed = jnp.stack([allowed_mask(length, starts_two[i], piece_len) for i in range(2)])
    key_met = after(key_rot, grads_far[levels[1]])
    scores = mm("sqhd,skhd->shqk", query_rot, key_met) * score_scale
    scores = jnp.where(allowed[:, None], scores, -1e30)
    row_max = jnp.max(scores, axis=-1, keepdims=True)
    exps = jnp.exp(scores - row_max)
    attn_probs = exps / jnp.sum(exps, axis=-1, keepdims=True)
    probs_low = attn_probs.astype(BF)
    context = flat(mm("shqk,skhd->sqhd", probs_low, after(values, grads_far[levels[2]], *second_near)).astype(BF))
    out_partial = product(context, output_half).reshape(2, length, width)
    attn_out = out_partial[0] + swap(out_partial[1].astype(BF)).astype(F32)
    residual = token_f[0] + attn_out
    norm_two = lax.rsqrt(jnp.mean(residual * residual, axis=-1, keepdims=True) + 1e-06)
    ffn_in = (residual * norm_two * gain_two_f).astype(BF)
    router_probs = jax.nn.softmax(product(ffn_in, router_full), axis=-1)
    gates = jnp.where(chosen, router_probs, 0.0)
    gates_high, gates_low = high_low(gates)
    sent = jnp.concatenate(
        [ffn_in, gates_high, gates_low, jnp.zeros((length, 128 - 2 * experts), BF)], axis=1
    )
    sent_other = swap(sent)
    rows_far = {levels[1]: shifted(sent, "z", levels[1])}
    grads_late = after([grads_far[step] for step in levels[1:]], sent)
    grads_all = [grads_sent, grads_pair]
    for piece in grads_late:
        grads_all += [piece, swap(piece)]
    own = me * EXP_DEV + jnp.arange(EXP_DEV)
    own_hot = (own[:, None] == jnp.arange(experts)[None, :]).astype(F32)
    named = jnp.stack([piece[:, width : width + experts] for piece in grads_all]).astype(F32)
    mask = mm("ste,oe->ost", named, own_hot)
    slots = jnp.where(mask > 0, jnp.cumsum(mask, axis=2) - 1.0, -1.0).astype(jnp.int32)
    slots = slots[:, :, None, :]

    ffn_two = jnp.stack([ffn_in, sent_other[:, :width]]).reshape(2 * length, width)
    grad_two = jnp.stack([out_grad, grads_pair[:, :width]]).reshape(2 * length, width)
    shared_gate_act = product(ffn_two, gate_half)
    shared_up_act = product(ffn_two, up_half)
    shared_hidden = (jax.nn.silu(shared_gate_act) * shared_up_act).astype(BF)
    shared_out = product(shared_hidden, down_half).astype(BF).reshape(2, length, width)
    shared_hidden_grad = product(grad_two, down_half.T)
    shared_gate_act_grad = (shared_hidden_grad * shared_up_act * silu_grad(shared_gate_act)).astype(
        BF
    )
    shared_up_act_grad = (shared_hidden_grad * jax.nn.silu(shared_gate_act)).astype(BF)
    shared_in_grad = (
        (product(shared_gate_act_grad, gate_half.T) + product(shared_up_act_grad, up_half.T))
        .astype(BF)
        .reshape(2, length, width)
    )
    shared_both = jnp.concatenate(
        [shared_in_grad, jnp.zeros((2, length, 128), BF), shared_out], axis=2
    )
    turn = lambda grad: joined(half(grad, core, 1), swap(half(grad, 1 - core, 1)), core, 0)
    shares = lambda value: value.reshape(side, side, value.shape[0] // dp, -1)
    sent_next = after(sent, rows_far[levels[1]], shared_in_grad, shared_out)
    for step in levels[2:]:
        rows_far[step] = shifted(sent_next, "z", step)
    rows_all = [sent, sent_other]
    for step in levels[1:]:
        rows_all += [rows_far[step], swap(rows_far[step])]
    both = ("yx", "xy")

    place_me = me.reshape(1).astype(jnp.int32)
    block = owners // 2
    near = expert_call(
        place_me, slots[:, :block], rows_all[:block], grads_all[:block],
        expert_gate, expert_up, expert_down, owners, 0,
    )
    wider = width + 128
    gate_low, up_low, hidden_low, grad_low = after(
        [shared_gate_act_grad, shared_up_act_grad, shared_hidden, grad_two], near[block]
    )
    shared_down_grad = product(hidden_low.T, grad_low).astype(BF)
    shared_gate_grad = product(ffn_two.T, gate_low).astype(BF)
    shared_up_grad = product(ffn_two.T, up_low).astype(BF)
    down_shares = turn(shared_down_grad).reshape(side, side, rows, narrow)
    cut = (rows // 2 + 15) // 16 * 16
    shared_part = [
        jnp.concatenate([shares(shared_gate_grad), down_shares[:, :, :cut]], axis=2),
        jnp.concatenate([shares(shared_up_grad), down_shares[:, :, cut:]], axis=2),
    ]
    chips = [None] * depth
    for place_at in range(1, depth // 2):
        chips[place_at] = near[2 * place_at].astype(F32) + swap(near[2 * place_at + 1]).astype(F32)
    sent_back = [None] + [chips[i][:, :wider].astype(BF) for i in range(1, depth // 2)]
    far_slots = after(slots[:, block:], *sent_back[1:], *shared_part)
    far = expert_call(
        place_me, far_slots, rows_all[block:], grads_all[block:],
        expert_gate, expert_up, expert_down, owners, 1, near[block:],
    )
    expert_in, res_grad, routed_hidden, routed_gate_grad, routed_up_grad = far[block:]
    gate_grad = mm("erd,erf->edf", expert_in, routed_gate_grad).astype(BF)
    met = after([swap(far[i]) for i in range(1, block, 2)], gate_grad)
    for i, other in enumerate(met):
        chips[depth // 2 + i] = far[2 * i].astype(F32) + other.astype(F32)
        sent_back.append(chips[depth // 2 + i][:, :wider].astype(BF))
    back_in = [shifted(sent_back[i], "z", -levels[i]) for i in range(1, depth)]
    shared_one = stage_one(shared_part, both, late=(gate_grad,))
    chips[0] = (near[0].astype(F32) + shared_both[0].astype(F32)) + swap(
        near[1] + shared_both[1]
    ).astype(F32)
    back = chips[0][:, :wider]
    for piece in back_in[: depth // 2 - 1]:
        back += after(piece, gate_grad).astype(F32)

    routed_up_grad = after(routed_up_grad, *sent_back[depth // 2 :], *shared_one, back)
    up_grad = mm("erd,erf->edf", expert_in, routed_up_grad).astype(BF)
    shared_two = stage_two(shared_one, both, late=(up_grad,))
    down_grad = mm("erf,erd->efd", routed_hidden, after(res_grad, *shared_two)).astype(BF)
    blocks = [
        [grad[e].reshape(side, side, grad.shape[1] // dp, grad.shape[2]) for e in range(EXP_DEV)]
        for grad in (gate_grad, up_grad, down_grad)
    ]
    gate_one = stage_one(blocks[0], both, shared_two)
    for piece in after(back_in[depth // 2 - 1 :], down_grad, *gate_one):
        back += piece.astype(F32)

    probs_grad = back[:, width : width + experts] + back[:, width + experts : width + 2 * experts]
    logits_grad = router_probs * (
        probs_grad - jnp.sum(router_probs * probs_grad, axis=-1, keepdims=True)
    )
    router_in_grad = product_high(logits_grad, router_full.astype(F32).T)
    ffn_in_grad = back[:, :width] + router_in_grad
    ffn_gain_terms = ffn_in_grad * residual * norm_two
    upstream_two = ffn_in_grad * gain_two_f
    residual_grad = (
        out_grad.astype(F32)
        + norm_two * upstream_two
        - residual * norm_two**3 * jnp.mean(upstream_two * residual, axis=-1, keepdims=True)
    )
    residual_low = residual_grad.astype(BF)
    attn_grad_two = two(residual_low).reshape(2 * length, width)
    output_grad = product(context.T, attn_grad_two).astype(BF)
    output_grad = turn(output_grad)
    context_grad = by_head(product(attn_grad_two, output_half.T).astype(BF))
    value_grad = flat(mm("shqk,sqhd->skhd", probs_low, context_grad).astype(BF))
    up_one = stage_one(blocks[1], both, gate_one, (value_grad,))
    context_late = after(context_grad, *up_one)
    value_wgrad = product(attn_in.T, value_grad).astype(BF)
    probs_grad_att = mm("sqhd,skhd->shqk", context_late, values)
    row_delta = jnp.sum(attn_probs * probs_grad_att, axis=-1, keepdims=True)
    scores_grad = (attn_probs * (probs_grad_att - row_delta)).astype(BF)
    early = [shares(output_grad), shares(value_wgrad)]
    scores_grad = after(scores_grad, *early)
    query_grad = mm("shqk,skhd->sqhd", scores_grad, key_rot) * score_scale
    key_grad = mm("shqk,sqhd->skhd", scores_grad, query_rot) * score_scale
    query_pre_grad = flat(rotate(query_grad, cosine, -sine_part).astype(BF))
    key_pre_grad = flat(rotate(key_grad, cosine, -sine_part).astype(BF))
    query_wgrad = product(attn_in.T, query_pre_grad).astype(BF)
    key_wgrad = product(attn_in.T, key_pre_grad).astype(BF)
    in_partial = (
        product(query_pre_grad, query_half.T)
        + product(key_pre_grad, key_half.T)
        + product(value_grad, value_half.T)
    ).reshape(2, length, width)
    attn_in_grad = in_partial[0] + swap(in_partial[1].astype(BF)).astype(F32)
    token_mine, norm_mine = token_f[0], norm_one[0]
    attn_gain_terms = attn_in_grad * token_mine * norm_mine
    upstream_one = attn_in_grad * gain_one_f
    tokens_grad = (
        residual_grad
        + norm_mine * upstream_one
        - token_mine * norm_mine**3 * jnp.mean(upstream_one * token_mine, axis=-1, keepdims=True)
    )
    lanes = jnp.arange(128)
    unit = lambda lane: jnp.broadcast_to((lanes == lane).astype(F32), (length, 128))
    small_grads = (
        product_high(ffn_in.astype(F32).T, jnp.pad(logits_grad, ((0, 0), (0, 128 - experts))))
        + product_high(ffn_gain_terms.T, unit(experts + 1))
        + product_high(attn_gain_terms.T, unit(experts))
    ).astype(BF)

    done_wgrads = (query_wgrad, key_wgrad)
    gate_two = stage_two(gate_one, both, up_one, done_wgrads)
    early_one = stage_one(early, both, up_one, done_wgrads)
    early_two = stage_two(early_one, both)
    late = [shares(query_wgrad), shares(jnp.concatenate([key_wgrad, small_grads], axis=1))]
    late_one = stage_one(late, both, early_one)
    late_two = stage_two(late_one, both, early_two)
    up_two = stage_two(up_one, both, late_one)
    down_two = stage_two(stage_one(blocks[2], both, late_two), both)
    expert_shares = [jnp.stack(pair).astype(F32) for pair in (gate_two, up_two, down_two)]
    shared_share = reduce_level(
        after(jnp.concatenate(shared_two, axis=0), back),
        ((value_grad,), done_wgrads, early_two, late_one),
    )
    early_share = reduce_level(jnp.concatenate(early_two, axis=1))
    late_share = reduce_level(jnp.concatenate(late_two, axis=1))

    moe_out = chips[0][:, wider:]
    piece = back
    for i in range(1, depth):
        moving = after(chips[i][:, wider:].astype(BF), piece, *(early_two if i > 1 else ()))
        piece = after(shifted(moving, "z", -levels[i]), *((value_grad,), late_one, late_two)[min(i - 1, 2)])
        moe_out += piece.astype(F32)

    early_other, late_other, shared_other = swap(early_share), swap(late_share), swap(shared_share)
    column = lambda mine, other, start, size: joined(
        mine[:, start : start + size], other[:, start : start + size], core, 1
    ).astype(F32)
    small_sum = late_share[:, 2 * wide :].astype(F32) + late_other[:, 2 * wide :].astype(F32)
    first_rows = rows + cut
    down_part = lambda share: jnp.concatenate(
        [share[rows:first_rows], share[first_rows + rows :]], axis=0
    ).reshape(-1, wide)
    down_rows = joined(down_part(shared_share), down_part(shared_other), core, 1).astype(F32)
    unit_cols = lambda start: joined(
        shared_share[start : start + rows], shared_other[start : start + rows], core, 1
    ).astype(F32)

    stream_out = residual + moe_out
    stat_rms = jnp.stack(
        [
            jnp.sqrt(jnp.mean(attn_out * attn_out)),
            jnp.sqrt(jnp.mean(moe_out * moe_out)),
            jnp.sqrt(jnp.mean(stream_out * stream_out)),
        ]
    )[None, :]
    return (
        stream_out.astype(BF),
        tokens_grad.astype(BF),
        column(late_share, late_other, 0, wide),
        column(late_share, late_other, wide, wide),
        column(early_share, early_other, wide, wide),
        column(early_share, early_other, 0, wide),
        small_sum[:, experts],
        small_sum[:, experts + 1],
        small_sum[:, :experts],
        unit_cols(0),
        unit_cols(first_rows),
        down_rows,
        *expert_shares,
        stat_rms,
    )


def solution(mesh):
    side = math.isqrt(mesh.shape["dp"])
    fine = Mesh(
        mesh.devices.reshape(side, side, mesh.shape["expert"] // 2, 2), ("y", "x", "z", "c")
    )
    whole = P(("y", "x", "z", "c"), None)
    dense = P(DP, None)
    routed = P(OWN, None, None)
    in_specs = (
        whole, dense, dense, dense, dense, P(DP), P(DP), dense, dense, dense, dense,
        routed, routed, routed, whole, P(("y", "x", "z", "c")), whole,
    )
    shares = P(OWN, DP, None)
    out_specs = (
        whole, whole, dense, dense, dense, dense, P(DP), P(DP), dense, dense, dense, dense,
        shares, shares, shares, whole,
    )
    return jax.shard_map(body, mesh=fine, in_specs=in_specs, out_specs=out_specs, check_vma=False)
```

```python
import functools
import math

import jax
import jax.numpy as jnp
from jax import lax
from jax.experimental import pallas as pl
from jax.experimental.pallas import tpu as pltpu
from jax.sharding import Mesh
from jax.sharding import PartitionSpec as P

HEAD_DIM = 128
TOP = 7
EXP_DEV = 2
BF = jnp.bfloat16
F32 = jnp.float32
DP = ("y", "x")
OWN = ("z", "c")
NT = (((1,), (1,)), ((), ()))
TN = (((0,), (0,)), ((), ()))


def dot(first, second, dims=(((1,), (0,)), ((), ()))):
    return lax.dot_general(first, second, dims, preferred_element_type=F32)


def expert_kernel(count, width, capacity, experts, chunk, me_ref, slots_ref, *refs):
    rows_refs = refs[:count]
    grads_refs = refs[count : 2 * count]
    gate_ref, up_ref, down_ref = refs[2 * count : 2 * count + 3]
    sums = refs[-10 - count : -10]
    xin, rgrad, hid, ggrad, ugrad = refs[-10:-5]
    ograd, in_ext, res_low, in_acc, out_acc = refs[-5:]
    step = pl.program_id(0)
    expert = me_ref[0] * EXP_DEV + step
    lane = lax.broadcasted_iota(jnp.int32, (capacity, 128), 1)
    mine = (lane == expert) | (lane == expert + experts)

    def spread(piece):
        want = slots_ref[step, piece]
        place = lax.broadcasted_iota(jnp.int32, (capacity, want.shape[-1]), 0)
        return (want == place).astype(F32)

    for piece in range(count):
        hot = spread(piece).astype(BF)
        area = pl.ds(piece * capacity, capacity)
        rows = dot(hot, rows_refs[piece][...])
        xin[0, area, :] = rows[:, :width].astype(BF)
        gates = jnp.sum(jnp.where(mine, rows[:, width:], 0.0), axis=1, keepdims=True)
        grads = dot(hot, grads_refs[piece][:, :width])
        ograd[area, :] = grads.astype(BF)
        rgrad[0, area, :] = (grads * gates).astype(BF)

    def part(index, carry):
        area = pl.ds(pl.multiple_of(index * chunk, chunk), chunk)
        rows = xin[0, area, :]
        res_grad = rgrad[0, area, :]
        gate = dot(rows, gate_ref[0])
        up = dot(rows, up_ref[0])
        hidden_grad = dot(res_grad, down_ref[0], NT)
        sig = jax.nn.sigmoid(gate)
        silu = gate * sig
        hidden = (silu * up).astype(BF)
        hid[0, area, :] = hidden
        gate_grad = (hidden_grad * up * (sig * (1.0 + gate * (1.0 - sig)))).astype(BF)
        up_grad = (hidden_grad * silu).astype(BF)
        ggrad[0, area, :] = gate_grad
        ugrad[0, area, :] = up_grad
        in_ext[area, pl.ds(0, width)] = (
            dot(gate_grad, gate_ref[0], NT) + dot(up_grad, up_ref[0], NT)
        ).astype(BF)
        res = dot(hidden, down_ref[0]).astype(BF)
        res_low[area, :] = res
        slot_gate = jnp.sum(res.astype(F32) * ograd[area, :].astype(F32), axis=1, keepdims=True)
        high = slot_gate.astype(BF).astype(F32)
        lanes = lax.broadcasted_iota(jnp.int32, (chunk, 128), 1)
        in_ext[area, pl.ds(width, 128)] = jnp.where(
            lanes == expert, high, jnp.where(lanes == expert + experts, slot_gate - high, 0.0)
        ).astype(BF)
        return carry

    lax.fori_loop(0, count * capacity // chunk, part, 0)

    for piece in range(count):
        hot = spread(piece)
        area = pl.ds(piece * capacity, capacity)
        low = hot.astype(BF)
        gates = jnp.sum(
            jnp.where(mine, dot(low, rows_refs[piece][:, width:]), 0.0), axis=1, keepdims=True
        )
        back = dot(low, in_ext[area, :], TN)
        result = dot((hot * gates).astype(BF), res_low[area, :], TN)

        @pl.when(step == 0)
        def _():
            in_acc[piece] = back
            out_acc[piece] = result

        @pl.when(step == EXP_DEV - 1)
        def _():
            wide = back.shape[1]
            sums[piece][:, :wide] = (in_acc[piece] + back).astype(BF)
            sums[piece][:, wide:] = (out_acc[piece] + result).astype(BF)


def expert_call(me, slots, rows, grads, gate, up, down, owners, first, carried=None):
    count = len(rows)
    length, wide = rows[0].shape
    width, hidden = gate.shape[1:]
    experts = EXP_DEV * owners
    capacity = 8 * length // experts
    block = count * capacity
    total = owners * capacity
    still = lambda shape: pl.BlockSpec(
        shape, lambda e, m: (0,) * len(shape), pipeline_mode=pl.Buffered(1)
    )
    weight = lambda a, b: pl.BlockSpec((1, a, b), lambda e, m: (e, 0, 0))
    kept = lambda cols: pl.BlockSpec((1, block, cols), lambda e, m: (e, first, 0))
    kept_cols = (width, width, hidden, hidden, hidden)
    in_specs = (
        [still((EXP_DEV, count, 1, length))]
        + [still((length, wide))] * (2 * count)
        + [weight(width, hidden), weight(width, hidden), weight(hidden, width)]
    )
    args = [me, slots, *rows, *grads, gate, up, down]
    alias = {}
    if carried is not None:
        for i, value in enumerate(carried):
            alias[len(args)] = count + i
            args.append(value)
            in_specs.append(pl.BlockSpec(memory_space=pl.ANY))
    sums = [(length, wide + width)] * count
    return pl.pallas_call(
        functools.partial(expert_kernel, count, width, capacity, experts, min(512, block)),
        out_shape=[jax.ShapeDtypeStruct(shape, BF) for shape in sums]
        + [jax.ShapeDtypeStruct((EXP_DEV, total, cols), BF) for cols in kept_cols],
        grid_spec=pltpu.PrefetchScalarGridSpec(
            num_scalar_prefetch=1,
            grid=(EXP_DEV,),
            in_specs=in_specs,
            out_specs=[still(shape) for shape in sums] + [kept(cols) for cols in kept_cols],
            scratch_shapes=[
                pltpu.VMEM((block, width), BF),
                pltpu.VMEM((block, wide), BF),
                pltpu.VMEM((block, width), BF),
                pltpu.VMEM((count, length, wide), F32),
                pltpu.VMEM((count, length, width), F32),
            ],
        ),
        input_output_aliases=alias,
        compiler_params=pltpu.CompilerParams(
            dimension_semantics=("arbitrary",), vmem_limit_bytes=60 * 1024 * 1024
        ),
        cost_estimate=pl.CostEstimate(
            flops=14 * EXP_DEV * block * width * hidden,
            transcendentals=EXP_DEV * block * hidden,
            bytes_accessed=60 * 1024 * 1024,
        ),
        name="experts",
    )(*args)


def place_kernel(count, offsets_ref, *refs):
    pieces, out = refs[:count], refs[count]
    for i in range(count):
        start = pl.multiple_of(offsets_ref[i], 16)
        out[pl.ds(start, pieces[i].shape[0]), :] = pieces[i][...]


def place(pieces, offsets, total):
    count, cols = len(pieces), pieces[0].shape[1]
    return pl.pallas_call(
        functools.partial(place_kernel, count),
        out_shape=jax.ShapeDtypeStruct((total, cols), pieces[0].dtype),
        in_specs=[pl.BlockSpec(memory_space=pltpu.SMEM)]
        + [pl.BlockSpec(memory_space=pltpu.VMEM)] * count,
        out_specs=pl.BlockSpec(memory_space=pltpu.VMEM),
        cost_estimate=pl.CostEstimate(
            flops=0, transcendentals=0, bytes_accessed=4 * total * cols
        ),
        name="place",
    )(jnp.stack(offsets).astype(jnp.int32), *pieces)


def product(first_arg, second_arg):
    return jnp.dot(first_arg, second_arg, preferred_element_type=F32)


def product_high(first_arg, second_arg):
    return jnp.dot(
        first_arg, second_arg, precision=lax.Precision.HIGHEST, preferred_element_type=F32
    )


def mm(spec, first_arg, second_arg):
    return jnp.einsum(spec, first_arg, second_arg, preferred_element_type=F32)


def rotary_tables(length, head_size):
    half_dim = head_size // 2
    frequency = 10000.0 ** (-jnp.arange(half_dim, dtype=F32) * 2.0 / head_size)
    angles = jnp.arange(length, dtype=F32)[:, None] * frequency[None, :]
    return (jnp.cos(angles), jnp.sin(angles))


def rotate(tensor, cosine, sine_part):
    half_dim = tensor.shape[-1] // 2
    first_half = tensor[..., :half_dim]
    second_half = tensor[..., half_dim:]
    cos_rows = cosine[:, None, :]
    sin_rows = sine_part[:, None, :]
    return jnp.concatenate(
        [
            first_half * cos_rows - second_half * sin_rows,
            first_half * sin_rows + second_half * cos_rows,
        ],
        axis=-1,
    )


def allowed_mask(length, piece_start, piece_len):
    row_index = jnp.arange(length, dtype=jnp.int32)[:, None]
    col_index = jnp.arange(length, dtype=jnp.int32)[None, :]
    row_inside = (row_index >= piece_start) & (row_index < piece_start + piece_len)
    col_inside = (col_index >= piece_start) & (col_index < piece_start + piece_len)
    return (col_index <= row_index) | row_inside & col_inside


def silu_grad(inputs):
    sigmoid_part = jax.nn.sigmoid(inputs)
    return sigmoid_part * (1.0 + inputs * (1.0 - sigmoid_part))


def high_low(values):
    high = values.astype(BF)
    low = (values - high.astype(F32)).astype(BF)
    return high, low


def shifted(value, axis, by):
    size = lax.axis_size(axis)
    return lax.ppermute(value, axis, [(i, (i + by) % size) for i in range(size)])


def swap(value):
    return shifted(value, "c", 1)


def half(value, index, axis):
    size = value.shape[axis] // 2
    return lax.dynamic_slice_in_dim(value, index * size, size, axis)


def joined(mine, other, core, axis):
    return jnp.where(
        core == 0, jnp.concatenate([mine, other], axis), jnp.concatenate([other, mine], axis)
    )


def pick(value, index, axis):
    return lax.dynamic_index_in_dim(value, index % value.shape[axis], axis, False)


def after(values, *first):
    if not isinstance(values, (list, tuple)):
        return lax.optimization_barrier((values, *first))[0]
    return list(lax.optimization_barrier((*values, *first))[: len(values)])


def ring_gather(value, axis):
    found = [value]
    for _ in range(lax.axis_size(axis) - 1):
        found.append(shifted(found[-1], axis, 1))
    return found


def gather_dp(value):
    rows = value.shape[0]
    cut = (rows // 2 + 15) // 16 * 16
    side = lax.axis_size("x")
    pieces, offsets = [], []

    def add(piece, start, back):
        from_y = (lax.axis_index("y") - back["y"]) % side
        from_x = (lax.axis_index("x") - back["x"]) % side
        pieces.append(piece)
        offsets.append((from_y * side + from_x) * rows + start)

    add(value, 0, {"x": 0, "y": 0})
    along = {axis: ring_gather(value, axis) for axis in "xy"}
    for axis, other in ("xy", "yx"):
        for step in range(1, side):
            add(along[axis][step], 0, {axis: step, other: 0})
    near = len(pieces)
    for start, stop, order in ((0, cut, "xy"), (cut, rows, "yx")):
        for first in range(1, side):
            kept = ring_gather(along[order[0]][first][start:stop], order[1])
            for second in range(1, side):
                add(kept[second], start, {order[0]: first, order[1]: second})
    full = lambda last: place(pieces[:near] + last, offsets, rows * side * side)
    return full, pieces[1:near], pieces[near:]


def ring_reduce(value, axis, at, late):
    size, index = lax.axis_size(axis), lax.axis_index(axis)
    moving = pick(value, index - 1, at)
    for step in range(2, size + 1):
        other = shifted(moving, axis, 1)
        if late:
            other = after(other, *late)
        moving = (other.astype(F32) + pick(value, index - step, at).astype(F32)).astype(BF)
    return moving


def stage_one(values, orders, first=(), late=()):
    values = after(values, *first) if first else values
    return [ring_reduce(v, o[0], "yx".index(o[0]), late) for v, o in zip(values, orders)]


def stage_two(values, orders, first=(), late=()):
    values = after(values, *first) if first else values
    return [ring_reduce(v, o[1], 0, late) for v, o in zip(values, orders)]


def crossed(value, bit):
    depth = lax.axis_size("z")
    return lax.ppermute(value, "z", [(i, i ^ bit) for i in range(depth)])


def reduce_level(value, late=((), (), (), ())):
    depth, level = lax.axis_size("z"), lax.axis_index("z")
    rows, cols = value.shape
    bits = depth.bit_length() - 1
    hold = lambda piece, first: after(piece, *first) if first else piece
    moving = value.reshape(*(2,) * bits, rows // depth, cols)
    for i in range(bits):
        mine = (level >> i) & 1
        at = bits - 1 - i
        other = hold(crossed(pick(moving, 1 - mine, at), 1 << i), late[i])
        moving = (other.astype(F32) + pick(moving, mine, at).astype(F32)).astype(BF)
    for i in reversed(range(bits)):
        mine = (level >> i) & 1
        other = hold(crossed(moving, 1 << i), late[2 * bits - 1 - i])
        at = bits - 1 - i
        moving = jnp.where(
            mine == 0, jnp.stack([moving, other], at), jnp.stack([other, moving], at)
        )
    return moving.reshape(rows, cols)


def body(
    tokens,
    query_weight,
    key_weight,
    value_weight,
    output_weight,
    attn_gain,
    ffn_gain,
    router_weight,
    shared_gate,
    shared_up,
    shared_down,
    expert_gate,
    expert_up,
    expert_down,
    expert_ids,
    piece_starts,
    out_grad,
):
    side = lax.axis_size("x")
    dp = side * side
    owners = lax.axis_size(OWN)
    depth = lax.axis_size("z")
    core = lax.axis_index("c")
    me = lax.axis_index(OWN)
    experts = EXP_DEV * owners
    length, width = tokens.shape
    rows = query_weight.shape[0]
    hidden = shared_gate.shape[1]
    wide, narrow = width // 2, hidden // 2
    head_count = wide // HEAD_DIM
    score_scale = HEAD_DIM ** (-0.5)
    piece_len = min(256, length // 2)
    capacity = 8 * length // experts
    two = lambda mine: jnp.stack([mine, swap(mine)])

    small = jnp.concatenate([router_weight, attn_gain[:, None], ffn_gain[:, None]], axis=1)
    small = jnp.pad(small, ((0, 0), (0, 128 - small.shape[1])))
    first_join, first_near, first_far = gather_dp(
        jnp.concatenate(
            [half(query_weight, core, 1), half(key_weight, core, 1), half(value_weight, core, 1), small],
            axis=1,
        )
    )
    first_full = first_join(first_far)
    tokens_two = two(tokens)
    starts_two = two(piece_starts[0])
    later = after([output_weight, shared_gate, shared_up, shared_down, out_grad], *first_near)
    second_shard = jnp.concatenate(
        [half(later[0], core, 1), half(later[1], core, 1), half(later[2], core, 1)]
        + [half(later[3], core, 1).reshape(rows, narrow)],
        axis=1,
    )
    second_join, second_near, second_far = gather_dp(after(second_shard, *first_far))

    chosen = (expert_ids[:, :, None] == jnp.arange(experts, dtype=jnp.int32)).any(axis=1)
    chosen_low = jnp.pad(chosen.astype(BF), ((0, 0), (0, 128 - experts)))

    levels = [0, depth // 2] + [step for step in range(1, depth) if step != depth // 2]

    grads_sent = jnp.concatenate([later[4], chosen_low], axis=1)
    grads_pair = swap(grads_sent)
    grads_far = {levels[1]: shifted(grads_sent, "z", levels[1])}
    turn_at = after(grads_sent, grads_far[levels[1]])
    for step in levels[2:-1]:
        grads_far[step] = shifted(turn_at, "z", step)
        turn_at = after(turn_at, grads_far[step])

    query_half = first_full[:, :wide]
    key_half = first_full[:, wide : 2 * wide]
    value_half = first_full[:, 2 * wide : 3 * wide]
    small_full = first_full[:, 3 * wide :]
    router_full = small_full[:, :experts]
    gain_one_f = small_full[:, experts].astype(F32)
    gain_two_f = small_full[:, experts + 1].astype(F32)
    token_f = tokens_two.astype(F32)
    norm_one = lax.rsqrt(jnp.mean(token_f * token_f, axis=-1, keepdims=True) + 1e-06)
    attn_in = (token_f * norm_one * gain_one_f).astype(BF).reshape(2 * length, width)
    cosine, sine_part = rotary_tables(length, HEAD_DIM)
    by_head = lambda value: value.reshape(2, length, head_count, HEAD_DIM)
    flat = lambda value: value.reshape(2 * length, wide)
    query_rot = rotate(by_head(product(attn_in, query_half)), cosine, sine_part).astype(BF)
    key_rot = rotate(by_head(product(attn_in, key_half)), cosine, sine_part).astype(BF)
    value_in = after(attn_in, grads_far[levels[1]])
    values = by_head(product(value_in, value_half).astype(BF))
    allowed = jnp.stack([allowed_mask(length, starts_two[i], piece_len) for i in range(2)])
    scores = mm("sqhd,skhd->shqk", query_rot, key_rot) * score_scale
    scores = jnp.where(allowed[:, None], scores, -1e30)
    row_max = jnp.max(scores, axis=-1, keepdims=True)
    exps = jnp.exp(scores - row_max)
    attn_probs = exps / jnp.sum(exps, axis=-1, keepdims=True)
    probs_low = attn_probs.astype(BF)
    second_full = second_join(after(second_far, probs_low))
    output_cols = second_full[:, :wide]
    gate_half = second_full[:, wide : wide + narrow]
    up_half = second_full[:, wide + narrow : wide + 2 * narrow]
    down_cols = second_full[:, wide + 2 * narrow :].reshape(hidden, wide)
    met = swap(
        jnp.concatenate([half(output_cols, 1 - core, 0), half(down_cols, 1 - core, 0)], axis=0)
    )
    output_half = joined(half(output_cols, core, 0), met[:wide], core, 1)
    down_half = joined(half(down_cols, core, 0), met[wide:], core, 1)
    context = flat(mm("shqk,skhd->sqhd", probs_low, after(values, *second_near)).astype(BF))
    held = [grads_far[step] for step in levels[2:-1]]
    out_partial = product(after(context, *held) if held else context, output_half).reshape(2, length, width)
    attn_out = out_partial[0] + swap(out_partial[1].astype(BF)).astype(F32)
    residual = token_f[0] + attn_out
    norm_two = lax.rsqrt(jnp.mean(residual * residual, axis=-1, keepdims=True) + 1e-06)
    ffn_in = (residual * norm_two * gain_two_f).astype(BF)
    router_probs = jax.nn.softmax(product(ffn_in, router_full), axis=-1)
    gates = jnp.where(chosen, router_probs, 0.0)
    gates_high, gates_low = high_low(gates)
    sent = jnp.concatenate(
        [ffn_in, gates_high, gates_low, jnp.zeros((length, 128 - 2 * experts), BF)], axis=1
    )
    sent_other = swap(sent)
    rows_far = {levels[1]: shifted(sent, "z", levels[1])}
    own = me * EXP_DEV + jnp.arange(EXP_DEV)
    own_hot = (own[:, None] == jnp.arange(experts)[None, :]).astype(F32)

    def slots_of(pieces):
        named = jnp.stack([piece[:, width : width + experts] for piece in pieces]).astype(F32)
        mask = mm("ste,oe->ost", named, own_hot)
        found = jnp.where(mask > 0, jnp.cumsum(mask, axis=2) - 1.0, -1.0).astype(jnp.int32)
        return found[:, :, None, :]

    def paired(pieces):
        return [both for piece in pieces for both in (piece, swap(piece))]

    grads_near = [grads_sent, grads_pair] + paired(
        after([grads_far[step] for step in levels[1 : depth // 2]], sent)
    )
    near_slots = slots_of(grads_near)

    ffn_two = jnp.stack([ffn_in, sent_other[:, :width]]).reshape(2 * length, width)
    grad_two = jnp.stack([out_grad, grads_pair[:, :width]]).reshape(2 * length, width)
    shared_gate_act = product(ffn_two, gate_half)
    shared_up_act = product(ffn_two, up_half)
    shared_hidden = (jax.nn.silu(shared_gate_act) * shared_up_act).astype(BF)
    shared_out = product(shared_hidden, down_half).astype(BF).reshape(2, length, width)
    shared_hidden_grad = product(grad_two, down_half.T)
    shared_gate_act_grad = (shared_hidden_grad * shared_up_act * silu_grad(shared_gate_act)).astype(
        BF
    )
    shared_up_act_grad = (shared_hidden_grad * jax.nn.silu(shared_gate_act)).astype(BF)
    shared_gate_grad = product(ffn_two.T, shared_gate_act_grad).astype(BF)
    shared_up_grad = product(ffn_two.T, shared_up_act_grad).astype(BF)
    shared_in_grad = (
        (product(shared_gate_act_grad, gate_half.T) + product(shared_up_act_grad, up_half.T))
        .astype(BF)
        .reshape(2, length, width)
    )
    shared_both = jnp.concatenate(
        [shared_in_grad, jnp.zeros((2, length, 128), BF), shared_out], axis=2
    )
    turn = lambda grad: joined(half(grad, core, 1), swap(half(grad, 1 - core, 1)), core, 0)
    shares = lambda value: value.reshape(side, side, value.shape[0] // dp, -1)
    shared_part = [shares(shared_gate_grad), shares(shared_up_grad)]
    both = ("yx", "xy")
    rows_near = [sent, sent_other] + paired([rows_far[step] for step in levels[1 : depth // 2]])
    sent_next = after([sent, grads_sent], rows_far[levels[1]], shared_in_grad, *shared_part)
    for step in levels[2:]:
        rows_far[step] = shifted(sent_next[0], "z", step)
    grads_far[levels[-1]] = shifted(sent_next[1], "z", levels[-1])
    rows_rest = paired([rows_far[step] for step in levels[depth // 2 :]])
    grads_rest = paired([grads_far[step] for step in levels[depth // 2 :]])

    place_me = me.reshape(1).astype(jnp.int32)
    block = owners // 2
    near = expert_call(
        place_me, near_slots, rows_near, grads_near,
        expert_gate, expert_up, expert_down, owners, 0,
    )
    wider = width + 128
    shared_one = stage_one(shared_part, both, late=(near[block],))
    hidden_low = after(shared_hidden, near[block])
    down_part = [shares(turn(product(hidden_low.T, grad_two).astype(BF)))]
    summed = lambda mine, other, part: (
        mine[:, part].astype(F32) + other[:, part].astype(F32)
    ).astype(BF)
    to_in, to_out = slice(0, wider), slice(wider, None)
    others = [swap(near[i]) for i in range(3, block, 2)]
    mines = [near[i] for i in range(2, block, 2)]
    sent_back = [summed(m, o, to_in) for m, o in zip(mines, others)]
    far_slots = after(slots_of(grads_rest), *sent_back, *shared_one, *down_part)
    far = expert_call(
        place_me, far_slots, rows_rest, grads_rest,
        expert_gate, expert_up, expert_down, owners, 1, near[block:],
    )
    expert_in, res_grad, routed_hidden, routed_gate_grad, routed_up_grad = far[block:]
    gate_grad = mm("erd,erf->edf", expert_in, routed_gate_grad).astype(BF)
    mines += [far[i] for i in range(0, block, 2)]
    near_back = [shifted(sent_back[i], "z", -levels[i + 1]) for i in range(depth // 2 - 1)]
    shared_two = stage_two(shared_one, both, late=(gate_grad,))
    others += after(
        [swap(far[i]) for i in range(1, block, 2)], gate_grad, *near_back, *shared_two
    )
    sent_back += [
        summed(m, o, to_in) for m, o in zip(mines[depth // 2 - 1 :], others[depth // 2 - 1 :])
    ]
    back_in = near_back + [
        shifted(sent_back[i], "z", -levels[i + 1]) for i in range(depth // 2 - 1, depth - 1)
    ]
    routed_up_grad, res_grad = after([routed_up_grad, res_grad], *sent_back)
    up_grad = mm("erd,erf->edf", expert_in, routed_up_grad).astype(BF)
    down_grad = mm("erf,erd->efd", routed_hidden, res_grad).astype(BF)
    own_chip = (near[0].astype(F32) + shared_both[0].astype(F32)) + swap(
        near[1] + shared_both[1]
    ).astype(F32)
    back = own_chip[:, :wider]
    for piece in after(back_in[: depth // 2 - 1], up_grad):
        back += piece.astype(F32)

    blocks = [
        [grad[e].reshape(side, side, grad.shape[1] // dp, grad.shape[2]) for e in range(EXP_DEV)]
        for grad in (gate_grad, up_grad, down_grad)
    ]
    gate_one = stage_one(blocks[0], both, (*shared_two, *sent_back[depth // 2 - 1 :]))
    for piece in after(back_in[depth // 2 - 1 :], down_grad, *gate_one):
        back += piece.astype(F32)

    probs_grad = back[:, width : width + experts] + back[:, width + experts : width + 2 * experts]
    logits_grad = router_probs * (
        probs_grad - jnp.sum(router_probs * probs_grad, axis=-1, keepdims=True)
    )
    router_in_grad = product_high(logits_grad, router_full.astype(F32).T)
    ffn_in_grad = back[:, :width] + router_in_grad
    ffn_gain_terms = ffn_in_grad * residual * norm_two
    upstream_two = ffn_in_grad * gain_two_f
    residual_grad = (
        out_grad.astype(F32)
        + norm_two * upstream_two
        - residual * norm_two**3 * jnp.mean(upstream_two * residual, axis=-1, keepdims=True)
    )
    residual_low = residual_grad.astype(BF)
    attn_grad_two = two(residual_low).reshape(2 * length, width)
    output_grad = product(context.T, attn_grad_two).astype(BF)
    output_grad = turn(output_grad)
    context_grad = by_head(product(attn_grad_two, output_half.T).astype(BF))
    value_grad = flat(mm("shqk,sqhd->skhd", probs_low, context_grad).astype(BF))
    up_one = stage_one(blocks[1], both, gate_one, (value_grad,))
    down_one = stage_one(down_part, both[:1], gate_one, (value_grad,))
    moving = after(summed(mines[0], others[0], to_out), back)
    arrived = [after(shifted(moving, "z", -levels[1]), value_grad)]
    context_late = after(context_grad, *up_one, *arrived, *down_one)
    value_wgrad = product(attn_in.T, value_grad).astype(BF)
    early = [shares(output_grad), shares(value_wgrad)]
    early_one = stage_one(early, both, up_one)
    probs_grad_att = mm("sqhd,skhd->shqk", context_late, values)
    row_delta = jnp.sum(attn_probs * probs_grad_att, axis=-1, keepdims=True)
    scores_grad = (attn_probs * (probs_grad_att - row_delta)).astype(BF)
    scores_grad = after(scores_grad, *early)
    query_grad = mm("shqk,skhd->sqhd", scores_grad, key_rot) * score_scale
    key_grad = mm("shqk,sqhd->skhd", scores_grad, query_rot) * score_scale
    query_pre_grad = flat(rotate(query_grad, cosine, -sine_part).astype(BF))
    key_pre_grad = flat(rotate(key_grad, cosine, -sine_part).astype(BF))
    query_wgrad = product(attn_in.T, query_pre_grad).astype(BF)
    key_wgrad = product(attn_in.T, key_pre_grad).astype(BF)
    in_partial = (
        product(query_pre_grad, query_half.T)
        + product(key_pre_grad, key_half.T)
        + product(value_grad, value_half.T)
    ).reshape(2, length, width)
    gate_two = stage_two(gate_one, both, up_one, (query_wgrad,))
    shared_down = stage_two(down_one, both[:1], late=(query_wgrad,))
    attn_in_grad = after(in_partial[0], *early_one, *gate_two, *shared_down) + swap(in_partial[1].astype(BF)).astype(F32)
    token_mine, norm_mine = token_f[0], norm_one[0]
    attn_gain_terms = attn_in_grad * token_mine * norm_mine
    upstream_one = attn_in_grad * gain_one_f
    tokens_grad = (
        residual_grad
        + norm_mine * upstream_one
        - token_mine * norm_mine**3 * jnp.mean(upstream_one * token_mine, axis=-1, keepdims=True)
    )
    lanes = jnp.arange(128)
    unit = lambda lane: jnp.broadcast_to((lanes == lane).astype(F32), (length, 128))
    small_grads = (
        product_high(ffn_in.astype(F32).T, jnp.pad(logits_grad, ((0, 0), (0, 128 - experts))))
        + product_high(ffn_gain_terms.T, unit(experts + 1))
        + product_high(attn_gain_terms.T, unit(experts))
    ).astype(BF)

    done_wgrads = (query_wgrad, key_wgrad)
    early_two = stage_two(early_one, both)
    late = [shares(query_wgrad), shares(jnp.concatenate([key_wgrad, small_grads], axis=1))]
    late_one = stage_one(late, both)
    late_two = stage_two(late_one, both, early_two)
    up_two = stage_two(up_one, both, late_two)
    down_two = stage_two(stage_one(blocks[2], both, late_two), both)
    expert_shares = [jnp.stack(pair).astype(F32) for pair in (gate_two, up_two, down_two)]
    shared_share = reduce_level(after(jnp.concatenate(shared_two, axis=0), back), ((value_grad,), done_wgrads, early_two, late_one))
    shared_share = after(shared_share, *late_two)
    early_share = reduce_level(jnp.concatenate([*early_two, *shared_down], axis=0))
    late_share = reduce_level(jnp.concatenate(late_two, axis=1))

    for i in range(1, depth - 1):
        moving = after(summed(mines[i], others[i], to_out), *early_one, arrived[-1])
        piece = shifted(moving, "z", -levels[i + 1])
        arrived.append(after(piece, *(late_one if i < depth - 2 else late_two)))
    moe_out = own_chip[:, wider:]
    for piece in arrived:
        moe_out += piece.astype(F32)

    early_other, late_other, shared_other = swap(early_share), swap(late_share), swap(shared_share)
    column = lambda mine, other, start, size: joined(
        mine[:, start : start + size], other[:, start : start + size], core, 1
    ).astype(F32)
    small_sum = late_share[:, 2 * wide :].astype(F32) + late_other[:, 2 * wide :].astype(F32)
    stacked = lambda mine, other, start, size: joined(
        mine[start : start + size], other[start : start + size], core, 1
    ).astype(F32)

    stream_out = residual + moe_out
    stat_rms = jnp.stack(
        [
            jnp.sqrt(jnp.mean(attn_out * attn_out)),
            jnp.sqrt(jnp.mean(moe_out * moe_out)),
            jnp.sqrt(jnp.mean(stream_out * stream_out)),
        ]
    )[None, :]
    return (
        stream_out.astype(BF),
        tokens_grad.astype(BF),
        column(late_share, late_other, 0, wide),
        column(late_share, late_other, wide, wide),
        stacked(early_share, early_other, rows, rows),
        stacked(early_share, early_other, 0, rows),
        small_sum[:, experts],
        small_sum[:, experts + 1],
        small_sum[:, :experts],
        stacked(shared_share, shared_other, 0, rows),
        stacked(shared_share, shared_other, rows, rows),
        stacked(early_share, early_other, 2 * rows, early_share.shape[0] - 2 * rows),
        *expert_shares,
        stat_rms,
    )


def solution(mesh):
    side = math.isqrt(mesh.shape["dp"])
    fine = Mesh(
        mesh.devices.reshape(side, side, mesh.shape["expert"] // 2, 2), ("y", "x", "z", "c")
    )
    whole = P(("y", "x", "z", "c"), None)
    dense = P(DP, None)
    routed = P(OWN, None, None)
    in_specs = (
        whole, dense, dense, dense, dense, P(DP), P(DP), dense, dense, dense, dense,
        routed, routed, routed, whole, P(("y", "x", "z", "c")), whole,
    )
    shares = P(OWN, DP, None)
    out_specs = (
        whole, whole, dense, dense, dense, dense, P(DP), P(DP), dense, dense, dense, dense,
        shares, shares, shares, whole,
    )
    return jax.shard_map(body, mesh=fine, in_specs=in_specs, out_specs=out_specs, check_vma=False)
```

```python
import functools
import math

import jax
import jax.numpy as jnp
from jax import lax
from jax.experimental import pallas as pl
from jax.experimental.pallas import tpu as pltpu
from jax.sharding import Mesh
from jax.sharding import PartitionSpec as P

HEAD_DIM = 128
TOP = 7
EXP_DEV = 2
BF = jnp.bfloat16
F32 = jnp.float32
DP = ("y", "x")
OWN = ("z", "c")
NT = (((1,), (1,)), ((), ()))
TN = (((0,), (0,)), ((), ()))


def dot(first, second, dims=(((1,), (0,)), ((), ()))):
    return lax.dot_general(first, second, dims, preferred_element_type=F32)


def expert_kernel(count, width, capacity, experts, chunk, me_ref, slots_ref, *refs):
    rows_refs = refs[:count]
    grads_refs = refs[count : 2 * count]
    gate_ref, up_ref, down_ref = refs[2 * count : 2 * count + 3]
    sums = refs[-10 - count : -10]
    xin, rgrad, hid, ggrad, ugrad = refs[-10:-5]
    ograd, in_ext, res_low, in_acc, out_acc = refs[-5:]
    step = pl.program_id(0)
    expert = me_ref[0] * EXP_DEV + step
    lane = lax.broadcasted_iota(jnp.int32, (capacity, 128), 1)
    mine = (lane == expert) | (lane == expert + experts)

    def spread(piece):
        want = slots_ref[step, piece]
        place = lax.broadcasted_iota(jnp.int32, (capacity, want.shape[-1]), 0)
        return (want == place).astype(F32)

    for piece in range(count):
        hot = spread(piece).astype(BF)
        area = pl.ds(piece * capacity, capacity)
        rows = dot(hot, rows_refs[piece][...])
        xin[0, area, :] = rows[:, :width].astype(BF)
        gates = jnp.sum(jnp.where(mine, rows[:, width:], 0.0), axis=1, keepdims=True)
        grads = dot(hot, grads_refs[piece][:, :width])
        ograd[area, :] = grads.astype(BF)
        rgrad[0, area, :] = (grads * gates).astype(BF)

    def part(index, carry):
        area = pl.ds(pl.multiple_of(index * chunk, chunk), chunk)
        rows = xin[0, area, :]
        res_grad = rgrad[0, area, :]
        gate = dot(rows, gate_ref[0])
        up = dot(rows, up_ref[0])
        hidden_grad = dot(res_grad, down_ref[0], NT)
        sig = jax.nn.sigmoid(gate)
        silu = gate * sig
        hidden = (silu * up).astype(BF)
        hid[0, area, :] = hidden
        gate_grad = (hidden_grad * up * (sig * (1.0 + gate * (1.0 - sig)))).astype(BF)
        up_grad = (hidden_grad * silu).astype(BF)
        ggrad[0, area, :] = gate_grad
        ugrad[0, area, :] = up_grad
        in_ext[area, pl.ds(0, width)] = (
            dot(gate_grad, gate_ref[0], NT) + dot(up_grad, up_ref[0], NT)
        ).astype(BF)
        res = dot(hidden, down_ref[0]).astype(BF)
        res_low[area, :] = res
        slot_gate = jnp.sum(res.astype(F32) * ograd[area, :].astype(F32), axis=1, keepdims=True)
        high = slot_gate.astype(BF).astype(F32)
        lanes = lax.broadcasted_iota(jnp.int32, (chunk, 128), 1)
        in_ext[area, pl.ds(width, 128)] = jnp.where(
            lanes == expert, high, jnp.where(lanes == expert + experts, slot_gate - high, 0.0)
        ).astype(BF)
        return carry

    lax.fori_loop(0, count * capacity // chunk, part, 0)

    for piece in range(count):
        hot = spread(piece)
        area = pl.ds(piece * capacity, capacity)
        low = hot.astype(BF)
        gates = jnp.sum(
            jnp.where(mine, dot(low, rows_refs[piece][:, width:]), 0.0), axis=1, keepdims=True
        )
        back = dot(low, in_ext[area, :], TN)
        result = dot((hot * gates).astype(BF), res_low[area, :], TN)

        @pl.when(step == 0)
        def _():
            in_acc[piece] = back
            out_acc[piece] = result

        @pl.when(step == EXP_DEV - 1)
        def _():
            wide = back.shape[1]
            sums[piece][:, :wide] = (in_acc[piece] + back).astype(BF)
            sums[piece][:, wide:] = (out_acc[piece] + result).astype(BF)


def expert_call(me, slots, rows, grads, gate, up, down, owners, first, carried=None):
    count = len(rows)
    length, wide = rows[0].shape
    width, hidden = gate.shape[1:]
    experts = EXP_DEV * owners
    capacity = 8 * length // experts
    block = count * capacity
    total = owners * capacity
    still = lambda shape: pl.BlockSpec(
        shape, lambda e, m: (0,) * len(shape), pipeline_mode=pl.Buffered(1)
    )
    weight = lambda a, b: pl.BlockSpec((1, a, b), lambda e, m: (e, 0, 0))
    kept = lambda cols: pl.BlockSpec((1, block, cols), lambda e, m: (e, first, 0))
    kept_cols = (width, width, hidden, hidden, hidden)
    in_specs = (
        [still((EXP_DEV, count, 1, length))]
        + [still((length, wide))] * (2 * count)
        + [weight(width, hidden), weight(width, hidden), weight(hidden, width)]
    )
    args = [me, slots, *rows, *grads, gate, up, down]
    alias = {}
    if carried is not None:
        for i, value in enumerate(carried):
            alias[len(args)] = count + i
            args.append(value)
            in_specs.append(pl.BlockSpec(memory_space=pl.ANY))
    sums = [(length, wide + width)] * count
    return pl.pallas_call(
        functools.partial(expert_kernel, count, width, capacity, experts, min(512, block)),
        out_shape=[jax.ShapeDtypeStruct(shape, BF) for shape in sums]
        + [jax.ShapeDtypeStruct((EXP_DEV, total, cols), BF) for cols in kept_cols],
        grid_spec=pltpu.PrefetchScalarGridSpec(
            num_scalar_prefetch=1,
            grid=(EXP_DEV,),
            in_specs=in_specs,
            out_specs=[still(shape) for shape in sums] + [kept(cols) for cols in kept_cols],
            scratch_shapes=[
                pltpu.VMEM((block, width), BF),
                pltpu.VMEM((block, wide), BF),
                pltpu.VMEM((block, width), BF),
                pltpu.VMEM((count, length, wide), F32),
                pltpu.VMEM((count, length, width), F32),
            ],
        ),
        input_output_aliases=alias,
        compiler_params=pltpu.CompilerParams(
            dimension_semantics=("arbitrary",), vmem_limit_bytes=60 * 1024 * 1024
        ),
        cost_estimate=pl.CostEstimate(
            flops=14 * EXP_DEV * block * width * hidden,
            transcendentals=EXP_DEV * block * hidden,
            bytes_accessed=60 * 1024 * 1024,
        ),
        name="experts",
    )(*args)


def place_kernel(count, offsets_ref, *refs):
    pieces, out = refs[:count], refs[count]
    for i in range(count):
        start = pl.multiple_of(offsets_ref[i], 16)
        out[pl.ds(start, pieces[i].shape[0]), :] = pieces[i][...]


def place(pieces, offsets, total):
    count, cols = len(pieces), pieces[0].shape[1]
    return pl.pallas_call(
        functools.partial(place_kernel, count),
        out_shape=jax.ShapeDtypeStruct((total, cols), pieces[0].dtype),
        in_specs=[pl.BlockSpec(memory_space=pltpu.SMEM)]
        + [pl.BlockSpec(memory_space=pltpu.VMEM)] * count,
        out_specs=pl.BlockSpec(memory_space=pltpu.VMEM),
        cost_estimate=pl.CostEstimate(
            flops=0, transcendentals=0, bytes_accessed=4 * total * cols
        ),
        name="place",
    )(jnp.stack(offsets).astype(jnp.int32), *pieces)


def product(first_arg, second_arg):
    return jnp.dot(first_arg, second_arg, preferred_element_type=F32)


def product_high(first_arg, second_arg):
    return jnp.dot(
        first_arg, second_arg, precision=lax.Precision.HIGHEST, preferred_element_type=F32
    )


def mm(spec, first_arg, second_arg):
    return jnp.einsum(spec, first_arg, second_arg, preferred_element_type=F32)


def rotary_tables(length, head_size):
    half_dim = head_size // 2
    frequency = 10000.0 ** (-jnp.arange(half_dim, dtype=F32) * 2.0 / head_size)
    angles = jnp.arange(length, dtype=F32)[:, None] * frequency[None, :]
    return (jnp.cos(angles), jnp.sin(angles))


def rotate(tensor, cosine, sine_part):
    half_dim = tensor.shape[-1] // 2
    first_half = tensor[..., :half_dim]
    second_half = tensor[..., half_dim:]
    cos_rows = cosine[:, None, :]
    sin_rows = sine_part[:, None, :]
    return jnp.concatenate(
        [
            first_half * cos_rows - second_half * sin_rows,
            first_half * sin_rows + second_half * cos_rows,
        ],
        axis=-1,
    )


def allowed_mask(length, piece_start, piece_len):
    row_index = jnp.arange(length, dtype=jnp.int32)[:, None]
    col_index = jnp.arange(length, dtype=jnp.int32)[None, :]
    row_inside = (row_index >= piece_start) & (row_index < piece_start + piece_len)
    col_inside = (col_index >= piece_start) & (col_index < piece_start + piece_len)
    return (col_index <= row_index) | row_inside & col_inside


def silu_grad(inputs):
    sigmoid_part = jax.nn.sigmoid(inputs)
    return sigmoid_part * (1.0 + inputs * (1.0 - sigmoid_part))


def high_low(values):
    high = values.astype(BF)
    low = (values - high.astype(F32)).astype(BF)
    return high, low


def shifted(value, axis, by):
    size = lax.axis_size(axis)
    return lax.ppermute(value, axis, [(i, (i + by) % size) for i in range(size)])


def swap(value):
    return shifted(value, "c", 1)


def half(value, index, axis):
    size = value.shape[axis] // 2
    return lax.dynamic_slice_in_dim(value, index * size, size, axis)


def joined(mine, other, core, axis):
    return jnp.where(
        core == 0, jnp.concatenate([mine, other], axis), jnp.concatenate([other, mine], axis)
    )


def pick(value, index, axis):
    return lax.dynamic_index_in_dim(value, index % value.shape[axis], axis, False)


def after(values, *first):
    if not isinstance(values, (list, tuple)):
        return lax.optimization_barrier((values, *first))[0]
    return list(lax.optimization_barrier((*values, *first))[: len(values)])


def ring_gather(value, axis):
    found = [value]
    for _ in range(lax.axis_size(axis) - 1):
        found.append(shifted(found[-1], axis, 1))
    return found


def gather_dp(value):
    rows = value.shape[0]
    cut = (rows // 2 + 15) // 16 * 16
    side = lax.axis_size("x")
    pieces, offsets = [], []

    def add(piece, start, back):
        from_y = (lax.axis_index("y") - back["y"]) % side
        from_x = (lax.axis_index("x") - back["x"]) % side
        pieces.append(piece)
        offsets.append((from_y * side + from_x) * rows + start)

    add(value, 0, {"x": 0, "y": 0})
    along = {axis: ring_gather(value, axis) for axis in "xy"}
    for axis, other in ("xy", "yx"):
        for step in range(1, side):
            add(along[axis][step], 0, {axis: step, other: 0})
    near = len(pieces)
    for start, stop, order in ((0, cut, "xy"), (cut, rows, "yx")):
        for first in range(1, side):
            kept = ring_gather(along[order[0]][first][start:stop], order[1])
            for second in range(1, side):
                add(kept[second], start, {order[0]: first, order[1]: second})
    full = lambda last: place(pieces[:near] + last, offsets, rows * side * side)
    return full, pieces[1:near], pieces[near:]


def ring_reduce(value, axis, at, late):
    size, index = lax.axis_size(axis), lax.axis_index(axis)
    moving = pick(value, index - 1, at)
    for step in range(2, size + 1):
        other = shifted(moving, axis, 1)
        if late:
            other = after(other, *late)
        moving = (other.astype(F32) + pick(value, index - step, at).astype(F32)).astype(BF)
    return moving


def stage_one(values, orders, first=(), late=()):
    values = after(values, *first) if first else values
    return [ring_reduce(v, o[0], "yx".index(o[0]), late) for v, o in zip(values, orders)]


def stage_two(values, orders, first=(), late=()):
    values = after(values, *first) if first else values
    return [ring_reduce(v, o[1], 0, late) for v, o in zip(values, orders)]


def crossed(value, bit):
    depth = lax.axis_size("z")
    return lax.ppermute(value, "z", [(i, i ^ bit) for i in range(depth)])


def reduce_level(value, late=((), (), (), ())):
    depth, level = lax.axis_size("z"), lax.axis_index("z")
    rows, cols = value.shape
    bits = depth.bit_length() - 1
    hold = lambda piece, first: after(piece, *first) if first else piece
    moving = value.reshape(*(2,) * bits, rows // depth, cols)
    for i in range(bits):
        mine = (level >> i) & 1
        at = bits - 1 - i
        other = hold(crossed(pick(moving, 1 - mine, at), 1 << i), late[i])
        moving = (other.astype(F32) + pick(moving, mine, at).astype(F32)).astype(BF)
    for i in reversed(range(bits)):
        mine = (level >> i) & 1
        other = hold(crossed(moving, 1 << i), late[2 * bits - 1 - i])
        at = bits - 1 - i
        moving = jnp.where(
            mine == 0, jnp.stack([moving, other], at), jnp.stack([other, moving], at)
        )
    return moving.reshape(rows, cols)


def body(
    tokens,
    query_weight,
    key_weight,
    value_weight,
    output_weight,
    attn_gain,
    ffn_gain,
    router_weight,
    shared_gate,
    shared_up,
    shared_down,
    expert_gate,
    expert_up,
    expert_down,
    expert_ids,
    piece_starts,
    out_grad,
):
    side = lax.axis_size("x")
    dp = side * side
    owners = lax.axis_size(OWN)
    depth = lax.axis_size("z")
    core = lax.axis_index("c")
    me = lax.axis_index(OWN)
    experts = EXP_DEV * owners
    length, width = tokens.shape
    rows = query_weight.shape[0]
    hidden = shared_gate.shape[1]
    wide, narrow = width // 2, hidden // 2
    head_count = wide // HEAD_DIM
    score_scale = HEAD_DIM ** (-0.5)
    piece_len = min(256, length // 2)
    capacity = 8 * length // experts
    two = lambda mine: jnp.stack([mine, swap(mine)])

    small = jnp.concatenate([router_weight, attn_gain[:, None], ffn_gain[:, None]], axis=1)
    small = jnp.pad(small, ((0, 0), (0, 128 - small.shape[1])))
    first_join, first_near, first_far = gather_dp(
        jnp.concatenate(
            [half(query_weight, core, 1), half(key_weight, core, 1), half(value_weight, core, 1), small],
            axis=1,
        )
    )
    first_full = first_join(first_far)
    tokens_two = two(tokens)
    starts_two = two(piece_starts[0])
    later = after([output_weight, shared_gate, shared_up, shared_down, out_grad], *first_near)
    second_shard = jnp.concatenate(
        [half(later[0], core, 1), half(later[1], core, 1), half(later[2], core, 1)]
        + [half(later[3], core, 1).reshape(rows, narrow)],
        axis=1,
    )
    second_join, second_near, second_far = gather_dp(after(second_shard, *first_far))

    chosen = (expert_ids[:, :, None] == jnp.arange(experts, dtype=jnp.int32)).any(axis=1)
    chosen_low = jnp.pad(chosen.astype(BF), ((0, 0), (0, 128 - experts)))

    levels = [0, depth // 2] + [step for step in range(1, depth) if step != depth // 2]

    grads_sent = jnp.concatenate([later[4], chosen_low], axis=1)
    grads_pair = swap(grads_sent)
    grads_far = {levels[1]: shifted(grads_sent, "z", levels[1])}
    turn_at = after(grads_sent, grads_far[levels[1]])
    for step in levels[2:-1]:
        grads_far[step] = shifted(turn_at, "z", step)
        turn_at = after(turn_at, grads_far[step])

    query_half = first_full[:, :wide]
    key_half = first_full[:, wide : 2 * wide]
    value_half = first_full[:, 2 * wide : 3 * wide]
    small_full = first_full[:, 3 * wide :]
    router_full = small_full[:, :experts]
    gain_one_f = small_full[:, experts].astype(F32)
    gain_two_f = small_full[:, experts + 1].astype(F32)
    token_f = tokens_two.astype(F32)
    norm_one = lax.rsqrt(jnp.mean(token_f * token_f, axis=-1, keepdims=True) + 1e-06)
    attn_in = (token_f * norm_one * gain_one_f).astype(BF).reshape(2 * length, width)
    cosine, sine_part = rotary_tables(length, HEAD_DIM)
    by_head = lambda value: value.reshape(2, length, head_count, HEAD_DIM)
    flat = lambda value: value.reshape(2 * length, wide)
    query_rot = rotate(by_head(product(attn_in, query_half)), cosine, sine_part).astype(BF)
    key_rot = rotate(by_head(product(attn_in, key_half)), cosine, sine_part).astype(BF)
    value_in = after(attn_in, grads_far[levels[1]])
    values = by_head(product(value_in, value_half).astype(BF))
    allowed = jnp.stack([allowed_mask(length, starts_two[i], piece_len) for i in range(2)])
    scores = mm("sqhd,skhd->shqk", query_rot, key_rot) * score_scale
    scores = jnp.where(allowed[:, None], scores, -1e30)
    row_max = jnp.max(scores, axis=-1, keepdims=True)
    exps = jnp.exp(scores - row_max)
    attn_probs = exps / jnp.sum(exps, axis=-1, keepdims=True)
    probs_low = attn_probs.astype(BF)
    second_full = second_join(after(second_far, probs_low))
    output_cols = second_full[:, :wide]
    gate_half = second_full[:, wide : wide + narrow]
    up_half = second_full[:, wide + narrow : wide + 2 * narrow]
    down_cols = second_full[:, wide + 2 * narrow :].reshape(hidden, wide)
    met = swap(
        jnp.concatenate([half(output_cols, 1 - core, 0), half(down_cols, 1 - core, 0)], axis=0)
    )
    output_half = joined(half(output_cols, core, 0), met[:wide], core, 1)
    down_half = joined(half(down_cols, core, 0), met[wide:], core, 1)
    context = flat(mm("shqk,skhd->sqhd", probs_low, after(values, *second_near)).astype(BF))
    held = [grads_far[step] for step in levels[2:-1]]
    out_partial = product(after(context, *held) if held else context, output_half).reshape(2, length, width)
    attn_out = out_partial[0] + swap(out_partial[1].astype(BF)).astype(F32)
    residual = token_f[0] + attn_out
    norm_two = lax.rsqrt(jnp.mean(residual * residual, axis=-1, keepdims=True) + 1e-06)
    ffn_in = (residual * norm_two * gain_two_f).astype(BF)
    router_probs = jax.nn.softmax(product(ffn_in, router_full), axis=-1)
    gates = jnp.where(chosen, router_probs, 0.0)
    gates_high, gates_low = high_low(gates)
    sent = jnp.concatenate(
        [ffn_in, gates_high, gates_low, jnp.zeros((length, 128 - 2 * experts), BF)], axis=1
    )
    sent_other = swap(sent)
    rows_far = {levels[1]: shifted(sent, "z", levels[1])}
    own = me * EXP_DEV + jnp.arange(EXP_DEV)
    own_hot = (own[:, None] == jnp.arange(experts)[None, :]).astype(F32)

    def slots_of(pieces):
        named = jnp.stack([piece[:, width : width + experts] for piece in pieces]).astype(F32)
        mask = mm("ste,oe->ost", named, own_hot)
        found = jnp.where(mask > 0, jnp.cumsum(mask, axis=2) - 1.0, -1.0).astype(jnp.int32)
        return found[:, :, None, :]

    def paired(pieces):
        return [both for piece in pieces for both in (piece, swap(piece))]

    grads_near = [grads_sent, grads_pair] + paired(
        after([grads_far[step] for step in levels[1 : depth // 2]], sent)
    )
    near_slots = slots_of(grads_near)

    ffn_two = jnp.stack([ffn_in, sent_other[:, :width]]).reshape(2 * length, width)
    grad_two = jnp.stack([out_grad, grads_pair[:, :width]]).reshape(2 * length, width)
    shared_gate_act = product(ffn_two, gate_half)
    shared_up_act = product(ffn_two, up_half)
    shared_hidden = (jax.nn.silu(shared_gate_act) * shared_up_act).astype(BF)
    shared_out = product(shared_hidden, down_half).astype(BF).reshape(2, length, width)
    shared_hidden_grad = product(grad_two, down_half.T)
    shared_gate_act_grad = (shared_hidden_grad * shared_up_act * silu_grad(shared_gate_act)).astype(
        BF
    )
    shared_up_act_grad = (shared_hidden_grad * jax.nn.silu(shared_gate_act)).astype(BF)
    shared_gate_grad = product(ffn_two.T, shared_gate_act_grad).astype(BF)
    shared_up_grad = product(ffn_two.T, shared_up_act_grad).astype(BF)
    shared_in_grad = (
        (product(shared_gate_act_grad, gate_half.T) + product(shared_up_act_grad, up_half.T))
        .astype(BF)
        .reshape(2, length, width)
    )
    shared_both = jnp.concatenate(
        [shared_in_grad, jnp.zeros((2, length, 128), BF), shared_out], axis=2
    )
    turn = lambda grad: joined(half(grad, core, 1), swap(half(grad, 1 - core, 1)), core, 0)
    shares = lambda value: value.reshape(side, side, value.shape[0] // dp, -1)
    shared_part = [shares(shared_gate_grad), shares(shared_up_grad)]
    both = ("yx", "xy")
    rows_near = [sent, sent_other] + paired([rows_far[step] for step in levels[1 : depth // 2]])
    sent_next = after([sent, grads_sent], rows_far[levels[1]], shared_in_grad, *shared_part)
    for step in levels[2:]:
        rows_far[step] = shifted(sent_next[0], "z", step)
    grads_far[levels[-1]] = shifted(sent_next[1], "z", levels[-1])
    rows_rest = paired([rows_far[step] for step in levels[depth // 2 :]])
    grads_rest = paired([grads_far[step] for step in levels[depth // 2 :]])

    place_me = me.reshape(1).astype(jnp.int32)
    block = owners // 2
    near = expert_call(
        place_me, near_slots, rows_near, grads_near,
        expert_gate, expert_up, expert_down, owners, 0,
    )
    wider = width + 128
    shared_one = stage_one(shared_part, both, late=(near[block],))
    hidden_low = after(shared_hidden, near[block])
    down_part = [shares(turn(product(hidden_low.T, grad_two).astype(BF)))]
    summed = lambda mine, other, part: (
        mine[:, part].astype(F32) + other[:, part].astype(F32)
    ).astype(BF)
    to_in, to_out = slice(0, wider), slice(wider, None)
    others = [swap(near[i]) for i in range(3, block, 2)]
    mines = [near[i] for i in range(2, block, 2)]
    sent_back = [summed(m, o, to_in) for m, o in zip(mines, others)]
    far_slots = after(slots_of(grads_rest), *sent_back, *shared_one, *down_part)
    far = expert_call(
        place_me, far_slots, rows_rest, grads_rest,
        expert_gate, expert_up, expert_down, owners, 1, near[block:],
    )
    expert_in, res_grad, routed_hidden, routed_gate_grad, routed_up_grad = far[block:]
    gate_grad = mm("erd,erf->edf", expert_in, routed_gate_grad).astype(BF)
    mines += [far[i] for i in range(0, block, 2)]
    near_back = [shifted(sent_back[i], "z", -levels[i + 1]) for i in range(depth // 2 - 1)]
    shared_two = stage_two(shared_one, both, late=(gate_grad,))
    others += after(
        [swap(far[i]) for i in range(1, block, 2)], gate_grad, *near_back, *shared_two
    )
    sent_back += [
        summed(m, o, to_in) for m, o in zip(mines[depth // 2 - 1 :], others[depth // 2 - 1 :])
    ]
    back_in = near_back + [
        shifted(sent_back[i], "z", -levels[i + 1]) for i in range(depth // 2 - 1, depth - 1)
    ]
    routed_up_grad = after(routed_up_grad, *sent_back)
    up_grad = mm("erd,erf->edf", expert_in, routed_up_grad).astype(BF)
    own_chip = (near[0].astype(F32) + shared_both[0].astype(F32)) + swap(
        near[1] + shared_both[1]
    ).astype(F32)
    back = own_chip[:, :wider]
    for piece in after(back_in[: depth // 2 - 1], up_grad):
        back += piece.astype(F32)

    in_blocks = lambda grad: [
        grad[e].reshape(side, side, grad.shape[1] // dp, grad.shape[2]) for e in range(EXP_DEV)
    ]
    gate_first = (*shared_two, *sent_back[depth // 2 - 1 :])
    gate_one = stage_one(in_blocks(gate_grad), both, gate_first, (back, up_grad))
    res_grad = after(res_grad, *gate_one)
    down_grad = mm("erf,erd->efd", routed_hidden, res_grad).astype(BF)
    for piece in after(back_in[depth // 2 - 1 :], down_grad):
        back += piece.astype(F32)

    probs_grad = back[:, width : width + experts] + back[:, width + experts : width + 2 * experts]
    logits_grad = router_probs * (
        probs_grad - jnp.sum(router_probs * probs_grad, axis=-1, keepdims=True)
    )
    router_in_grad = product_high(logits_grad, router_full.astype(F32).T)
    ffn_in_grad = back[:, :width] + router_in_grad
    ffn_gain_terms = ffn_in_grad * residual * norm_two
    upstream_two = ffn_in_grad * gain_two_f
    residual_grad = (
        out_grad.astype(F32)
        + norm_two * upstream_two
        - residual * norm_two**3 * jnp.mean(upstream_two * residual, axis=-1, keepdims=True)
    )
    residual_low = residual_grad.astype(BF)
    attn_grad_two = two(residual_grad.astype(BF)).reshape(2 * length, width)
    output_grad = product(context.T, attn_grad_two).astype(BF)
    output_grad = turn(output_grad)
    context_grad = by_head(product(attn_grad_two, output_half.T).astype(BF))
    value_grad = flat(mm("shqk,sqhd->skhd", probs_low, context_grad).astype(BF))
    up_one = stage_one(in_blocks(up_grad), both, gate_one, (value_grad,))
    down_one = stage_one(down_part, both[:1], gate_one, (value_grad,))
    moving = after(summed(mines[0], others[0], to_out), back)
    arrived = [after(shifted(moving, "z", -levels[1]), value_grad)]
    context_late = after(context_grad, *up_one, *arrived, *down_one)
    value_wgrad = product(attn_in.T, value_grad).astype(BF)
    early = [shares(output_grad), shares(value_wgrad)]
    probs_grad_att = mm("sqhd,skhd->shqk", context_late, values)
    row_delta = jnp.sum(attn_probs * probs_grad_att, axis=-1, keepdims=True)
    scores_grad = (attn_probs * (probs_grad_att - row_delta)).astype(BF)
    scores_grad = after(scores_grad, *early)
    query_grad = mm("shqk,skhd->sqhd", scores_grad, key_rot) * score_scale
    key_grad = mm("shqk,sqhd->skhd", scores_grad, query_rot) * score_scale
    query_pre_grad = flat(rotate(query_grad, cosine, -sine_part).astype(BF))
    key_pre_grad = flat(rotate(key_grad, cosine, -sine_part).astype(BF))
    query_wgrad = product(attn_in.T, query_pre_grad).astype(BF)
    key_wgrad = product(attn_in.T, key_pre_grad).astype(BF)
    in_partial = (
        product(query_pre_grad, query_half.T)
        + product(key_pre_grad, key_half.T)
        + product(value_grad, value_half.T)
    ).reshape(2, length, width)
    gate_two = stage_two(gate_one, both, up_one, (query_wgrad,))
    shared_down = stage_two(down_one, both[:1], late=(query_wgrad,))
    attn_in_grad = after(in_partial[0], *gate_two, *shared_down) + swap(in_partial[1].astype(BF)).astype(F32)
    token_mine, norm_mine = token_f[0], norm_one[0]
    attn_gain_terms = attn_in_grad * token_mine * norm_mine
    upstream_one = attn_in_grad * gain_one_f
    tokens_grad = (
        residual_grad
        + norm_mine * upstream_one
        - token_mine * norm_mine**3 * jnp.mean(upstream_one * token_mine, axis=-1, keepdims=True)
    )
    lanes = jnp.arange(128)
    unit = lambda lane: jnp.broadcast_to((lanes == lane).astype(F32), (length, 128))
    small_grads = (
        product_high(ffn_in.astype(F32).T, jnp.pad(logits_grad, ((0, 0), (0, 128 - experts))))
        + product_high(ffn_gain_terms.T, unit(experts + 1))
        + product_high(attn_gain_terms.T, unit(experts))
    ).astype(BF)

    done_wgrads = (query_wgrad, key_wgrad)
    early_one = stage_one(early, both, up_one, (small_grads,))
    early_two = stage_two(early_one, both)
    late = [shares(query_wgrad), shares(jnp.concatenate([key_wgrad, small_grads], axis=1))]
    late_one = stage_one(late, both)
    late_two = stage_two(late_one, both, early_two)
    up_two = stage_two(up_one, both, late_one)
    down_two = stage_two(stage_one(in_blocks(down_grad), both, up_two), both)
    expert_shares = [jnp.stack(pair).astype(F32) for pair in (gate_two, up_two, down_two)]
    shared_share = reduce_level(after(jnp.concatenate(shared_two, axis=0), back), ((value_grad,), done_wgrads, early_two, late_one))
    shared_share = after(shared_share, *late_two)
    early_share = reduce_level(jnp.concatenate([*early_two, *shared_down], axis=0))
    late_share = reduce_level(jnp.concatenate(late_two, axis=1))

    for i in range(1, depth - 1):
        moving = after(summed(mines[i], others[i], to_out), arrived[-1])
        piece = shifted(moving, "z", -levels[i + 1])
        arrived.append(after(piece, *((query_wgrad,) if i < depth - 2 else early_two)))
    moe_out = own_chip[:, wider:]
    for piece in arrived:
        moe_out += piece.astype(F32)

    early_other, late_other, shared_other = swap(early_share), swap(late_share), swap(shared_share)
    column = lambda mine, other, start, size: joined(
        mine[:, start : start + size], other[:, start : start + size], core, 1
    ).astype(F32)
    small_sum = late_share[:, 2 * wide :].astype(F32) + late_other[:, 2 * wide :].astype(F32)
    stacked = lambda mine, other, start, size: joined(
        mine[start : start + size], other[start : start + size], core, 1
    ).astype(F32)

    stream_out = residual + moe_out
    stat_rms = jnp.stack(
        [
            jnp.sqrt(jnp.mean(attn_out * attn_out)),
            jnp.sqrt(jnp.mean(moe_out * moe_out)),
            jnp.sqrt(jnp.mean(stream_out * stream_out)),
        ]
    )[None, :]
    return (
        stream_out.astype(BF),
        tokens_grad.astype(BF),
        column(late_share, late_other, 0, wide),
        column(late_share, late_other, wide, wide),
        stacked(early_share, early_other, rows, rows),
        stacked(early_share, early_other, 0, rows),
        small_sum[:, experts],
        small_sum[:, experts + 1],
        small_sum[:, :experts],
        stacked(shared_share, shared_other, 0, rows),
        stacked(shared_share, shared_other, rows, rows),
        stacked(early_share, early_other, 2 * rows, early_share.shape[0] - 2 * rows),
        *expert_shares,
        stat_rms,
    )


def solution(mesh):
    side = math.isqrt(mesh.shape["dp"])
    fine = Mesh(
        mesh.devices.reshape(side, side, mesh.shape["expert"] // 2, 2), ("y", "x", "z", "c")
    )
    whole = P(("y", "x", "z", "c"), None)
    dense = P(DP, None)
    routed = P(OWN, None, None)
    in_specs = (
        whole, dense, dense, dense, dense, P(DP), P(DP), dense, dense, dense, dense,
        routed, routed, routed, whole, P(("y", "x", "z", "c")), whole,
    )
    shares = P(OWN, DP, None)
    out_specs = (
        whole, whole, dense, dense, dense, dense, P(DP), P(DP), dense, dense, dense, dense,
        shares, shares, shares, whole,
    )
    return jax.shard_map(body, mesh=fine, in_specs=in_specs, out_specs=out_specs, check_vma=False)
```

```python
import functools
import math

import jax
import jax.numpy as jnp
from jax import lax
from jax.experimental import pallas as pl
from jax.experimental.pallas import tpu as pltpu
from jax.sharding import Mesh
from jax.sharding import PartitionSpec as P

HEAD_DIM = 128
TOP = 7
EXP_DEV = 2
BF = jnp.bfloat16
F32 = jnp.float32
DP = ("y", "x")
OWN = ("z", "c")
NT = (((1,), (1,)), ((), ()))
TN = (((0,), (0,)), ((), ()))


def dot(first, second, dims=(((1,), (0,)), ((), ()))):
    return lax.dot_general(first, second, dims, preferred_element_type=F32)


def expert_kernel(count, width, capacity, experts, chunk, me_ref, slots_ref, *refs):
    rows_refs = refs[:count]
    grads_refs = refs[count : 2 * count]
    gate_ref, up_ref, down_ref = refs[2 * count : 2 * count + 3]
    sums = refs[-10 - count : -10]
    xin, rgrad, hid, ggrad, ugrad = refs[-10:-5]
    ograd, in_ext, res_low, in_acc, out_acc = refs[-5:]
    step = pl.program_id(0)
    expert = me_ref[0] * EXP_DEV + step
    lane = lax.broadcasted_iota(jnp.int32, (capacity, 128), 1)
    mine = (lane == expert) | (lane == expert + experts)

    def spread(piece):
        want = slots_ref[step, piece]
        place = lax.broadcasted_iota(jnp.int32, (capacity, want.shape[-1]), 0)
        return (want == place).astype(F32)

    for piece in range(count):
        hot = spread(piece).astype(BF)
        area = pl.ds(piece * capacity, capacity)
        rows = dot(hot, rows_refs[piece][...])
        xin[0, area, :] = rows[:, :width].astype(BF)
        gates = jnp.sum(jnp.where(mine, rows[:, width:], 0.0), axis=1, keepdims=True)
        grads = dot(hot, grads_refs[piece][:, :width])
        ograd[area, :] = grads.astype(BF)
        rgrad[0, area, :] = (grads * gates).astype(BF)

    def part(index, carry):
        area = pl.ds(pl.multiple_of(index * chunk, chunk), chunk)
        rows = xin[0, area, :]
        res_grad = rgrad[0, area, :]
        gate = dot(rows, gate_ref[0])
        up = dot(rows, up_ref[0])
        hidden_grad = dot(res_grad, down_ref[0], NT)
        sig = jax.nn.sigmoid(gate)
        silu = gate * sig
        hidden = (silu * up).astype(BF)
        hid[0, area, :] = hidden
        gate_grad = (hidden_grad * up * (sig * (1.0 + gate * (1.0 - sig)))).astype(BF)
        up_grad = (hidden_grad * silu).astype(BF)
        ggrad[0, area, :] = gate_grad
        ugrad[0, area, :] = up_grad
        in_ext[area, pl.ds(0, width)] = (
            dot(gate_grad, gate_ref[0], NT) + dot(up_grad, up_ref[0], NT)
        ).astype(BF)
        res = dot(hidden, down_ref[0]).astype(BF)
        res_low[area, :] = res
        slot_gate = jnp.sum(res.astype(F32) * ograd[area, :].astype(F32), axis=1, keepdims=True)
        high = slot_gate.astype(BF).astype(F32)
        lanes = lax.broadcasted_iota(jnp.int32, (chunk, 128), 1)
        in_ext[area, pl.ds(width, 128)] = jnp.where(
            lanes == expert, high, jnp.where(lanes == expert + experts, slot_gate - high, 0.0)
        ).astype(BF)
        return carry

    lax.fori_loop(0, count * capacity // chunk, part, 0)

    for piece in range(count):
        hot = spread(piece)
        area = pl.ds(piece * capacity, capacity)
        low = hot.astype(BF)
        gates = jnp.sum(
            jnp.where(mine, dot(low, rows_refs[piece][:, width:]), 0.0), axis=1, keepdims=True
        )
        back = dot(low, in_ext[area, :], TN)
        result = dot((hot * gates).astype(BF), res_low[area, :], TN)

        @pl.when(step == 0)
        def _():
            in_acc[piece] = back
            out_acc[piece] = result

        @pl.when(step == EXP_DEV - 1)
        def _():
            wide = back.shape[1]
            sums[piece][:, :wide] = (in_acc[piece] + back).astype(BF)
            sums[piece][:, wide:] = (out_acc[piece] + result).astype(BF)


def expert_call(me, slots, rows, grads, gate, up, down, owners, first, carried=None):
    count = len(rows)
    length, wide = rows[0].shape
    width, hidden = gate.shape[1:]
    experts = EXP_DEV * owners
    capacity = 8 * length // experts
    block = count * capacity
    total = owners * capacity
    still = lambda shape: pl.BlockSpec(
        shape, lambda e, m: (0,) * len(shape), pipeline_mode=pl.Buffered(1)
    )
    weight = lambda a, b: pl.BlockSpec((1, a, b), lambda e, m: (e, 0, 0))
    kept = lambda cols: pl.BlockSpec((1, block, cols), lambda e, m: (e, first, 0))
    kept_cols = (width, width, hidden, hidden, hidden)
    in_specs = (
        [still((EXP_DEV, count, 1, length))]
        + [still((length, wide))] * (2 * count)
        + [weight(width, hidden), weight(width, hidden), weight(hidden, width)]
    )
    args = [me, slots, *rows, *grads, gate, up, down]
    alias = {}
    if carried is not None:
        for i, value in enumerate(carried):
            alias[len(args)] = count + i
            args.append(value)
            in_specs.append(pl.BlockSpec(memory_space=pl.ANY))
    sums = [(length, wide + width)] * count
    return pl.pallas_call(
        functools.partial(expert_kernel, count, width, capacity, experts, min(512, block)),
        out_shape=[jax.ShapeDtypeStruct(shape, BF) for shape in sums]
        + [jax.ShapeDtypeStruct((EXP_DEV, total, cols), BF) for cols in kept_cols],
        grid_spec=pltpu.PrefetchScalarGridSpec(
            num_scalar_prefetch=1,
            grid=(EXP_DEV,),
            in_specs=in_specs,
            out_specs=[still(shape) for shape in sums] + [kept(cols) for cols in kept_cols],
            scratch_shapes=[
                pltpu.VMEM((block, width), BF),
                pltpu.VMEM((block, wide), BF),
                pltpu.VMEM((block, width), BF),
                pltpu.VMEM((count, length, wide), F32),
                pltpu.VMEM((count, length, width), F32),
            ],
        ),
        input_output_aliases=alias,
        compiler_params=pltpu.CompilerParams(
            dimension_semantics=("arbitrary",), vmem_limit_bytes=60 * 1024 * 1024
        ),
        cost_estimate=pl.CostEstimate(
            flops=14 * EXP_DEV * block * width * hidden,
            transcendentals=EXP_DEV * block * hidden,
            bytes_accessed=60 * 1024 * 1024,
        ),
        name="experts",
    )(*args)


def place_kernel(count, offsets_ref, *refs):
    pieces, out = refs[:count], refs[count]
    for i in range(count):
        start = pl.multiple_of(offsets_ref[i], 16)
        out[pl.ds(start, pieces[i].shape[0]), :] = pieces[i][...]


def place(pieces, offsets, total):
    count, cols = len(pieces), pieces[0].shape[1]
    return pl.pallas_call(
        functools.partial(place_kernel, count),
        out_shape=jax.ShapeDtypeStruct((total, cols), pieces[0].dtype),
        in_specs=[pl.BlockSpec(memory_space=pltpu.SMEM)]
        + [pl.BlockSpec(memory_space=pltpu.VMEM)] * count,
        out_specs=pl.BlockSpec(memory_space=pltpu.VMEM),
        cost_estimate=pl.CostEstimate(
            flops=0, transcendentals=0, bytes_accessed=4 * total * cols
        ),
        name="place",
    )(jnp.stack(offsets).astype(jnp.int32), *pieces)


def product(first_arg, second_arg):
    return jnp.dot(first_arg, second_arg, preferred_element_type=F32)


def product_high(first_arg, second_arg):
    return jnp.dot(
        first_arg, second_arg, precision=lax.Precision.HIGHEST, preferred_element_type=F32
    )


def mm(spec, first_arg, second_arg):
    return jnp.einsum(spec, first_arg, second_arg, preferred_element_type=F32)


def rotary_tables(length, head_size):
    half_dim = head_size // 2
    frequency = 10000.0 ** (-jnp.arange(half_dim, dtype=F32) * 2.0 / head_size)
    angles = jnp.arange(length, dtype=F32)[:, None] * frequency[None, :]
    return (jnp.cos(angles), jnp.sin(angles))


def rotate(tensor, cosine, sine_part):
    half_dim = tensor.shape[-1] // 2
    first_half = tensor[..., :half_dim]
    second_half = tensor[..., half_dim:]
    cos_rows = cosine[:, None, :]
    sin_rows = sine_part[:, None, :]
    return jnp.concatenate(
        [
            first_half * cos_rows - second_half * sin_rows,
            first_half * sin_rows + second_half * cos_rows,
        ],
        axis=-1,
    )


def allowed_mask(length, piece_start, piece_len):
    row_index = jnp.arange(length, dtype=jnp.int32)[:, None]
    col_index = jnp.arange(length, dtype=jnp.int32)[None, :]
    row_inside = (row_index >= piece_start) & (row_index < piece_start + piece_len)
    col_inside = (col_index >= piece_start) & (col_index < piece_start + piece_len)
    return (col_index <= row_index) | row_inside & col_inside


def silu_grad(inputs):
    sigmoid_part = jax.nn.sigmoid(inputs)
    return sigmoid_part * (1.0 + inputs * (1.0 - sigmoid_part))


def high_low(values):
    high = values.astype(BF)
    low = (values - high.astype(F32)).astype(BF)
    return high, low


def shifted(value, axis, by):
    size = lax.axis_size(axis)
    return lax.ppermute(value, axis, [(i, (i + by) % size) for i in range(size)])


def swap(value):
    return shifted(value, "c", 1)


def half(value, index, axis):
    size = value.shape[axis] // 2
    return lax.dynamic_slice_in_dim(value, index * size, size, axis)


def joined(mine, other, core, axis):
    return jnp.where(
        core == 0, jnp.concatenate([mine, other], axis), jnp.concatenate([other, mine], axis)
    )


def pick(value, index, axis):
    return lax.dynamic_index_in_dim(value, index % value.shape[axis], axis, False)


def after(values, *first):
    if not isinstance(values, (list, tuple)):
        return lax.optimization_barrier((values, *first))[0]
    return list(lax.optimization_barrier((*values, *first))[: len(values)])


def ring_gather(value, axis):
    found = [value]
    for _ in range(lax.axis_size(axis) - 1):
        found.append(shifted(found[-1], axis, 1))
    return found


def gather_dp(value):
    rows = value.shape[0]
    cut = (rows // 2 + 15) // 16 * 16
    side = lax.axis_size("x")
    pieces, offsets = [], []

    def add(piece, start, back):
        from_y = (lax.axis_index("y") - back["y"]) % side
        from_x = (lax.axis_index("x") - back["x"]) % side
        pieces.append(piece)
        offsets.append((from_y * side + from_x) * rows + start)

    add(value, 0, {"x": 0, "y": 0})
    along = {axis: ring_gather(value, axis) for axis in "xy"}
    for axis, other in ("xy", "yx"):
        for step in range(1, side):
            add(along[axis][step], 0, {axis: step, other: 0})
    near = len(pieces)
    for start, stop, order in ((0, cut, "xy"), (cut, rows, "yx")):
        for first in range(1, side):
            kept = ring_gather(along[order[0]][first][start:stop], order[1])
            for second in range(1, side):
                add(kept[second], start, {order[0]: first, order[1]: second})
    full = lambda last: place(pieces[:near] + last, offsets, rows * side * side)
    return full, pieces[1:near], pieces[near:]


def ring_reduce(value, axis, at, late):
    size, index = lax.axis_size(axis), lax.axis_index(axis)
    moving = pick(value, index - 1, at)
    for step in range(2, size + 1):
        other = shifted(moving, axis, 1)
        if late:
            other = after(other, *late)
        moving = (other.astype(F32) + pick(value, index - step, at).astype(F32)).astype(BF)
    return moving


def stage_one(values, orders, first=(), late=()):
    values = after(values, *first) if first else values
    return [ring_reduce(v, o[0], "yx".index(o[0]), late) for v, o in zip(values, orders)]


def stage_two(values, orders, first=(), late=()):
    values = after(values, *first) if first else values
    return [ring_reduce(v, o[1], 0, late) for v, o in zip(values, orders)]


def crossed(value, bit):
    depth = lax.axis_size("z")
    return lax.ppermute(value, "z", [(i, i ^ bit) for i in range(depth)])


def reduce_level(value, late=((), (), (), ())):
    depth, level = lax.axis_size("z"), lax.axis_index("z")
    rows, cols = value.shape
    bits = depth.bit_length() - 1
    hold = lambda piece, first: after(piece, *first) if first else piece
    moving = value.reshape(*(2,) * bits, rows // depth, cols)
    for i in range(bits):
        mine = (level >> i) & 1
        at = bits - 1 - i
        other = hold(crossed(pick(moving, 1 - mine, at), 1 << i), late[i])
        moving = (other.astype(F32) + pick(moving, mine, at).astype(F32)).astype(BF)
    for i in reversed(range(bits)):
        mine = (level >> i) & 1
        other = hold(crossed(moving, 1 << i), late[2 * bits - 1 - i])
        at = bits - 1 - i
        moving = jnp.where(
            mine == 0, jnp.stack([moving, other], at), jnp.stack([other, moving], at)
        )
    return moving.reshape(rows, cols)


def body(
    tokens,
    query_weight,
    key_weight,
    value_weight,
    output_weight,
    attn_gain,
    ffn_gain,
    router_weight,
    shared_gate,
    shared_up,
    shared_down,
    expert_gate,
    expert_up,
    expert_down,
    expert_ids,
    piece_starts,
    out_grad,
):
    side = lax.axis_size("x")
    dp = side * side
    owners = lax.axis_size(OWN)
    depth = lax.axis_size("z")
    core = lax.axis_index("c")
    me = lax.axis_index(OWN)
    experts = EXP_DEV * owners
    length, width = tokens.shape
    rows = query_weight.shape[0]
    hidden = shared_gate.shape[1]
    wide, narrow = width // 2, hidden // 2
    head_count = wide // HEAD_DIM
    score_scale = HEAD_DIM ** (-0.5)
    piece_len = min(256, length // 2)
    capacity = 8 * length // experts
    two = lambda mine: jnp.stack([mine, swap(mine)])

    small = jnp.concatenate([router_weight, attn_gain[:, None], ffn_gain[:, None]], axis=1)
    small = jnp.pad(small, ((0, 0), (0, 128 - small.shape[1])))
    first_join, first_near, first_far = gather_dp(
        jnp.concatenate(
            [half(query_weight, core, 1), half(key_weight, core, 1), half(value_weight, core, 1), small],
            axis=1,
        )
    )
    first_full = first_join(first_far)
    tokens_two = two(tokens)
    starts_two = two(piece_starts[0])
    later = after([output_weight, shared_gate, shared_up, shared_down, out_grad], *first_near)
    second_shard = jnp.concatenate(
        [half(later[0], core, 1), half(later[1], core, 1), half(later[2], core, 1)]
        + [half(later[3], core, 1).reshape(rows, narrow)],
        axis=1,
    )
    second_join, second_near, second_far = gather_dp(after(second_shard, *first_far))

    chosen = (expert_ids[:, :, None] == jnp.arange(experts, dtype=jnp.int32)).any(axis=1)
    chosen_low = jnp.pad(chosen.astype(BF), ((0, 0), (0, 128 - experts)))

    levels = [0, depth // 2] + [step for step in range(1, depth) if step != depth // 2]

    grads_sent = jnp.concatenate([later[4], chosen_low], axis=1)
    grads_pair = swap(grads_sent)
    grads_far = {levels[1]: shifted(grads_sent, "z", levels[1])}
    turn_at = after(grads_sent, grads_far[levels[1]])
    for step in levels[2:-1]:
        grads_far[step] = shifted(turn_at, "z", step)
        turn_at = after(turn_at, grads_far[step])

    query_half = first_full[:, :wide]
    key_half = first_full[:, wide : 2 * wide]
    value_half = first_full[:, 2 * wide : 3 * wide]
    small_full = first_full[:, 3 * wide :]
    router_full = small_full[:, :experts]
    gain_one_f = small_full[:, experts].astype(F32)
    gain_two_f = small_full[:, experts + 1].astype(F32)
    token_f = tokens_two.astype(F32)
    norm_one = lax.rsqrt(jnp.mean(token_f * token_f, axis=-1, keepdims=True) + 1e-06)
    attn_in = (token_f * norm_one * gain_one_f).astype(BF).reshape(2 * length, width)
    cosine, sine_part = rotary_tables(length, HEAD_DIM)
    by_head = lambda value: value.reshape(2, length, head_count, HEAD_DIM)
    flat = lambda value: value.reshape(2 * length, wide)
    query_rot = rotate(by_head(product(attn_in, query_half)), cosine, sine_part).astype(BF)
    key_rot = rotate(by_head(product(attn_in, key_half)), cosine, sine_part).astype(BF)
    value_in = after(attn_in, grads_far[levels[1]])
    values = by_head(product(value_in, value_half).astype(BF))
    allowed = jnp.stack([allowed_mask(length, starts_two[i], piece_len) for i in range(2)])
    scores = mm("sqhd,skhd->shqk", query_rot, key_rot) * score_scale
    scores = jnp.where(allowed[:, None], scores, -1e30)
    row_max = jnp.max(scores, axis=-1, keepdims=True)
    exps = jnp.exp(scores - row_max)
    attn_probs = exps / jnp.sum(exps, axis=-1, keepdims=True)
    probs_low = attn_probs.astype(BF)
    second_full = second_join(after(second_far, probs_low))
    output_cols = second_full[:, :wide]
    gate_half = second_full[:, wide : wide + narrow]
    up_half = second_full[:, wide + narrow : wide + 2 * narrow]
    down_cols = second_full[:, wide + 2 * narrow :].reshape(hidden, wide)
    met = swap(
        jnp.concatenate([half(output_cols, 1 - core, 0), half(down_cols, 1 - core, 0)], axis=0)
    )
    output_half = joined(half(output_cols, core, 0), met[:wide], core, 1)
    down_half = joined(half(down_cols, core, 0), met[wide:], core, 1)
    context = flat(mm("shqk,skhd->sqhd", probs_low, after(values, *second_near)).astype(BF))
    held = [grads_far[step] for step in levels[2:-1]]
    out_partial = product(after(context, *held) if held else context, output_half).reshape(2, length, width)
    attn_out = out_partial[0] + swap(out_partial[1].astype(BF)).astype(F32)
    residual = token_f[0] + attn_out
    norm_two = lax.rsqrt(jnp.mean(residual * residual, axis=-1, keepdims=True) + 1e-06)
    ffn_in = (residual * norm_two * gain_two_f).astype(BF)
    router_probs = jax.nn.softmax(product(ffn_in, router_full), axis=-1)
    gates = jnp.where(chosen, router_probs, 0.0)
    gates_high, gates_low = high_low(gates)
    sent = jnp.concatenate(
        [ffn_in, gates_high, gates_low, jnp.zeros((length, 128 - 2 * experts), BF)], axis=1
    )
    sent_other = swap(sent)
    rows_far = {levels[1]: shifted(sent, "z", levels[1])}
    own = me * EXP_DEV + jnp.arange(EXP_DEV)
    own_hot = (own[:, None] == jnp.arange(experts)[None, :]).astype(F32)

    def slots_of(pieces):
        named = jnp.stack([piece[:, width : width + experts] for piece in pieces]).astype(F32)
        mask = mm("ste,oe->ost", named, own_hot)
        found = jnp.where(mask > 0, jnp.cumsum(mask, axis=2) - 1.0, -1.0).astype(jnp.int32)
        return found[:, :, None, :]

    def paired(pieces):
        return [both for piece in pieces for both in (piece, swap(piece))]

    grads_near = [grads_sent, grads_pair] + paired(
        after([grads_far[step] for step in levels[1 : depth // 2]], sent)
    )
    near_slots = slots_of(grads_near)

    ffn_two = jnp.stack([ffn_in, sent_other[:, :width]]).reshape(2 * length, width)
    grad_two = jnp.stack([out_grad, grads_pair[:, :width]]).reshape(2 * length, width)
    shared_gate_act = product(ffn_two, gate_half)
    shared_up_act = product(ffn_two, up_half)
    shared_hidden = (jax.nn.silu(shared_gate_act) * shared_up_act).astype(BF)
    shared_out = product(shared_hidden, down_half).astype(BF).reshape(2, length, width)
    shared_hidden_grad = product(grad_two, down_half.T)
    shared_gate_act_grad = (shared_hidden_grad * shared_up_act * silu_grad(shared_gate_act)).astype(
        BF
    )
    shared_up_act_grad = (shared_hidden_grad * jax.nn.silu(shared_gate_act)).astype(BF)
    shared_gate_grad = product(ffn_two.T, shared_gate_act_grad).astype(BF)
    shared_up_grad = product(ffn_two.T, shared_up_act_grad).astype(BF)
    shared_in_grad = (
        (product(shared_gate_act_grad, gate_half.T) + product(shared_up_act_grad, up_half.T))
        .astype(BF)
        .reshape(2, length, width)
    )
    shared_both = jnp.concatenate(
        [shared_in_grad, jnp.zeros((2, length, 128), BF), shared_out], axis=2
    )
    turn = lambda grad: joined(half(grad, core, 1), swap(half(grad, 1 - core, 1)), core, 0)
    shares = lambda value: value.reshape(side, side, value.shape[0] // dp, -1)
    shared_part = [shares(shared_gate_grad), shares(shared_up_grad)]
    both = ("yx", "xy")
    rows_near = [sent, sent_other] + paired([rows_far[step] for step in levels[1 : depth // 2]])
    sent_next = after([sent, grads_sent], rows_far[levels[1]], shared_in_grad, *shared_part)
    for step in levels[2:]:
        rows_far[step] = shifted(sent_next[0], "z", step)
    grads_far[levels[-1]] = shifted(sent_next[1], "z", levels[-1])
    rows_rest = paired([rows_far[step] for step in levels[depth // 2 :]])
    grads_rest = paired([grads_far[step] for step in levels[depth // 2 :]])

    place_me = me.reshape(1).astype(jnp.int32)
    block = owners // 2
    near = expert_call(
        place_me, near_slots, rows_near, grads_near,
        expert_gate, expert_up, expert_down, owners, 0,
    )
    wider = width + 128
    shared_one = stage_one(shared_part, both, late=(near[block],))
    hidden_low = after(shared_hidden, near[block])
    down_part = [shares(turn(product(hidden_low.T, grad_two).astype(BF)))]
    summed = lambda mine, other, part: (
        mine[:, part].astype(F32) + other[:, part].astype(F32)
    ).astype(BF)
    to_in, to_out = slice(0, wider), slice(wider, None)
    others = [swap(near[i]) for i in range(3, block, 2)]
    mines = [near[i] for i in range(2, block, 2)]
    sent_back = [summed(m, o, to_in) for m, o in zip(mines, others)]
    far_slots = after(slots_of(grads_rest), *sent_back, *shared_one, *down_part)
    far = expert_call(
        place_me, far_slots, rows_rest, grads_rest,
        expert_gate, expert_up, expert_down, owners, 1, near[block:],
    )
    expert_in, res_grad, routed_hidden, routed_gate_grad, routed_up_grad = far[block:]
    gate_grad = mm("erd,erf->edf", expert_in, routed_gate_grad).astype(BF)
    mines += [far[i] for i in range(0, block, 2)]
    near_back = [shifted(sent_back[i], "z", -levels[i + 1]) for i in range(depth // 2 - 1)]
    shared_two = stage_two(shared_one, both, late=(gate_grad,))
    others += after(
        [swap(far[i]) for i in range(1, block, 2)], gate_grad, *near_back, *shared_two
    )
    sent_back += [
        summed(m, o, to_in) for m, o in zip(mines[depth // 2 - 1 :], others[depth // 2 - 1 :])
    ]
    back_in = near_back + [
        shifted(sent_back[i], "z", -levels[i + 1]) for i in range(depth // 2 - 1, depth - 1)
    ]
    routed_up_grad, res_grad = after([routed_up_grad, res_grad], *sent_back)
    up_grad = mm("erd,erf->edf", expert_in, routed_up_grad).astype(BF)
    down_grad = mm("erf,erd->efd", routed_hidden, res_grad).astype(BF)
    own_chip = (near[0].astype(F32) + shared_both[0].astype(F32)) + swap(
        near[1] + shared_both[1]
    ).astype(F32)
    back = own_chip[:, :wider]
    for piece in after(back_in[: depth // 2 - 1], up_grad):
        back += piece.astype(F32)

    blocks = [
        [grad[e].reshape(side, side, grad.shape[1] // dp, grad.shape[2]) for e in range(EXP_DEV)]
        for grad in (gate_grad, up_grad, down_grad)
    ]
    gate_one = stage_one(blocks[0], both, (*shared_two, *sent_back[depth // 2 - 1 :]))
    for piece in after(back_in[depth // 2 - 1 :], down_grad, *gate_one):
        back += piece.astype(F32)

    probs_grad = back[:, width : width + experts] + back[:, width + experts : width + 2 * experts]
    logits_grad = router_probs * (
        probs_grad - jnp.sum(router_probs * probs_grad, axis=-1, keepdims=True)
    )
    router_in_grad = product_high(logits_grad, router_full.astype(F32).T)
    ffn_in_grad = back[:, :width] + router_in_grad
    ffn_gain_terms = ffn_in_grad * residual * norm_two
    upstream_two = ffn_in_grad * gain_two_f
    residual_grad = (
        out_grad.astype(F32)
        + norm_two * upstream_two
        - residual * norm_two**3 * jnp.mean(upstream_two * residual, axis=-1, keepdims=True)
    )
    residual_low = residual_grad.astype(BF)
    attn_grad_two = two(residual_low).reshape(2 * length, width)
    output_grad = product(context.T, attn_grad_two).astype(BF)
    output_grad = turn(output_grad)
    context_grad = by_head(product(attn_grad_two, output_half.T).astype(BF))
    value_grad = flat(mm("shqk,sqhd->skhd", probs_low, context_grad).astype(BF))
    up_one = stage_one(blocks[1], both, gate_one, (value_grad,))
    down_one = stage_one(down_part, both[:1], gate_one, (value_grad,))
    moving = after(summed(mines[0], others[0], to_out), back)
    context_late = after(context_grad, *up_one, *down_one)
    value_wgrad = product(attn_in.T, value_grad).astype(BF)
    early = [shares(output_grad), shares(value_wgrad)]
    probs_grad_att = mm("sqhd,skhd->shqk", context_late, values)
    row_delta = jnp.sum(attn_probs * probs_grad_att, axis=-1, keepdims=True)
    scores_grad = (attn_probs * (probs_grad_att - row_delta)).astype(BF)
    arrived = [after(shifted(moving, "z", -levels[1]), scores_grad)]
    scores_grad = after(scores_grad, *early, *arrived)
    query_grad = mm("shqk,skhd->sqhd", scores_grad, key_rot) * score_scale
    key_grad = mm("shqk,sqhd->skhd", scores_grad, query_rot) * score_scale
    query_pre_grad = flat(rotate(query_grad, cosine, -sine_part).astype(BF))
    key_pre_grad = flat(rotate(key_grad, cosine, -sine_part).astype(BF))
    query_wgrad = product(attn_in.T, query_pre_grad).astype(BF)
    key_wgrad = product(attn_in.T, key_pre_grad).astype(BF)
    in_partial = (
        product(query_pre_grad, query_half.T)
        + product(key_pre_grad, key_half.T)
        + product(value_grad, value_half.T)
    ).reshape(2, length, width)
    gate_two = stage_two(gate_one, both, up_one, (query_wgrad,))
    shared_down = stage_two(down_one, both[:1], late=(query_wgrad,))
    attn_in_grad = after(in_partial[0], *gate_two, *shared_down) + swap(in_partial[1].astype(BF)).astype(F32)
    token_mine, norm_mine = token_f[0], norm_one[0]
    attn_gain_terms = attn_in_grad * token_mine * norm_mine
    upstream_one = attn_in_grad * gain_one_f
    tokens_grad = (
        residual_grad
        + norm_mine * upstream_one
        - token_mine * norm_mine**3 * jnp.mean(upstream_one * token_mine, axis=-1, keepdims=True)
    )
    lanes = jnp.arange(128)
    unit = lambda lane: jnp.broadcast_to((lanes == lane).astype(F32), (length, 128))
    small_grads = (
        product_high(ffn_in.astype(F32).T, jnp.pad(logits_grad, ((0, 0), (0, 128 - experts))))
        + product_high(ffn_gain_terms.T, unit(experts + 1))
        + product_high(attn_gain_terms.T, unit(experts))
    ).astype(BF)

    done_wgrads = (query_wgrad, key_wgrad)
    early_one = stage_one(early, both, up_one, (small_grads,))
    early_two = stage_two(early_one, both)
    late = [shares(query_wgrad), shares(jnp.concatenate([key_wgrad, small_grads], axis=1))]
    late_one = stage_one(late, both)
    late_two = stage_two(late_one, both, early_two)
    up_two = stage_two(up_one, both, late_one)
    down_two = stage_two(stage_one(blocks[2], both, up_two), both)
    expert_shares = [jnp.stack(pair).astype(F32) for pair in (gate_two, up_two, down_two)]
    shared_share = reduce_level(after(jnp.concatenate(shared_two, axis=0), back), ((value_grad,), done_wgrads, early_two, late_one))
    shared_share = after(shared_share, *late_two)
    early_share = reduce_level(jnp.concatenate([*early_two, *shared_down], axis=0))
    late_share = reduce_level(jnp.concatenate(late_two, axis=1))

    for i in range(1, depth - 1):
        moving = after(summed(mines[i], others[i], to_out), arrived[-1])
        piece = shifted(moving, "z", -levels[i + 1])
        arrived.append(after(piece, *((small_grads,) if i < depth - 2 else early_two)))
    moe_out = own_chip[:, wider:]
    for piece in arrived:
        moe_out += piece.astype(F32)

    early_other, late_other, shared_other = swap(early_share), swap(late_share), swap(shared_share)
    column = lambda mine, other, start, size: joined(
        mine[:, start : start + size], other[:, start : start + size], core, 1
    ).astype(F32)
    small_sum = late_share[:, 2 * wide :].astype(F32) + late_other[:, 2 * wide :].astype(F32)
    stacked = lambda mine, other, start, size: joined(
        mine[start : start + size], other[start : start + size], core, 1
    ).astype(F32)

    stream_out = residual + moe_out
    stat_rms = jnp.stack(
        [
            jnp.sqrt(jnp.mean(attn_out * attn_out)),
            jnp.sqrt(jnp.mean(moe_out * moe_out)),
            jnp.sqrt(jnp.mean(stream_out * stream_out)),
        ]
    )[None, :]
    return (
        stream_out.astype(BF),
        tokens_grad.astype(BF),
        column(late_share, late_other, 0, wide),
        column(late_share, late_other, wide, wide),
        stacked(early_share, early_other, rows, rows),
        stacked(early_share, early_other, 0, rows),
        small_sum[:, experts],
        small_sum[:, experts + 1],
        small_sum[:, :experts],
        stacked(shared_share, shared_other, 0, rows),
        stacked(shared_share, shared_other, rows, rows),
        stacked(early_share, early_other, 2 * rows, early_share.shape[0] - 2 * rows),
        *expert_shares,
        stat_rms,
    )


def solution(mesh):
    side = math.isqrt(mesh.shape["dp"])
    fine = Mesh(
        mesh.devices.reshape(side, side, mesh.shape["expert"] // 2, 2), ("y", "x", "z", "c")
    )
    whole = P(("y", "x", "z", "c"), None)
    dense = P(DP, None)
    routed = P(OWN, None, None)
    in_specs = (
        whole, dense, dense, dense, dense, P(DP), P(DP), dense, dense, dense, dense,
        routed, routed, routed, whole, P(("y", "x", "z", "c")), whole,
    )
    shares = P(OWN, DP, None)
    out_specs = (
        whole, whole, dense, dense, dense, dense, P(DP), P(DP), dense, dense, dense, dense,
        shares, shares, shares, whole,
    )
    return jax.shard_map(body, mesh=fine, in_specs=in_specs, out_specs=out_specs, check_vma=False)
```

```python
import functools
import math

import jax
import jax.numpy as jnp
from jax import lax
from jax.experimental import pallas as pl
from jax.experimental.pallas import tpu as pltpu
from jax.sharding import Mesh
from jax.sharding import PartitionSpec as P

HEAD_DIM = 128
TOP = 7
EXP_DEV = 2
BF = jnp.bfloat16
F32 = jnp.float32
DP = ("y", "x")
OWN = ("z", "c")
NT = (((1,), (1,)), ((), ()))
TN = (((0,), (0,)), ((), ()))


def dot(first, second, dims=(((1,), (0,)), ((), ()))):
    return lax.dot_general(first, second, dims, preferred_element_type=F32)


def expert_kernel(count, width, capacity, experts, chunk, me_ref, slots_ref, *refs):
    rows_refs = refs[:count]
    grads_refs = refs[count : 2 * count]
    gate_ref, up_ref, down_ref = refs[2 * count : 2 * count + 3]
    sums = refs[-10 - count : -10]
    xin, rgrad, hid, ggrad, ugrad = refs[-10:-5]
    ograd, in_ext, res_low, in_acc, out_acc = refs[-5:]
    step = pl.program_id(0)
    expert = me_ref[0] * EXP_DEV + step
    lane = lax.broadcasted_iota(jnp.int32, (capacity, 128), 1)
    mine = (lane == expert) | (lane == expert + experts)

    def spread(piece):
        want = slots_ref[step, piece]
        place = lax.broadcasted_iota(jnp.int32, (capacity, want.shape[-1]), 0)
        return (want == place).astype(F32)

    for piece in range(count):
        hot = spread(piece).astype(BF)
        area = pl.ds(piece * capacity, capacity)
        rows = dot(hot, rows_refs[piece][...])
        xin[0, area, :] = rows[:, :width].astype(BF)
        gates = jnp.sum(jnp.where(mine, rows[:, width:], 0.0), axis=1, keepdims=True)
        grads = dot(hot, grads_refs[piece][:, :width])
        ograd[area, :] = grads.astype(BF)
        rgrad[0, area, :] = (grads * gates).astype(BF)

    def part(index, carry):
        area = pl.ds(pl.multiple_of(index * chunk, chunk), chunk)
        rows = xin[0, area, :]
        res_grad = rgrad[0, area, :]
        gate = dot(rows, gate_ref[0])
        up = dot(rows, up_ref[0])
        hidden_grad = dot(res_grad, down_ref[0], NT)
        sig = jax.nn.sigmoid(gate)
        silu = gate * sig
        hidden = (silu * up).astype(BF)
        hid[0, area, :] = hidden
        gate_grad = (hidden_grad * up * (sig * (1.0 + gate * (1.0 - sig)))).astype(BF)
        up_grad = (hidden_grad * silu).astype(BF)
        ggrad[0, area, :] = gate_grad
        ugrad[0, area, :] = up_grad
        in_ext[area, pl.ds(0, width)] = (
            dot(gate_grad, gate_ref[0], NT) + dot(up_grad, up_ref[0], NT)
        ).astype(BF)
        res = dot(hidden, down_ref[0]).astype(BF)
        res_low[area, :] = res
        slot_gate = jnp.sum(res.astype(F32) * ograd[area, :].astype(F32), axis=1, keepdims=True)
        high = slot_gate.astype(BF).astype(F32)
        lanes = lax.broadcasted_iota(jnp.int32, (chunk, 128), 1)
        in_ext[area, pl.ds(width, 128)] = jnp.where(
            lanes == expert, high, jnp.where(lanes == expert + experts, slot_gate - high, 0.0)
        ).astype(BF)
        return carry

    lax.fori_loop(0, count * capacity // chunk, part, 0)

    for piece in range(count):
        hot = spread(piece)
        area = pl.ds(piece * capacity, capacity)
        low = hot.astype(BF)
        gates = jnp.sum(
            jnp.where(mine, dot(low, rows_refs[piece][:, width:]), 0.0), axis=1, keepdims=True
        )
        back = dot(low, in_ext[area, :], TN)
        result = dot((hot * gates).astype(BF), res_low[area, :], TN)

        @pl.when(step == 0)
        def _():
            in_acc[piece] = back
            out_acc[piece] = result

        @pl.when(step == EXP_DEV - 1)
        def _():
            wide = back.shape[1]
            sums[piece][:, :wide] = (in_acc[piece] + back).astype(BF)
            sums[piece][:, wide:] = (out_acc[piece] + result).astype(BF)


def expert_call(me, slots, rows, grads, gate, up, down, owners, first, carried=None):
    count = len(rows)
    length, wide = rows[0].shape
    width, hidden = gate.shape[1:]
    experts = EXP_DEV * owners
    capacity = 8 * length // experts
    block = count * capacity
    total = owners * capacity
    still = lambda shape: pl.BlockSpec(
        shape, lambda e, m: (0,) * len(shape), pipeline_mode=pl.Buffered(1)
    )
    weight = lambda a, b: pl.BlockSpec((1, a, b), lambda e, m: (e, 0, 0))
    kept = lambda cols: pl.BlockSpec((1, block, cols), lambda e, m: (e, first, 0))
    kept_cols = (width, width, hidden, hidden, hidden)
    in_specs = (
        [still((EXP_DEV, count, 1, length))]
        + [still((length, wide))] * (2 * count)
        + [weight(width, hidden), weight(width, hidden), weight(hidden, width)]
    )
    args = [me, slots, *rows, *grads, gate, up, down]
    alias = {}
    if carried is not None:
        for i, value in enumerate(carried):
            alias[len(args)] = count + i
            args.append(value)
            in_specs.append(pl.BlockSpec(memory_space=pl.ANY))
    sums = [(length, wide + width)] * count
    return pl.pallas_call(
        functools.partial(expert_kernel, count, width, capacity, experts, min(512, block)),
        out_shape=[jax.ShapeDtypeStruct(shape, BF) for shape in sums]
        + [jax.ShapeDtypeStruct((EXP_DEV, total, cols), BF) for cols in kept_cols],
        grid_spec=pltpu.PrefetchScalarGridSpec(
            num_scalar_prefetch=1,
            grid=(EXP_DEV,),
            in_specs=in_specs,
            out_specs=[still(shape) for shape in sums] + [kept(cols) for cols in kept_cols],
            scratch_shapes=[
                pltpu.VMEM((block, width), BF),
                pltpu.VMEM((block, wide), BF),
                pltpu.VMEM((block, width), BF),
                pltpu.VMEM((count, length, wide), F32),
                pltpu.VMEM((count, length, width), F32),
            ],
        ),
        input_output_aliases=alias,
        compiler_params=pltpu.CompilerParams(
            dimension_semantics=("arbitrary",), vmem_limit_bytes=60 * 1024 * 1024
        ),
        cost_estimate=pl.CostEstimate(
            flops=14 * EXP_DEV * block * width * hidden,
            transcendentals=EXP_DEV * block * hidden,
            bytes_accessed=60 * 1024 * 1024,
        ),
        name="experts",
    )(*args)


def place_kernel(count, offsets_ref, *refs):
    pieces, out = refs[:count], refs[count]
    for i in range(count):
        start = pl.multiple_of(offsets_ref[i], 16)
        out[pl.ds(start, pieces[i].shape[0]), :] = pieces[i][...]


def place(pieces, offsets, total):
    count, cols = len(pieces), pieces[0].shape[1]
    return pl.pallas_call(
        functools.partial(place_kernel, count),
        out_shape=jax.ShapeDtypeStruct((total, cols), pieces[0].dtype),
        in_specs=[pl.BlockSpec(memory_space=pltpu.SMEM)]
        + [pl.BlockSpec(memory_space=pltpu.VMEM)] * count,
        out_specs=pl.BlockSpec(memory_space=pltpu.VMEM),
        cost_estimate=pl.CostEstimate(
            flops=0, transcendentals=0, bytes_accessed=4 * total * cols
        ),
        name="place",
    )(jnp.stack(offsets).astype(jnp.int32), *pieces)


def product(first_arg, second_arg):
    return jnp.dot(first_arg, second_arg, preferred_element_type=F32)


def product_high(first_arg, second_arg):
    return jnp.dot(
        first_arg, second_arg, precision=lax.Precision.HIGHEST, preferred_element_type=F32
    )


def mm(spec, first_arg, second_arg):
    return jnp.einsum(spec, first_arg, second_arg, preferred_element_type=F32)


def rotary_tables(length, head_size):
    half_dim = head_size // 2
    frequency = 10000.0 ** (-jnp.arange(half_dim, dtype=F32) * 2.0 / head_size)
    angles = jnp.arange(length, dtype=F32)[:, None] * frequency[None, :]
    return (jnp.cos(angles), jnp.sin(angles))


def rotate(tensor, cosine, sine_part):
    half_dim = tensor.shape[-1] // 2
    first_half = tensor[..., :half_dim]
    second_half = tensor[..., half_dim:]
    cos_rows = cosine[:, None, :]
    sin_rows = sine_part[:, None, :]
    return jnp.concatenate(
        [
            first_half * cos_rows - second_half * sin_rows,
            first_half * sin_rows + second_half * cos_rows,
        ],
        axis=-1,
    )


def allowed_mask(length, piece_start, piece_len):
    row_index = jnp.arange(length, dtype=jnp.int32)[:, None]
    col_index = jnp.arange(length, dtype=jnp.int32)[None, :]
    row_inside = (row_index >= piece_start) & (row_index < piece_start + piece_len)
    col_inside = (col_index >= piece_start) & (col_index < piece_start + piece_len)
    return (col_index <= row_index) | row_inside & col_inside


def silu_grad(inputs):
    sigmoid_part = jax.nn.sigmoid(inputs)
    return sigmoid_part * (1.0 + inputs * (1.0 - sigmoid_part))


def high_low(values):
    high = values.astype(BF)
    low = (values - high.astype(F32)).astype(BF)
    return high, low


def shifted(value, axis, by):
    size = lax.axis_size(axis)
    return lax.ppermute(value, axis, [(i, (i + by) % size) for i in range(size)])


def swap(value):
    return shifted(value, "c", 1)


def half(value, index, axis):
    size = value.shape[axis] // 2
    return lax.dynamic_slice_in_dim(value, index * size, size, axis)


def joined(mine, other, core, axis):
    return jnp.where(
        core == 0, jnp.concatenate([mine, other], axis), jnp.concatenate([other, mine], axis)
    )


def pick(value, index, axis):
    return lax.dynamic_index_in_dim(value, index % value.shape[axis], axis, False)


def after(values, *first):
    if not isinstance(values, (list, tuple)):
        return lax.optimization_barrier((values, *first))[0]
    return list(lax.optimization_barrier((*values, *first))[: len(values)])


def ring_gather(value, axis):
    found = [value]
    for _ in range(lax.axis_size(axis) - 1):
        found.append(shifted(found[-1], axis, 1))
    return found


def gather_dp(value):
    rows = value.shape[0]
    cut = (rows // 2 + 15) // 16 * 16
    side = lax.axis_size("x")
    pieces, offsets = [], []

    def add(piece, start, back):
        from_y = (lax.axis_index("y") - back["y"]) % side
        from_x = (lax.axis_index("x") - back["x"]) % side
        pieces.append(piece)
        offsets.append((from_y * side + from_x) * rows + start)

    add(value, 0, {"x": 0, "y": 0})
    along = {axis: ring_gather(value, axis) for axis in "xy"}
    for axis, other in ("xy", "yx"):
        for step in range(1, side):
            add(along[axis][step], 0, {axis: step, other: 0})
    near = len(pieces)
    for start, stop, order in ((0, cut, "xy"), (cut, rows, "yx")):
        for first in range(1, side):
            kept = ring_gather(along[order[0]][first][start:stop], order[1])
            for second in range(1, side):
                add(kept[second], start, {order[0]: first, order[1]: second})
    full = lambda last: place(pieces[:near] + last, offsets, rows * side * side)
    return full, pieces[1:near], pieces[near:]


def ring_reduce(value, axis, at, late):
    size, index = lax.axis_size(axis), lax.axis_index(axis)
    moving = pick(value, index - 1, at)
    for step in range(2, size + 1):
        other = shifted(moving, axis, 1)
        if late:
            other = after(other, *late)
        moving = (other.astype(F32) + pick(value, index - step, at).astype(F32)).astype(BF)
    return moving


def stage_one(values, orders, first=(), late=()):
    values = after(values, *first) if first else values
    return [ring_reduce(v, o[0], "yx".index(o[0]), late) for v, o in zip(values, orders)]


def stage_two(values, orders, first=(), late=()):
    values = after(values, *first) if first else values
    return [ring_reduce(v, o[1], 0, late) for v, o in zip(values, orders)]


def crossed(value, bit):
    depth = lax.axis_size("z")
    return lax.ppermute(value, "z", [(i, i ^ bit) for i in range(depth)])


def reduce_level(value, late=((), (), (), ())):
    depth, level = lax.axis_size("z"), lax.axis_index("z")
    rows, cols = value.shape
    bits = depth.bit_length() - 1
    hold = lambda piece, first: after(piece, *first) if first else piece
    moving = value.reshape(*(2,) * bits, rows // depth, cols)
    for i in range(bits):
        mine = (level >> i) & 1
        at = bits - 1 - i
        other = hold(crossed(pick(moving, 1 - mine, at), 1 << i), late[i])
        moving = (other.astype(F32) + pick(moving, mine, at).astype(F32)).astype(BF)
    for i in reversed(range(bits)):
        mine = (level >> i) & 1
        other = hold(crossed(moving, 1 << i), late[2 * bits - 1 - i])
        at = bits - 1 - i
        moving = jnp.where(
            mine == 0, jnp.stack([moving, other], at), jnp.stack([other, moving], at)
        )
    return moving.reshape(rows, cols)


def body(
    tokens,
    query_weight,
    key_weight,
    value_weight,
    output_weight,
    attn_gain,
    ffn_gain,
    router_weight,
    shared_gate,
    shared_up,
    shared_down,
    expert_gate,
    expert_up,
    expert_down,
    expert_ids,
    piece_starts,
    out_grad,
):
    side = lax.axis_size("x")
    dp = side * side
    owners = lax.axis_size(OWN)
    depth = lax.axis_size("z")
    core = lax.axis_index("c")
    me = lax.axis_index(OWN)
    experts = EXP_DEV * owners
    length, width = tokens.shape
    rows = query_weight.shape[0]
    hidden = shared_gate.shape[1]
    wide, narrow = width // 2, hidden // 2
    head_count = wide // HEAD_DIM
    score_scale = HEAD_DIM ** (-0.5)
    piece_len = min(256, length // 2)
    capacity = 8 * length // experts
    two = lambda mine: jnp.stack([mine, swap(mine)])

    small = jnp.concatenate([router_weight, attn_gain[:, None], ffn_gain[:, None]], axis=1)
    small = jnp.pad(small, ((0, 0), (0, 128 - small.shape[1])))
    first_join, first_near, first_far = gather_dp(
        jnp.concatenate(
            [half(query_weight, core, 1), half(key_weight, core, 1), half(value_weight, core, 1), small],
            axis=1,
        )
    )
    first_full = first_join(first_far)
    tokens_two = two(tokens)
    starts_two = two(piece_starts[0])
    later = after([output_weight, shared_gate, shared_up, shared_down, out_grad], *first_near)
    second_shard = jnp.concatenate(
        [half(later[0], core, 1)]
        + [jnp.pad(half(later[3], core, 1), ((0, rows - shared_down.shape[0]), (0, 0)))]
        + [half(later[1], core, 1), half(later[2], core, 1)],
        axis=1,
    )
    second_join, second_near, second_far = gather_dp(after(second_shard, *first_far))

    chosen = (expert_ids[:, :, None] == jnp.arange(experts, dtype=jnp.int32)).any(axis=1)
    chosen_low = jnp.pad(chosen.astype(BF), ((0, 0), (0, 128 - experts)))

    levels = [0, depth // 2] + [step for step in range(1, depth) if step != depth // 2]

    grads_sent = jnp.concatenate([later[4], chosen_low], axis=1)
    grads_pair = swap(grads_sent)
    grads_far = {levels[1]: shifted(grads_sent, "z", levels[1])}
    turn_at = after(grads_sent, grads_far[levels[1]])
    for step in levels[2:-1]:
        grads_far[step] = shifted(turn_at, "z", step)
        turn_at = after(turn_at, grads_far[step])

    query_half = first_full[:, :wide]
    key_half = first_full[:, wide : 2 * wide]
    value_half = first_full[:, 2 * wide : 3 * wide]
    small_full = first_full[:, 3 * wide :]
    router_full = small_full[:, :experts]
    gain_one_f = small_full[:, experts].astype(F32)
    gain_two_f = small_full[:, experts + 1].astype(F32)
    token_f = tokens_two.astype(F32)
    norm_one = lax.rsqrt(jnp.mean(token_f * token_f, axis=-1, keepdims=True) + 1e-06)
    attn_in = (token_f * norm_one * gain_one_f).astype(BF).reshape(2 * length, width)
    cosine, sine_part = rotary_tables(length, HEAD_DIM)
    by_head = lambda value: value.reshape(2, length, head_count, HEAD_DIM)
    flat = lambda value: value.reshape(2 * length, wide)
    query_rot = rotate(by_head(product(attn_in, query_half)), cosine, sine_part).astype(BF)
    key_rot = rotate(by_head(product(attn_in, key_half)), cosine, sine_part).astype(BF)
    value_in = after(attn_in, grads_far[levels[1]])
    values = by_head(product(value_in, value_half).astype(BF))
    allowed = jnp.stack([allowed_mask(length, starts_two[i], piece_len) for i in range(2)])
    scores = mm("sqhd,skhd->shqk", query_rot, key_rot) * score_scale
    scores = jnp.where(allowed[:, None], scores, -1e30)
    row_max = jnp.max(scores, axis=-1, keepdims=True)
    exps = jnp.exp(scores - row_max)
    attn_probs = exps / jnp.sum(exps, axis=-1, keepdims=True)
    probs_low = attn_probs.astype(BF)
    second_full = second_join(after(second_far, probs_low))
    output_cols = second_full[:, :wide]
    gate_half = second_full[:, 2 * wide : 2 * wide + narrow]
    up_half = second_full[:, 2 * wide + narrow :]
    down_cols = second_full[:, wide : 2 * wide].reshape(dp, rows, wide)
    down_cols = down_cols[:, : shared_down.shape[0]].reshape(hidden, wide)
    met = swap(
        jnp.concatenate([half(output_cols, 1 - core, 0), half(down_cols, 1 - core, 0)], axis=0)
    )
    output_half = joined(half(output_cols, core, 0), met[:wide], core, 1)
    down_half = joined(half(down_cols, core, 0), met[wide:], core, 1)
    context = flat(mm("shqk,skhd->sqhd", probs_low, after(values, *second_near)).astype(BF))
    held = [grads_far[step] for step in levels[2:-1]]
    out_partial = product(after(context, *held) if held else context, output_half).reshape(2, length, width)
    attn_out = out_partial[0] + swap(out_partial[1].astype(BF)).astype(F32)
    residual = token_f[0] + attn_out
    norm_two = lax.rsqrt(jnp.mean(residual * residual, axis=-1, keepdims=True) + 1e-06)
    ffn_in = (residual * norm_two * gain_two_f).astype(BF)
    router_probs = jax.nn.softmax(product(ffn_in, router_full), axis=-1)
    gates = jnp.where(chosen, router_probs, 0.0)
    gates_high, gates_low = high_low(gates)
    sent = jnp.concatenate(
        [ffn_in, gates_high, gates_low, jnp.zeros((length, 128 - 2 * experts), BF)], axis=1
    )
    sent_other = swap(sent)
    rows_far = {levels[1]: shifted(sent, "z", levels[1])}
    own = me * EXP_DEV + jnp.arange(EXP_DEV)
    own_hot = (own[:, None] == jnp.arange(experts)[None, :]).astype(F32)

    def slots_of(pieces):
        named = jnp.stack([piece[:, width : width + experts] for piece in pieces]).astype(F32)
        mask = mm("ste,oe->ost", named, own_hot)
        found = jnp.where(mask > 0, jnp.cumsum(mask, axis=2) - 1.0, -1.0).astype(jnp.int32)
        return found[:, :, None, :]

    def paired(pieces):
        return [both for piece in pieces for both in (piece, swap(piece))]

    grads_near = [grads_sent, grads_pair] + paired(
        after([grads_far[step] for step in levels[1 : depth // 2]], sent)
    )
    near_slots = slots_of(grads_near)

    ffn_two = jnp.stack([ffn_in, sent_other[:, :width]]).reshape(2 * length, width)
    grad_two = jnp.stack([out_grad, grads_pair[:, :width]]).reshape(2 * length, width)
    shared_gate_act = product(ffn_two, gate_half)
    shared_up_act = product(ffn_two, up_half)
    shared_hidden = (jax.nn.silu(shared_gate_act) * shared_up_act).astype(BF)
    shared_out = product(shared_hidden, down_half).astype(BF).reshape(2, length, width)
    shared_hidden_grad = product(grad_two, down_half.T)
    shared_gate_act_grad = (shared_hidden_grad * shared_up_act * silu_grad(shared_gate_act)).astype(
        BF
    )
    shared_up_act_grad = (shared_hidden_grad * jax.nn.silu(shared_gate_act)).astype(BF)
    shared_gate_grad = product(ffn_two.T, shared_gate_act_grad).astype(BF)
    shared_up_grad = product(ffn_two.T, shared_up_act_grad).astype(BF)
    shared_in_grad = (
        (product(shared_gate_act_grad, gate_half.T) + product(shared_up_act_grad, up_half.T))
        .astype(BF)
        .reshape(2, length, width)
    )
    shared_both = jnp.concatenate(
        [shared_in_grad, jnp.zeros((2, length, 128), BF), shared_out], axis=2
    )
    turn = lambda grad: joined(half(grad, core, 1), swap(half(grad, 1 - core, 1)), core, 0)
    shares = lambda value: value.reshape(side, side, value.shape[0] // dp, -1)
    shared_part = [shares(shared_gate_grad), shares(shared_up_grad)]
    both = ("yx", "xy")
    rows_near = [sent, sent_other] + paired([rows_far[step] for step in levels[1 : depth // 2]])
    sent_next = after([sent, grads_sent], rows_far[levels[1]], shared_in_grad, *shared_part)
    for step in levels[2:]:
        rows_far[step] = shifted(sent_next[0], "z", step)
    grads_far[levels[-1]] = shifted(sent_next[1], "z", levels[-1])
    rows_rest = paired([rows_far[step] for step in levels[depth // 2 :]])
    grads_rest = paired([grads_far[step] for step in levels[depth // 2 :]])

    place_me = me.reshape(1).astype(jnp.int32)
    block = owners // 2
    near = expert_call(
        place_me, near_slots, rows_near, grads_near,
        expert_gate, expert_up, expert_down, owners, 0,
    )
    wider = width + 128
    shared_one = stage_one(shared_part, both, late=(near[block],))
    hidden_low = after(shared_hidden, near[block])
    down_part = [shares(turn(product(hidden_low.T, grad_two).astype(BF)))]
    summed = lambda mine, other, part: (
        mine[:, part].astype(F32) + other[:, part].astype(F32)
    ).astype(BF)
    to_in, to_out = slice(0, wider), slice(wider, None)
    others = [swap(near[i]) for i in range(3, block, 2)]
    mines = [near[i] for i in range(2, block, 2)]
    sent_back = [summed(m, o, to_in) for m, o in zip(mines, others)]
    far_slots = after(slots_of(grads_rest), *sent_back, *shared_one, *down_part)
    far = expert_call(
        place_me, far_slots, rows_rest, grads_rest,
        expert_gate, expert_up, expert_down, owners, 1, near[block:],
    )
    expert_in, res_grad, routed_hidden, routed_gate_grad, routed_up_grad = far[block:]
    gate_grad = mm("erd,erf->edf", expert_in, routed_gate_grad).astype(BF)
    mines += [far[i] for i in range(0, block, 2)]
    near_back = [shifted(sent_back[i], "z", -levels[i + 1]) for i in range(depth // 2 - 1)]
    shared_two = stage_two(shared_one, both, late=(gate_grad,))
    others += after(
        [swap(far[i]) for i in range(1, block, 2)], gate_grad, *near_back, *shared_two
    )
    sent_back += [
        summed(m, o, to_in) for m, o in zip(mines[depth // 2 - 1 :], others[depth // 2 - 1 :])
    ]
    back_in = near_back + [
        shifted(sent_back[i], "z", -levels[i + 1]) for i in range(depth // 2 - 1, depth - 1)
    ]
    routed_up_grad, res_grad = after([routed_up_grad, res_grad], *sent_back)
    up_grad = mm("erd,erf->edf", expert_in, routed_up_grad).astype(BF)
    down_grad = mm("erf,erd->efd", routed_hidden, res_grad).astype(BF)
    own_chip = (near[0].astype(F32) + shared_both[0].astype(F32)) + swap(
        near[1] + shared_both[1]
    ).astype(F32)
    back = own_chip[:, :wider]
    for piece in after(back_in[: depth // 2 - 1], up_grad):
        back += piece.astype(F32)

    blocks = [
        [grad[e].reshape(side, side, grad.shape[1] // dp, grad.shape[2]) for e in range(EXP_DEV)]
        for grad in (gate_grad, up_grad, down_grad)
    ]
    gate_one = stage_one(blocks[0], both, (*shared_two, *sent_back[depth // 2 - 1 :]))
    for piece in after(back_in[depth // 2 - 1 :], down_grad, *gate_one):
        back += piece.astype(F32)

    probs_grad = back[:, width : width + experts] + back[:, width + experts : width + 2 * experts]
    logits_grad = router_probs * (
        probs_grad - jnp.sum(router_probs * probs_grad, axis=-1, keepdims=True)
    )
    router_in_grad = product_high(logits_grad, router_full.astype(F32).T)
    ffn_in_grad = back[:, :width] + router_in_grad
    ffn_gain_terms = ffn_in_grad * residual * norm_two
    upstream_two = ffn_in_grad * gain_two_f
    residual_grad = (
        out_grad.astype(F32)
        + norm_two * upstream_two
        - residual * norm_two**3 * jnp.mean(upstream_two * residual, axis=-1, keepdims=True)
    )
    residual_low = residual_grad.astype(BF)
    attn_grad_two = two(residual_low).reshape(2 * length, width)
    output_grad = product(context.T, attn_grad_two).astype(BF)
    output_grad = turn(output_grad)
    context_grad = by_head(product(attn_grad_two, output_half.T).astype(BF))
    value_grad = flat(mm("shqk,sqhd->skhd", probs_low, context_grad).astype(BF))
    up_one = stage_one(blocks[1], both, gate_one, (value_grad,))
    down_one = stage_one(down_part, both[:1], gate_one, (value_grad,))
    moving = after(summed(mines[0], others[0], to_out), back)
    context_late = after(context_grad, *up_one, *down_one)
    value_wgrad = product(attn_in.T, value_grad).astype(BF)
    early = [shares(output_grad), shares(value_wgrad)]
    probs_grad_att = mm("sqhd,skhd->shqk", context_late, values)
    row_delta = jnp.sum(attn_probs * probs_grad_att, axis=-1, keepdims=True)
    scores_grad = (attn_probs * (probs_grad_att - row_delta)).astype(BF)
    arrived = [after(shifted(moving, "z", -levels[1]), scores_grad)]
    scores_grad = after(scores_grad, *early, *arrived)
    query_grad = mm("shqk,skhd->sqhd", scores_grad, key_rot) * score_scale
    key_grad = mm("shqk,sqhd->skhd", scores_grad, query_rot) * score_scale
    query_pre_grad = flat(rotate(query_grad, cosine, -sine_part).astype(BF))
    key_pre_grad = flat(rotate(key_grad, cosine, -sine_part).astype(BF))
    query_wgrad = product(attn_in.T, query_pre_grad).astype(BF)
    key_wgrad = product(attn_in.T, key_pre_grad).astype(BF)
    in_partial = (
        product(query_pre_grad, query_half.T)
        + product(key_pre_grad, key_half.T)
        + product(value_grad, value_half.T)
    ).reshape(2, length, width)
    gate_two = stage_two(gate_one, both, up_one, (query_wgrad,))
    shared_down = stage_two(down_one, both[:1], late=(query_wgrad,))
    attn_in_grad = after(in_partial[0], *gate_two, *shared_down) + swap(in_partial[1].astype(BF)).astype(F32)
    token_mine, norm_mine = token_f[0], norm_one[0]
    attn_gain_terms = attn_in_grad * token_mine * norm_mine
    upstream_one = attn_in_grad * gain_one_f
    tokens_grad = (
        residual_grad
        + norm_mine * upstream_one
        - token_mine * norm_mine**3 * jnp.mean(upstream_one * token_mine, axis=-1, keepdims=True)
    )
    lanes = jnp.arange(128)
    unit = lambda lane: jnp.broadcast_to((lanes == lane).astype(F32), (length, 128))
    small_grads = (
        product_high(ffn_in.astype(F32).T, jnp.pad(logits_grad, ((0, 0), (0, 128 - experts))))
        + product_high(ffn_gain_terms.T, unit(experts + 1))
        + product_high(attn_gain_terms.T, unit(experts))
    ).astype(BF)

    done_wgrads = (query_wgrad, key_wgrad)
    early_one = stage_one(early, both, up_one, (small_grads,))
    early_two = stage_two(early_one, both)
    late = [shares(query_wgrad), shares(jnp.concatenate([key_wgrad, small_grads], axis=1))]
    late_one = stage_one(late, both)
    late_two = stage_two(late_one, both, early_two)
    up_two = stage_two(up_one, both, late_one)
    down_two = stage_two(stage_one(blocks[2], both, up_two), both)
    expert_shares = [jnp.stack(pair).astype(F32) for pair in (gate_two, up_two, down_two)]
    shared_share = reduce_level(after(jnp.concatenate(shared_two, axis=0), back), ((value_grad,), done_wgrads, early_two, late_one))
    shared_share = after(shared_share, *late_two)
    early_share = reduce_level(jnp.concatenate([*early_two, *shared_down], axis=0))
    late_share = reduce_level(jnp.concatenate(late_two, axis=1))

    for i in range(1, depth - 1):
        moving = after(summed(mines[i], others[i], to_out), arrived[-1])
        piece = shifted(moving, "z", -levels[i + 1])
        arrived.append(after(piece, *((small_grads,) if i < depth - 2 else early_two)))
    moe_out = own_chip[:, wider:]
    for piece in arrived:
        moe_out += piece.astype(F32)

    early_other, late_other, shared_other = swap(early_share), swap(late_share), swap(shared_share)
    column = lambda mine, other, start, size: joined(
        mine[:, start : start + size], other[:, start : start + size], core, 1
    ).astype(F32)
    small_sum = late_share[:, 2 * wide :].astype(F32) + late_other[:, 2 * wide :].astype(F32)
    stacked = lambda mine, other, start, size: joined(
        mine[start : start + size], other[start : start + size], core, 1
    ).astype(F32)

    stream_out = residual + moe_out
    stat_rms = jnp.stack(
        [
            jnp.sqrt(jnp.mean(attn_out * attn_out)),
            jnp.sqrt(jnp.mean(moe_out * moe_out)),
            jnp.sqrt(jnp.mean(stream_out * stream_out)),
        ]
    )[None, :]
    return (
        stream_out.astype(BF),
        tokens_grad.astype(BF),
        column(late_share, late_other, 0, wide),
        column(late_share, late_other, wide, wide),
        stacked(early_share, early_other, rows, rows),
        stacked(early_share, early_other, 0, rows),
        small_sum[:, experts],
        small_sum[:, experts + 1],
        small_sum[:, :experts],
        stacked(shared_share, shared_other, 0, rows),
        stacked(shared_share, shared_other, rows, rows),
        stacked(early_share, early_other, 2 * rows, early_share.shape[0] - 2 * rows),
        *expert_shares,
        stat_rms,
    )


def solution(mesh):
    side = math.isqrt(mesh.shape["dp"])
    fine = Mesh(
        mesh.devices.reshape(side, side, mesh.shape["expert"] // 2, 2), ("y", "x", "z", "c")
    )
    whole = P(("y", "x", "z", "c"), None)
    dense = P(DP, None)
    routed = P(OWN, None, None)
    in_specs = (
        whole, dense, dense, dense, dense, P(DP), P(DP), dense, dense, dense, dense,
        routed, routed, routed, whole, P(("y", "x", "z", "c")), whole,
    )
    shares = P(OWN, DP, None)
    out_specs = (
        whole, whole, dense, dense, dense, dense, P(DP), P(DP), dense, dense, dense, dense,
        shares, shares, shares, whole,
    )
    return jax.shard_map(body, mesh=fine, in_specs=in_specs, out_specs=out_specs, check_vma=False)
```
